32 devices in a mesh: expert: 8 (over z, x), tensor: 4 (over y, core).
Axes of the slice: x: 2, y: 2, z: 4, core: 2. Of those that a mesh axis runs over, the one named last changes fastest.
Arguments:
- inputs: bfloat16 [8, 256, 2048], P(None, 'expert'), may hold values from -6 to 6
- cotangent: bfloat16 [8, 256, 2048], P(None, 'expert'), may hold values from -6 to 6
- lengths: int32 [8], replicated, may hold values from 1 to 256, 1536 in all
- permutation: int32 [8], replicated, may hold values from 0 to 7, each once
- routes: int32 [2048, 8], P('expert'), may hold values from 0 to 15, all different within a row; in each aligned block of 256 rows (0 to 255, 256 to 511, ...) at most 132 rows name the same one
- query_weight: float32 [2048, 2048], P('expert', 'tensor'), may hold values from -0.125 to 0.125
- key_weight: float32 [2048, 2048], P('expert', 'tensor'), may hold values from -0.125 to 0.125
- value_weight: float32 [2048, 2048], P('expert', 'tensor'), may hold values from -0.125 to 0.125
- proj_weight: float32 [2048, 2048], P('tensor', 'expert'), may hold values from -2 to 2
- first_gain: float32 [2048], P('expert'), may hold values from 0.5 to 1.5
- second_gain: float32 [2048], P('expert'), may hold values from 0.5 to 1.5
- query_gain: float32 [128], P('expert'), may hold values from 0.5 to 1.5
- key_gain: float32 [128], P('expert'), may hold values from 0.5 to 1.5
- router_weight: float32 [2048, 16], P('expert'), may hold values from -0.0625 to 0.0625
- gate_weight: float32 [16, 2048, 1024], P('expert', None, 'tensor'), may hold values from -0.125 to 0.125
- up_weight: float32 [16, 2048, 1024], P('expert', None, 'tensor'), may hold values from -0.125 to 0.125
- down_weight: float32 [16, 1024, 2048], P('expert', 'tensor'), may hold values from -0.75 to 0.75
Outputs:
- output: bfloat16 [8, 256, 2048], P(None, 'expert')
- input_grad: bfloat16 [8, 256, 2048], P(None, 'expert')
- query_grad: float32 [2048, 2048], P('expert', 'tensor')
- key_grad: float32 [2048, 2048], P('expert', 'tensor')
- value_grad: float32 [2048, 2048], P('expert', 'tensor')
- proj_grad: float32 [2048, 2048], P('tensor', 'expert')
- first_gain_grad: float32 [2048], P('expert')
- second_gain_grad: float32 [2048], P('expert')
- query_gain_grad: float32 [128], P('expert')
- key_gain_grad: float32 [128], P('expert')
- router_grad: float32 [2048, 16], P('expert')
- gate_grad: float32 [16, 2048, 1024], P('expert', None, 'tensor')
- up_grad: float32 [16, 2048, 1024], P('expert', None, 'tensor')
- down_grad: float32 [16, 1024, 2048], P('expert', 'tensor')
The draws below stay inside these ranges and needn't reach their ends.
Inputs may be any that keep to these rules, and one draw needn't show every extreme that they name: `lengths`: some sequence has all 256 rows valid. `permutation`: each slot holds a different sequence. `routes`: each row names 8 different experts. Among the 256 rows of one slot no expert is named by more than 132 rows, a bound that some block reaches.
All inputs are finite; a program needn't handle non-finite values.
Results may differ from the reference program's by a relative error of at most 0.024.
Values may be sent and summed in bfloat16 or wider, within the bound.
A program may use at most 320 MiB of HBM per device.

```python
import math
import jax
import jax.numpy as jnp
import numpy as np
from jax import lax

D = 2048
H = 16
HD = 128
FFE = 1024
TOPK = 8
TOK_DEV = 256
EXPERTS = 16
SEQS = 8
TOKENS = 2048
MOST = 132
N_TENSOR = 4


def block_levels(own_key, shape, split, smallest, top_value):
    loudness, own = 1.0, jax.random.fold_in(own_key, 6)
    for dim, parts in split:
        heights = jnp.exp(jax.random.uniform(jax.random.fold_in(own, dim), (parts,), jnp.float32, smallest / len(split), top_value / len(split)))
        loudness = loudness * jnp.repeat(heights, shape[dim] // parts).reshape([-1 if axis == dim else 1 for axis in range(len(shape))])
    return loudness


def split_up(amount, total, most, skew):
    loads = [(1 << 20) // math.isqrt(grade ** skew) + 1 for grade in range(2, amount + 1)]
    rest, holding = total - most - (amount - 1), [1] * (amount - 1)
    while rest > 0:
        candidates = [i for i in range(amount - 1) if holding[i] < most]
        pool, left = sum([loads[i] for i in candidates]), rest
        for i in candidates:
            extra = min(most - holding[i], max(1, left * loads[i] // pool), rest)
            holding[i] = holding[i] + extra
            rest = rest - extra
    return np.array([most] + holding)


def ragged_sizes(rng, amount, total, bound, slope):
    if amount == 2:
        one = jax.random.randint(rng, (), max(1, total - bound), min(bound, total - 1) + 1)
        return jnp.stack([one, total - one])
    sizes = jnp.asarray(split_up(amount, total, bound, slope), jnp.int32)
    pairs = (amount - 1) // 2
    source_of, receiver = sizes[1:1 + 2 * pairs:2], sizes[2:2 + 2 * pairs:2]
    slack = jnp.minimum(source_of - 1, bound - receiver)
    shifted = jax.random.randint(jax.random.fold_in(rng, 1), (pairs,), 0, 1 << 20) % (slack + 1)
    sizes = sizes.at[1:1 + 2 * pairs:2].set(source_of - shifted).at[2:2 + 2 * pairs:2].set(receiver + shifted)
    return sizes[jax.random.permutation(jax.random.fold_in(rng, 2), amount)]


def shared_out(own_key, own, number, rows, count, top, bound, skew):
    sequence = jax.random.permutation(own_key, count)
    packed, ordinary = shares(count, rows * top, bound, skew, True), shares(count, rows * top, bound, skew, False)
    places = jnp.arange(count)

    def named(sizes, rotation):
        used = int((sizes > 0).sum())
        fixed = max(1, used // 4)
        moved = fixed + (places - fixed + rotation * (used - fixed)) % max(1, count - fixed)
        return jnp.zeros((count,), jnp.int32).at[sequence[jnp.where(places < fixed, places, moved)]].set(jnp.asarray(sizes, jnp.int32))

    sizes = jnp.where(number % 4 == 0, named(packed, number // 4), named(ordinary, number - number // 4 - 1))
    mixed = jax.random.permutation(jax.random.fold_in(own, 3), count)
    giver, receiver = mixed[0:count // 2 * 2:2], mixed[1:count // 2 * 2:2]
    room = jnp.minimum(sizes[giver] - 1, bound - sizes[receiver]) // 2
    room = jnp.where((giver == sequence[0]) | (receiver == sequence[0]) | (sizes[receiver] == 0), 0, jnp.maximum(room, 0))
    moved = jax.random.randint(jax.random.fold_in(own, 4), (count // 2,), 0, 1 << 20) % (room + 1)
    sizes = sizes.at[giver].add(-moved).at[receiver].add(moved)
    items = jnp.searchsorted(jnp.cumsum(sizes), jnp.arange(rows * top), side="right").astype(jnp.int32)
    listing = items.reshape(top, rows).T
    listing = listing[jax.random.permutation(jax.random.fold_in(own, 1), rows)]
    rotation = jax.random.randint(jax.random.fold_in(own, 2), (rows, 1), 0, top)
    return jnp.take_along_axis(listing, (jnp.arange(top)[None, :] + rotation) % top, axis=1)


def shares(amount, total, most, skew, full):
    weights = [(1 << 20) // math.isqrt(standing ** skew) + 1 for standing in range(1, amount + 1)]
    largest = most if full else min(most, max(-(-total // amount), total * weights[0] // sum(weights)))
    least = 1 if total - largest >= amount - 1 else 0
    given, rest = [largest] + [least] * (amount - 1), total - largest - least * (amount - 1)
    while rest > 0:
        movable = [i for i in range(1, amount) if given[i] < largest] or [i for i in range(1, amount) if given[i] < most]
        pool, budget = sum([weights[i] for i in movable]), rest
        for i in movable:
            addition = min(most - given[i], max(1, budget * weights[i] // pool), rest)
            given[i] = given[i] + addition
            rest = rest - addition
    return np.array(given)


def normal_values(stream_key, shape, scale, limit, cuts=(), held_as=jnp.bfloat16):
    array = jax.random.normal(stream_key, shape, jnp.float32) * scale
    if len(cuts) > 0:
        array = block_levels(stream_key, shape, cuts, -0.22, 0.18) * array
    return jnp.clip(array, min=-limit, max=limit).astype(held_as)


def setup_inputs(seed: int = 0) -> dict:
    key_list = jax.random.split(jax.random.key(seed), 18)
    inputs = normal_values(key_list[0], (SEQS, TOK_DEV, D), 1.0, 6.0, ((1, 8),))
    cotangent = normal_values(key_list[1], (SEQS, TOK_DEV, D), 1.0, 6.0, ((1, 8),))
    lengths = ragged_sizes(key_list[2], SEQS, SEQS * TOK_DEV * 3 // 4, TOK_DEV, 1).astype(jnp.int32)
    permutation = jax.random.permutation(key_list[3], SEQS).astype(jnp.int32)
    routes_keys = jax.random.split(jax.random.fold_in(key_list[4], 1), TOKENS // TOK_DEV)
    routes_turns = jax.random.permutation(jax.random.fold_in(key_list[4], 3), TOKENS // TOK_DEV)
    routes = jax.vmap(lambda own, number: shared_out(jax.random.fold_in(key_list[4], 2), own, number, TOK_DEV, EXPERTS, TOPK, MOST, 2))(routes_keys, routes_turns).reshape((TOKENS, TOPK))
    query_weight = normal_values(key_list[5], (D, H * HD), D ** -0.5, 0.125, ((0, 8), (1, 4)), jnp.float32)
    key_weight = normal_values(key_list[6], (D, H * HD), D ** -0.5, 0.125, ((0, 8), (1, 4)), jnp.float32)
    value_weight = normal_values(key_list[7], (D, H * HD), D ** -0.5, 0.125, ((0, 8), (1, 4)), jnp.float32)
    proj_weight = normal_values(key_list[8], (H * HD, D), (max(8, H * HD // 256)) ** -0.5, 2.0, ((0, 4), (1, 8)), jnp.float32)
    first_gain = jnp.clip(1.0 + 0.1 * jax.random.normal(key_list[9], (D,), jnp.float32), 0.5, 1.5)
    second_gain = jnp.clip(1.0 + 0.1 * jax.random.normal(key_list[10], (D,), jnp.float32), 0.5, 1.5)
    query_gain = jnp.clip(1.0 + 0.1 * jax.random.normal(key_list[11], (HD,), jnp.float32), 0.5, 1.5)
    key_gain = jnp.clip(1.0 + 0.1 * jax.random.normal(key_list[12], (HD,), jnp.float32), 0.5, 1.5)
    router_weight = normal_values(key_list[13], (D, EXPERTS), (4 * D) ** -0.5, 0.0625, ((0, 8),), jnp.float32)
    gate_weight = normal_values(key_list[14], (EXPERTS, D, FFE), D ** -0.5, 0.125, ((0, 8), (2, 4)), jnp.float32)
    up_weight = normal_values(key_list[15], (EXPERTS, D, FFE), D ** -0.5, 0.125, ((0, 8), (2, 4)), jnp.float32)
    down_weight = normal_values(key_list[16], (EXPERTS, FFE, D), (FFE // 16) ** -0.5, 0.75, ((0, 8), (1, 4)), jnp.float32)
    return dict(inputs=inputs, cotangent=cotangent, lengths=lengths, permutation=permutation, routes=routes, query_weight=query_weight, key_weight=key_weight, value_weight=value_weight, proj_weight=proj_weight, first_gain=first_gain, second_gain=second_gain, query_gain=query_gain, key_gain=key_gain, router_weight=router_weight, gate_weight=gate_weight, up_weight=up_weight, down_weight=down_weight)


EPS = 1e-06
ROPE_BASE = 50000.0
NEG_FILL = -1e+30

@jax.custom_vjp
def low(v):
    return lax.optimization_barrier(v.astype(jnp.bfloat16)).astype(jnp.float32)

@jax.custom_vjp
def low_back(v):
    return v

def low_keep(v):
    return (low(v), None)

def low_pass(kept, grad):
    return (grad,)

def back_keep(v):
    return (v, None)

def back_low(kept, grad):
    return (low(grad),)
low.defvjp(low_keep, low_pass)
low_back.defvjp(back_keep, back_low)

def matmul(left, right):
    return jnp.dot(left, right, precision=lax.Precision.HIGHEST)

def rms_scale(values, gain):
    return values * lax.rsqrt(lax.optimization_barrier(jnp.mean(values * values, axis=-1, keepdims=True)) + EPS) * gain

def rope_tables(seq_count, width):
    halfway = width // 2
    frequency = jnp.power(ROPE_BASE, -jnp.arange(halfway, dtype=jnp.float32) * (2.0 / width))
    angles = jnp.arange(seq_count, dtype=jnp.float32)[:, None] * frequency[None, :]
    return (jnp.cos(angles)[:, None, :], jnp.sin(angles)[:, None, :])

def rotate(values, cos_table, sin_table):
    halfway = values.shape[-1] // 2
    former = values[..., :halfway]
    latter = values[..., halfway:]
    return jnp.concatenate([former * cos_table - latter * sin_table, latter * cos_table + former * sin_table], axis=-1)

def attend_sequence(seq_rows, length, query_matrix, key_matrix, value_matrix, proj_matrix, gain_one, gain_query, gain_key, cos_table, sin_table):
    seq_count = seq_rows.shape[0]
    normed = low(rms_scale(seq_rows, gain_one))
    queries = low_back(matmul(normed, query_matrix)).reshape(seq_count, H, HD)
    keys_raw = low_back(matmul(normed, key_matrix)).reshape(seq_count, H, HD)
    values = low(low_back(matmul(normed, value_matrix))).reshape(seq_count, H, HD)
    queries = low(rotate(rms_scale(queries, gain_query), cos_table, sin_table))
    keys_rot = low(rotate(rms_scale(keys_raw, gain_key), cos_table, sin_table))
    scores = jnp.einsum('qhd,khd->hqk', queries, keys_rot, precision=lax.Precision.HIGHEST) / math.sqrt(HD)
    scores = low_back(scores)
    usable = jnp.arange(seq_count) < length
    scores = jnp.where(usable[None, None, :], scores, NEG_FILL)
    weights = low(jax.nn.softmax(scores, axis=-1))
    context = jnp.einsum('hqk,khd->qhd', weights, values, precision=lax.Precision.HIGHEST)
    context = low(low_back(context)).reshape(seq_count, H * HD)
    return matmul(context, proj_matrix)

def layer(slot_rows, query_weight, key_weight, value_weight, proj_weight, first_gain, second_gain, query_gain, key_gain, router_weight, gate_weight, up_weight, down_weight, slot_lengths, routes):
    query_matrix = low(query_weight)
    key_matrix = low(key_weight)
    value_matrix = low(value_weight)
    proj_matrix = low(proj_weight)
    gain_one = low(first_gain)
    gain_two = low(second_gain)
    gain_query = low(query_gain)
    gain_key = low(key_gain)
    router_matrix = low(router_weight)
    gate_matrix = low(gate_weight)
    up_matrix = low(up_weight)
    down_matrix = low(down_weight)
    cos_table, sin_table = rope_tables(TOK_DEV, HD)
    attend = jax.checkpoint(attend_sequence)

    def sequence_step(carry, item):
        return (carry, attend(item[0], item[1], query_matrix, key_matrix, value_matrix, proj_matrix, gain_one, gain_query, gain_key, cos_table, sin_table))
    _, attn_out = lax.scan(sequence_step, jnp.zeros((), jnp.float32), (slot_rows.reshape(SEQS, TOK_DEV, D), slot_lengths))
    residual = slot_rows + low_back(attn_out.reshape(TOKENS, D))
    normed_two = low(rms_scale(residual, gain_two))
    logits = low_back(matmul(normed_two, router_matrix))
    chosen = jnp.take_along_axis(logits, routes, axis=1)
    gate_probs = jax.nn.softmax(chosen, axis=-1)
    flat_routes = routes.reshape(-1)
    ordering = jnp.argsort(flat_routes, stable=True).astype(jnp.int32)
    counts = lax.optimization_barrier(jnp.sum((flat_routes[:, None] == jnp.arange(EXPERTS, dtype=jnp.int32)[None, :]).astype(jnp.int32), axis=0))
    starts = (jnp.cumsum(counts) - counts).astype(jnp.int32)
    capacity_rows = SEQS * MOST
    order_padded = jnp.concatenate([ordering, jnp.zeros((capacity_rows,), jnp.int32)])
    gate_flat = gate_probs.reshape(-1)
    slice_width = FFE // N_TENSOR

    def expert_piece(normed_all, gate_all, gate_one_e, up_one_e, down_one_e, start, filled):
        places = jnp.arange(capacity_rows, dtype=jnp.int32)
        pair_ids = lax.dynamic_slice_in_dim(order_padded, start.astype(jnp.int32), capacity_rows)
        token_ids = pair_ids // TOPK
        inputs_here = normed_all[token_ids]
        weighting = gate_all[pair_ids] * (places < filled).astype(jnp.float32)
        result = jnp.zeros((capacity_rows, D), jnp.float32)
        for quarter in range(N_TENSOR):
            first_col = quarter * slice_width
            last_col = first_col + slice_width
            rows_part = low_back(inputs_here)
            gate_pre = low_back(matmul(rows_part, gate_one_e[:, first_col:last_col]))
            up_pre = low_back(matmul(rows_part, up_one_e[:, first_col:last_col]))
            hidden = low(jax.nn.silu(gate_pre) * up_pre)
            result = result + low(low_back(matmul(hidden, down_one_e[first_col:last_col, :])))
        return (result * weighting[:, None], token_ids)
    piece = jax.checkpoint(expert_piece)

    def expert_step(accum, item):
        contrib, token_ids = piece(normed_two, gate_flat, item[0], item[1], item[2], item[3], item[4])
        return (accum.at[token_ids].add(contrib), None)
    moe_out, _ = lax.scan(expert_step, jnp.zeros((TOKENS, D), jnp.float32), (gate_matrix, up_matrix, down_matrix, starts, counts))
    return residual + moe_out

def reference(inputs, cotangent, lengths, permutation, routes, query_weight, key_weight, value_weight, proj_weight, first_gain, second_gain, query_gain, key_gain, router_weight, gate_weight, up_weight, down_weight):
    slot_lengths = lengths[permutation]
    inverse = jnp.argsort(permutation).astype(jnp.int32)

    def forward(source, query_matrix, key_matrix, value_matrix, proj_matrix, gain_one, gain_two, gain_query, gain_key, router_matrix, gate_matrix, up_matrix, down_matrix):
        slot_rows = source[permutation].reshape(TOKENS, D)
        slot_result = layer(slot_rows, query_matrix, key_matrix, value_matrix, proj_matrix, gain_one, gain_two, gain_query, gain_key, router_matrix, gate_matrix, up_matrix, down_matrix, slot_lengths, routes)
        return slot_result.reshape(SEQS, TOK_DEV, D)[inverse]
    result, pull_back = jax.vjp(forward, inputs.astype(jnp.float32), query_weight, key_weight, value_weight, proj_weight, first_gain, second_gain, query_gain, key_gain, router_weight, gate_weight, up_weight, down_weight)
    gradients = pull_back(cotangent.astype(jnp.float32))
    return (result.astype(jnp.bfloat16), gradients[0].astype(jnp.bfloat16), gradients[1], gradients[2], gradients[3], gradients[4], gradients[5], gradients[6], gradients[7], gradients[8], gradients[9], gradients[10], gradients[11], gradients[12])
```

```python
import math

import jax
import jax.numpy as jnp
from jax import lax
from jax.sharding import PartitionSpec as P

HD = 128
TOPK = 8


EPS = 1e-06
ROPE_BASE = 50000.0
NEG_FILL = -1e30


def norm_parts(values, gain):
    inverse = lax.rsqrt(jnp.mean(values * values, axis=-1, keepdims=True) + EPS)
    unit_rows = values * inverse
    return (unit_rows * gain, unit_rows, inverse)


def norm_back(grad_normed, gain, unit_rows, inverse):
    grad_unit = grad_normed * gain
    inner_mean = jnp.mean(grad_unit * unit_rows, axis=-1, keepdims=True)
    return inverse * (grad_unit - unit_rows * inner_mean)


def rope_tables(seq_count, width):
    halfway = width // 2
    frequency = jnp.power(ROPE_BASE, -jnp.arange(halfway, dtype=jnp.float32) * (2.0 / width))
    angles = jnp.arange(seq_count, dtype=jnp.float32)[:, None] * frequency[None, :]
    return (jnp.cos(angles)[:, None, :], jnp.sin(angles)[:, None, :])


def rotate(values, cos_table, sin_table):
    halfway = values.shape[-1] // 2
    former = values[..., :halfway]
    latter = values[..., halfway:]
    return jnp.concatenate(
        [former * cos_table - latter * sin_table, latter * cos_table + former * sin_table], axis=-1
    )


def on_device(
    inputs,
    cotangent,
    lengths,
    permutation,
    routes,
    query_weight,
    key_weight,
    value_weight,
    proj_weight,
    first_gain,
    second_gain,
    query_gain,
    key_gain,
    router_weight,
    gate_weight,
    up_weight,
    down_weight,
):
    model_width = inputs.shape[2]
    local_heads = query_weight.shape[1] // HD
    expert_count = router_weight.shape[1]
    groups_count = lax.axis_size("expert")
    local_experts = gate_weight.shape[0]
    slot_index = lax.axis_index("expert")
    seq_ids = jnp.arange(permutation.shape[0], dtype=jnp.int32)
    my_sequence = jnp.sum(jnp.where(seq_ids == slot_index, permutation, 0))
    my_length = jnp.sum(jnp.where(seq_ids == my_sequence, lengths, 0))
    slot_of_seq = jnp.sum(
        jnp.where(permutation[None, :] == seq_ids[:, None], seq_ids[None, :], 0), axis=1
    )
    dealt_in, dealt_grad = (
        lax.all_to_all(inputs[permutation], "expert", split_axis=0, concat_axis=1, tiled=True),
        lax.all_to_all(cotangent[permutation], "expert", split_axis=0, concat_axis=1, tiled=True),
    )
    token_rows = dealt_in.shape[1]
    capacity = token_rows * TOPK * 33 // (32 * expert_count)
    block_rows = min(512, token_rows)
    score_scale = math.sqrt(HD)
    gathered = (
        lax.all_gather(query_weight.astype(jnp.bfloat16), "expert", axis=0, tiled=True),
        lax.all_gather(key_weight.astype(jnp.bfloat16), "expert", axis=0, tiled=True),
        lax.all_gather(value_weight.astype(jnp.bfloat16), "expert", axis=0, tiled=True),
        lax.all_gather(proj_weight.astype(jnp.bfloat16), "expert", axis=1, tiled=True),
        lax.all_gather(first_gain.astype(jnp.bfloat16), "expert", axis=0, tiled=True),
        lax.all_gather(second_gain.astype(jnp.bfloat16), "expert", axis=0, tiled=True),
        lax.all_gather(query_gain.astype(jnp.bfloat16), "expert", axis=0, tiled=True),
        lax.all_gather(key_gain.astype(jnp.bfloat16), "expert", axis=0, tiled=True),
        lax.all_gather(router_weight.astype(jnp.bfloat16), "expert", axis=0, tiled=True),
    )
    query_matrix = gathered[0]
    key_matrix = gathered[1]
    value_matrix = gathered[2]
    proj_matrix = gathered[3]
    gain_one = gathered[4].astype(jnp.float32)
    gain_two = gathered[5].astype(jnp.float32)
    gain_query = gathered[6].astype(jnp.float32)
    gain_key = gathered[7].astype(jnp.float32)
    router_matrix = gathered[8]
    gate_matrix = gate_weight.astype(jnp.bfloat16)
    up_matrix = up_weight.astype(jnp.bfloat16)
    down_matrix = down_weight.astype(jnp.bfloat16)
    source = dealt_in.reshape(token_rows, model_width).astype(jnp.float32)
    normed_one_f, unit_one, inverse_one = norm_parts(source, gain_one)
    normed_one = normed_one_f.astype(jnp.bfloat16)
    queries_raw = jnp.dot(normed_one, query_matrix, preferred_element_type=jnp.float32).reshape(
        token_rows, local_heads, HD
    )
    keys_raw = jnp.dot(normed_one, key_matrix, preferred_element_type=jnp.float32).reshape(
        token_rows, local_heads, HD
    )
    values = (
        jnp.dot(normed_one, value_matrix, preferred_element_type=jnp.float32)
        .astype(jnp.bfloat16)
        .reshape(token_rows, local_heads, HD)
    )
    cos_table, sin_table = rope_tables(token_rows, HD)
    query_normed, query_unit, query_inverse = norm_parts(queries_raw, gain_query)
    key_normed, key_unit, key_inverse = norm_parts(keys_raw, gain_key)
    queries = rotate(query_normed, cos_table, sin_table).astype(jnp.bfloat16)
    keys_rot = rotate(key_normed, cos_table, sin_table).astype(jnp.bfloat16)
    usable = jnp.arange(token_rows) < my_length

    def block_scores():
        scores = (
            jnp.einsum("qhd,khd->hqk", queries, keys_rot, preferred_element_type=jnp.float32)
            / score_scale
        )
        return (queries, jnp.where(usable[None, None, :], scores, NEG_FILL))

    query_block, scores = block_scores()
    maximum = jnp.max(scores, axis=-1, keepdims=True)
    exponent = jnp.exp(scores - maximum)
    row_total = jnp.sum(exponent, axis=-1, keepdims=True)
    softmax_rows = (exponent / row_total).astype(jnp.bfloat16)
    context_blocks = jnp.einsum(
        "hqk,khd->qhd", softmax_rows, values, preferred_element_type=jnp.float32
    ).astype(jnp.bfloat16)
    lse_blocks = [maximum + jnp.log(row_total)]
    context = context_blocks.reshape(token_rows, local_heads * HD)
    attn_part = jnp.dot(context, proj_matrix, preferred_element_type=jnp.float32)
    attn_total = lax.psum_scatter(attn_part, "tensor", scatter_dimension=0, tiled=True)
    own_rows = attn_total.shape[0]
    tensor_index = lax.axis_index("tensor")
    residual = lax.dynamic_slice_in_dim(source, tensor_index * own_rows, own_rows) + attn_total
    own_routes = lax.dynamic_slice_in_dim(routes, tensor_index * own_rows, own_rows)
    grad_out_low = lax.dynamic_slice_in_dim(
        dealt_grad.reshape(token_rows, model_width), tensor_index * own_rows, own_rows
    )
    normed_two_f, unit_two, inverse_two = norm_parts(residual, gain_two)
    normed_two = normed_two_f.astype(jnp.bfloat16)
    logits = jnp.dot(normed_two, router_matrix, preferred_element_type=jnp.float32)
    choose = (
        own_routes[:, :, None] == jnp.arange(expert_count, dtype=jnp.int32)[None, None, :]
    ).astype(jnp.float32)
    named = jnp.sum(choose, axis=1) > 0.5
    masked = jnp.where(named, logits, NEG_FILL)
    gates = jax.nn.softmax(masked, axis=-1)
    everyone = ("expert", "tensor")
    all_rows = lax.all_gather(normed_two, everyone, axis=0, tiled=True)
    all_grad = lax.all_gather(grad_out_low, everyone, axis=0, tiled=True)
    all_gates = lax.all_gather(gates, everyone, axis=0, tiled=True)
    my_gates = lax.dynamic_slice_in_dim(all_gates, slot_index * local_experts, local_experts, axis=1)
    out_total = 0.0
    rows_total = 0.0
    gate_columns = []
    weight_grads = []
    for number in range(local_experts):
        gate_column = my_gates[:, number : number + 1]
        gate_pre = jnp.dot(all_rows, gate_matrix[number], preferred_element_type=jnp.float32)
        up_pre = jnp.dot(all_rows, up_matrix[number], preferred_element_type=jnp.float32)
        grad_plain = lax.dot_general(
            all_grad, down_matrix[number], (((1,), (1,)), ((), ())), preferred_element_type=jnp.float32
        )
        sigmoid_gate = jax.nn.sigmoid(gate_pre)
        silu_gate = gate_pre * sigmoid_gate
        hidden = silu_gate * up_pre
        gate_columns.append(jnp.sum(hidden * grad_plain, axis=-1, keepdims=True))
        gated = (gate_column * hidden).astype(jnp.bfloat16)
        grad_hidden = gate_column * grad_plain
        grad_gate_pre = (
            grad_hidden * up_pre * sigmoid_gate * (1.0 + gate_pre * (1.0 - sigmoid_gate))
        ).astype(jnp.bfloat16)
        grad_up_pre = (grad_hidden * silu_gate).astype(jnp.bfloat16)
        out_total = out_total + jnp.dot(
            gated, down_matrix[number], preferred_element_type=jnp.float32
        )
        rows_total = rows_total + lax.dot_general(
            grad_gate_pre, gate_matrix[number], (((1,), (1,)), ((), ())), preferred_element_type=jnp.float32
        ) + lax.dot_general(
            grad_up_pre, up_matrix[number], (((1,), (1,)), ((), ())), preferred_element_type=jnp.float32
        )
        over_rows = (((0,), (0,)), ((), ()))
        weight_grads.append((
            lax.dot_general(all_rows, grad_gate_pre, over_rows, preferred_element_type=jnp.float32),
            lax.dot_general(all_rows, grad_up_pre, over_rows, preferred_element_type=jnp.float32),
            lax.dot_general(gated, all_grad, over_rows, preferred_element_type=jnp.float32),
        ))
    gate_grad, up_grad, down_grad = (
        jnp.stack([grads[which] for grads in weight_grads]) for which in range(3)
    )
    spread = (
        jnp.arange(expert_count)[None, None, :]
        == (slot_index * local_experts + jnp.arange(local_experts))[None, :, None]
    ).astype(jnp.float32)
    gate_part = jnp.sum(jnp.concatenate(gate_columns, axis=1)[:, :, None] * spread, axis=1)
    moe_total = lax.psum_scatter(
        out_total.astype(jnp.bfloat16), everyone, scatter_dimension=0, tiled=True
    ).astype(jnp.float32)
    grad_normed_two = lax.psum_scatter(
        rows_total.astype(jnp.bfloat16), everyone, scatter_dimension=0, tiled=True
    ).astype(jnp.float32)
    gate_grad_total = lax.psum_scatter(gate_part, everyone, scatter_dimension=0, tiled=True)
    output = lax.all_gather(
        (residual + moe_total).astype(jnp.bfloat16), "tensor", axis=0, tiled=True
    )
    grad_out = grad_out_low.astype(jnp.float32)
    grad_logits = (
        gates * (gate_grad_total - jnp.sum(gates * gate_grad_total, axis=-1, keepdims=True))
    ).astype(jnp.bfloat16)
    grad_normed_two = grad_normed_two + jnp.dot(
        grad_logits, router_matrix.T, preferred_element_type=jnp.float32
    )
    router_grad = lax.psum(
        jnp.dot(normed_two.T, grad_logits, preferred_element_type=jnp.float32), "tensor"
    )
    second_gain_grad = lax.psum(jnp.sum(grad_normed_two * unit_two, axis=0), "tensor")
    grad_state = grad_out + norm_back(grad_normed_two, gain_two, unit_two, inverse_two)
    grad_state = lax.all_gather(grad_state, "tensor", axis=0, tiled=True)
    grad_context_in = grad_state.astype(jnp.bfloat16)
    proj_grad = jnp.dot(context.T, grad_context_in, preferred_element_type=jnp.float32)
    grad_context = (
        jnp.dot(grad_context_in, proj_matrix.T, preferred_element_type=jnp.float32)
        .astype(jnp.bfloat16)
        .reshape(token_rows, local_heads, HD)
    )
    grad_values = jnp.zeros((token_rows, local_heads, HD), jnp.float32)
    grad_keys_rot = jnp.zeros((token_rows, local_heads, HD), jnp.float32)
    grad_query_blocks = []
    for number, start_row in enumerate(range(0, token_rows, block_rows)):
        query_block, scores = block_scores()
        softmax_f = jnp.exp(scores - lse_blocks[number])
        grad_values = jnp.einsum(
            "hqk,qhd->khd",
            softmax_f.astype(jnp.bfloat16),
            grad_context,
            preferred_element_type=jnp.float32,
        )
        grad_probs = jnp.einsum(
            "qhd,khd->hqk", grad_context, values, preferred_element_type=jnp.float32
        )
        grad_scores = (
            softmax_f * (grad_probs - jnp.sum(grad_probs * softmax_f, axis=-1, keepdims=True))
        ).astype(jnp.bfloat16)
        grad_query_blocks.append(
            jnp.einsum("hqk,khd->qhd", grad_scores, keys_rot, preferred_element_type=jnp.float32)
            / score_scale
        )
        grad_keys_rot = (
            jnp.einsum("hqk,qhd->khd", grad_scores, query_block, preferred_element_type=jnp.float32)
            / score_scale
        )
    grad_queries_n = rotate(grad_query_blocks[0], cos_table, -sin_table)
    grad_keys_n = rotate(grad_keys_rot, cos_table, -sin_table)
    query_gain_part = jnp.sum(grad_queries_n * query_unit, axis=(0, 1))
    key_gain_part = jnp.sum(grad_keys_n * key_unit, axis=(0, 1))
    grad_queries_raw = (
        norm_back(grad_queries_n, gain_query, query_unit, query_inverse)
        .astype(jnp.bfloat16)
        .reshape(token_rows, local_heads * HD)
    )
    grad_keys_raw = (
        norm_back(grad_keys_n, gain_key, key_unit, key_inverse)
        .astype(jnp.bfloat16)
        .reshape(token_rows, local_heads * HD)
    )
    grad_values_low = grad_values.astype(jnp.bfloat16).reshape(token_rows, local_heads * HD)
    query_grad = jnp.dot(normed_one.T, grad_queries_raw, preferred_element_type=jnp.float32)
    key_grad = jnp.dot(normed_one.T, grad_keys_raw, preferred_element_type=jnp.float32)
    value_grad = jnp.dot(normed_one.T, grad_values_low, preferred_element_type=jnp.float32)
    normed_one_part = jnp.dot(grad_queries_raw, query_matrix.T, preferred_element_type=jnp.float32)
    normed_one_part = normed_one_part + jnp.dot(
        grad_keys_raw, key_matrix.T, preferred_element_type=jnp.float32
    )
    normed_one_part = normed_one_part + jnp.dot(
        grad_values_low, value_matrix.T, preferred_element_type=jnp.float32
    )
    grad_normed_one, query_gain_total, key_gain_total = (
        lax.psum(normed_one_part.astype(jnp.bfloat16), "tensor").astype(jnp.float32),
        lax.psum(query_gain_part.astype(jnp.bfloat16), "tensor").astype(jnp.float32),
        lax.psum(key_gain_part.astype(jnp.bfloat16), "tensor").astype(jnp.float32),
    )
    first_gain_grad = jnp.sum(grad_normed_one * unit_one, axis=0)
    input_grad = (grad_state + norm_back(grad_normed_one, gain_one, unit_one, inverse_one)).astype(
        jnp.bfloat16
    )
    shards = (
        lax.psum_scatter(
            query_grad.astype(jnp.bfloat16), "expert", scatter_dimension=0, tiled=True
        ).astype(jnp.float32),
        lax.psum_scatter(
            key_grad.astype(jnp.bfloat16), "expert", scatter_dimension=0, tiled=True
        ).astype(jnp.float32),
        lax.psum_scatter(
            value_grad.astype(jnp.bfloat16), "expert", scatter_dimension=0, tiled=True
        ).astype(jnp.float32),
        lax.psum_scatter(
            proj_grad.astype(jnp.bfloat16), "expert", scatter_dimension=1, tiled=True
        ).astype(jnp.float32),
        lax.psum_scatter(
            first_gain_grad.astype(jnp.bfloat16), "expert", scatter_dimension=0, tiled=True
        ).astype(jnp.float32),
        lax.psum_scatter(
            second_gain_grad.astype(jnp.bfloat16), "expert", scatter_dimension=0, tiled=True
        ).astype(jnp.float32),
        lax.psum_scatter(
            query_gain_total.astype(jnp.bfloat16), "expert", scatter_dimension=0, tiled=True
        ).astype(jnp.float32),
        lax.psum_scatter(
            key_gain_total.astype(jnp.bfloat16), "expert", scatter_dimension=0, tiled=True
        ).astype(jnp.float32),
        lax.psum_scatter(
            router_grad.astype(jnp.bfloat16), "expert", scatter_dimension=0, tiled=True
        ).astype(jnp.float32),
    )
    back_out, back_grad = (
        lax.all_to_all(
            output.reshape(1, token_rows, model_width),
            "expert",
            split_axis=1,
            concat_axis=0,
            tiled=True,
        ),
        lax.all_to_all(
            input_grad.reshape(1, token_rows, model_width),
            "expert",
            split_axis=1,
            concat_axis=0,
            tiled=True,
        ),
    )
    ordered_out = back_out[slot_of_seq]
    ordered_grad = back_grad[slot_of_seq]
    return (
        ordered_out,
        ordered_grad,
        shards[0],
        shards[1],
        shards[2],
        shards[3],
        shards[4],
        shards[5],
        shards[6],
        shards[7],
        shards[8],
        gate_grad,
        up_grad,
        down_grad,
    )


def on_device_paired(
    inputs,
    cotangent,
    lengths,
    permutation,
    routes,
    query_weight,
    key_weight,
    value_weight,
    proj_weight,
    first_gain,
    second_gain,
    query_gain,
    key_gain,
    router_weight,
    gate_weight,
    up_weight,
    down_weight,
):
    model_width = inputs.shape[2]
    local_heads = query_weight.shape[1] // HD
    expert_count = router_weight.shape[1]
    groups_count = lax.axis_size("expert")
    local_experts = gate_weight.shape[0]
    slot_index = lax.axis_index("expert")
    seq_ids = jnp.arange(permutation.shape[0], dtype=jnp.int32)
    my_sequence = jnp.sum(jnp.where(seq_ids == slot_index, permutation, 0))
    my_length = jnp.sum(jnp.where(seq_ids == my_sequence, lengths, 0))
    slot_of_seq = jnp.sum(
        jnp.where(permutation[None, :] == seq_ids[:, None], seq_ids[None, :], 0), axis=1
    )
    dealt_in, dealt_grad = (
        lax.all_to_all(inputs[permutation], "expert", split_axis=0, concat_axis=1, tiled=True),
        lax.all_to_all(cotangent[permutation], "expert", split_axis=0, concat_axis=1, tiled=True),
    )
    token_rows = dealt_in.shape[1]
    capacity = token_rows * TOPK * 33 // (32 * expert_count)
    block_rows = min(512, token_rows)
    score_scale = math.sqrt(HD)
    gathered = (
        lax.all_gather(query_weight.astype(jnp.bfloat16), "expert", axis=0, tiled=True),
        lax.all_gather(key_weight.astype(jnp.bfloat16), "expert", axis=0, tiled=True),
        lax.all_gather(value_weight.astype(jnp.bfloat16), "expert", axis=0, tiled=True),
        lax.all_gather(proj_weight.astype(jnp.bfloat16), "expert", axis=1, tiled=True),
        lax.all_gather(first_gain.astype(jnp.bfloat16), "expert", axis=0, tiled=True),
        lax.all_gather(second_gain.astype(jnp.bfloat16), "expert", axis=0, tiled=True),
        lax.all_gather(query_gain.astype(jnp.bfloat16), "expert", axis=0, tiled=True),
        lax.all_gather(key_gain.astype(jnp.bfloat16), "expert", axis=0, tiled=True),
        lax.all_gather(router_weight.astype(jnp.bfloat16), "expert", axis=0, tiled=True),
    )
    query_matrix = gathered[0]
    key_matrix = gathered[1]
    value_matrix = gathered[2]
    proj_matrix = gathered[3]
    gain_one = gathered[4].astype(jnp.float32)
    gain_two = gathered[5].astype(jnp.float32)
    gain_query = gathered[6].astype(jnp.float32)
    gain_key = gathered[7].astype(jnp.float32)
    router_matrix = gathered[8]
    gate_matrix = gate_weight.astype(jnp.bfloat16)
    up_matrix = up_weight.astype(jnp.bfloat16)
    down_matrix = down_weight.astype(jnp.bfloat16)
    source = dealt_in.reshape(token_rows, model_width).astype(jnp.float32)
    normed_one_f, unit_one, inverse_one = norm_parts(source, gain_one)
    normed_one = normed_one_f.astype(jnp.bfloat16)
    queries_raw = jnp.dot(normed_one, query_matrix, preferred_element_type=jnp.float32).reshape(
        token_rows, local_heads, HD
    )
    keys_raw = jnp.dot(normed_one, key_matrix, preferred_element_type=jnp.float32).reshape(
        token_rows, local_heads, HD
    )
    values = (
        jnp.dot(normed_one, value_matrix, preferred_element_type=jnp.float32)
        .astype(jnp.bfloat16)
        .reshape(token_rows, local_heads, HD)
    )
    cos_table, sin_table = rope_tables(token_rows, HD)
    query_normed, query_unit, query_inverse = norm_parts(queries_raw, gain_query)
    key_normed, key_unit, key_inverse = norm_parts(keys_raw, gain_key)
    queries = rotate(query_normed, cos_table, sin_table).astype(jnp.bfloat16)
    keys_rot = rotate(key_normed, cos_table, sin_table).astype(jnp.bfloat16)
    usable = jnp.arange(token_rows) < my_length

    def block_scores():
        scores = (
            jnp.einsum("qhd,khd->hqk", queries, keys_rot, preferred_element_type=jnp.float32)
            / score_scale
        )
        return (queries, jnp.where(usable[None, None, :], scores, NEG_FILL))

    query_block, scores = block_scores()
    maximum = jnp.max(scores, axis=-1, keepdims=True)
    exponent = jnp.exp(scores - maximum)
    row_total = jnp.sum(exponent, axis=-1, keepdims=True)
    softmax_rows = (exponent / row_total).astype(jnp.bfloat16)
    context_blocks = jnp.einsum(
        "hqk,khd->qhd", softmax_rows, values, preferred_element_type=jnp.float32
    ).astype(jnp.bfloat16)
    lse_blocks = [maximum + jnp.log(row_total)]
    context = context_blocks.reshape(token_rows, local_heads * HD)
    attn_part = jnp.dot(context, proj_matrix, preferred_element_type=jnp.float32)
    attn_total = lax.psum(attn_part, "tensor")
    residual = source + attn_total
    normed_two_f, unit_two, inverse_two = norm_parts(residual, gain_two)
    normed_two = normed_two_f.astype(jnp.bfloat16)
    logits = jnp.dot(normed_two, router_matrix, preferred_element_type=jnp.float32)
    choose = (
        routes[:, :, None] == jnp.arange(expert_count, dtype=jnp.int32)[None, None, :]
    ).astype(jnp.float32)
    chosen = jnp.sum(choose * logits[:, None, :], axis=-1)
    gate_probs = jax.nn.softmax(chosen, axis=-1)
    flat_routes = routes.reshape(-1)
    route_hits = (
        flat_routes[:, None] == jnp.arange(expert_count, dtype=jnp.int32)[None, :]
    ).astype(jnp.int32)
    rank_ids = jnp.sum(jnp.cumsum(route_hits, axis=0) * route_hits, axis=1) - 1
    slot_ids = flat_routes * capacity + rank_ids
    pair_tokens = jnp.arange(flat_routes.shape[0], dtype=jnp.int32) // TOPK
    send_rows = (
        jnp.zeros((expert_count * capacity, model_width), jnp.bfloat16)
        .at[slot_ids]
        .set(normed_two[pair_tokens])
    )
    send_rows = send_rows.reshape(groups_count, local_experts, capacity, model_width)
    received = lax.all_to_all(send_rows, "expert", split_axis=0, concat_axis=0, tiled=True)
    gate_pre = jnp.einsum(
        "secd,edf->secf", received, gate_matrix, preferred_element_type=jnp.float32
    )
    up_pre = jnp.einsum("secd,edf->secf", received, up_matrix, preferred_element_type=jnp.float32)
    hidden = (jax.nn.silu(gate_pre) * up_pre).astype(jnp.bfloat16)
    result = jnp.einsum(
        "secf,efd->secd", hidden, down_matrix, preferred_element_type=jnp.float32
    ).astype(jnp.bfloat16)
    returned = lax.all_to_all(result, "expert", split_axis=0, concat_axis=0, tiled=True)
    picked = returned.reshape(expert_count * capacity, model_width)[slot_ids].reshape(
        token_rows, TOPK, model_width
    )
    combined = jnp.sum(gate_probs[:, :, None] * picked.astype(jnp.float32), axis=1)
    moe_total = lax.psum(combined.astype(jnp.bfloat16), "tensor").astype(jnp.float32)
    output = (residual + moe_total).astype(jnp.bfloat16)
    grad_out = dealt_grad.reshape(token_rows, model_width).astype(jnp.float32)
    gate_grad_part = jnp.sum(grad_out[:, None, :] * picked.astype(jnp.float32), axis=-1)
    routed_grad = (
        (gate_probs[:, :, None] * grad_out[:, None, :])
        .astype(jnp.bfloat16)
        .reshape(token_rows * TOPK, model_width)
    )
    grad_send = (
        jnp.zeros((expert_count * capacity, model_width), jnp.bfloat16)
        .at[slot_ids]
        .set(routed_grad)
    )
    grad_send = grad_send.reshape(groups_count, local_experts, capacity, model_width)
    grad_rows, rows_in = (
        lax.all_to_all(grad_send, "expert", split_axis=0, concat_axis=0, tiled=True),
        lax.all_to_all(send_rows, "expert", split_axis=0, concat_axis=0, tiled=True),
    )
    gate_pre = jnp.einsum(
        "secd,edf->secf", rows_in, gate_matrix, preferred_element_type=jnp.float32
    )
    up_pre = jnp.einsum("secd,edf->secf", rows_in, up_matrix, preferred_element_type=jnp.float32)
    grad_hidden = jnp.einsum(
        "secd,efd->secf", grad_rows, down_matrix, preferred_element_type=jnp.float32
    )
    sigmoid_gate = jax.nn.sigmoid(gate_pre)
    silu_gate = gate_pre * sigmoid_gate
    grad_gate_pre = (
        grad_hidden * up_pre * sigmoid_gate * (1.0 + gate_pre * (1.0 - sigmoid_gate))
    ).astype(jnp.bfloat16)
    grad_up_pre = (grad_hidden * silu_gate).astype(jnp.bfloat16)
    hidden = (silu_gate * up_pre).astype(jnp.bfloat16)
    rows_grad = (
        jnp.einsum("secf,edf->secd", grad_gate_pre, gate_matrix, preferred_element_type=jnp.float32)
        + jnp.einsum("secf,edf->secd", grad_up_pre, up_matrix, preferred_element_type=jnp.float32)
    ).astype(jnp.bfloat16)
    down_grad = jnp.einsum("secf,secd->efd", hidden, grad_rows, preferred_element_type=jnp.float32)
    gate_grad = jnp.einsum(
        "secd,secf->edf", rows_in, grad_gate_pre, preferred_element_type=jnp.float32
    )
    up_grad = jnp.einsum("secd,secf->edf", rows_in, grad_up_pre, preferred_element_type=jnp.float32)
    returned_grad = lax.all_to_all(rows_grad, "expert", split_axis=0, concat_axis=0, tiled=True)
    returned_pairs = returned_grad.reshape(expert_count * capacity, model_width)[slot_ids].reshape(
        token_rows, TOPK, model_width
    )
    normed_two_part = jnp.sum(returned_pairs.astype(jnp.float32), axis=1)
    grad_normed_two, gate_grad_total = lax.psum((normed_two_part, gate_grad_part), "tensor")
    grad_chosen = gate_probs * (
        gate_grad_total - jnp.sum(gate_probs * gate_grad_total, axis=-1, keepdims=True)
    )
    grad_logits = jnp.sum(choose * grad_chosen[:, :, None], axis=1).astype(jnp.bfloat16)
    grad_normed_two = grad_normed_two + jnp.dot(
        grad_logits, router_matrix.T, preferred_element_type=jnp.float32
    )
    router_grad = jnp.dot(normed_two.T, grad_logits, preferred_element_type=jnp.float32)
    second_gain_grad = jnp.sum(grad_normed_two * unit_two, axis=0)
    grad_state = grad_out + norm_back(grad_normed_two, gain_two, unit_two, inverse_two)
    grad_context_in = grad_state.astype(jnp.bfloat16)
    proj_grad = jnp.dot(context.T, grad_context_in, preferred_element_type=jnp.float32)
    grad_context = (
        jnp.dot(grad_context_in, proj_matrix.T, preferred_element_type=jnp.float32)
        .astype(jnp.bfloat16)
        .reshape(token_rows, local_heads, HD)
    )
    grad_values = jnp.zeros((token_rows, local_heads, HD), jnp.float32)
    grad_keys_rot = jnp.zeros((token_rows, local_heads, HD), jnp.float32)
    grad_query_blocks = []
    for number, start_row in enumerate(range(0, token_rows, block_rows)):
        query_block, scores = block_scores()
        softmax_f = jnp.exp(scores - lse_blocks[number])
        grad_values = jnp.einsum(
            "hqk,qhd->khd",
            softmax_f.astype(jnp.bfloat16),
            grad_context,
            preferred_element_type=jnp.float32,
        )
        grad_probs = jnp.einsum(
            "qhd,khd->hqk", grad_context, values, preferred_element_type=jnp.float32
        )
        grad_scores = (
            softmax_f * (grad_probs - jnp.sum(grad_probs * softmax_f, axis=-1, keepdims=True))
        ).astype(jnp.bfloat16)
        grad_query_blocks.append(
            jnp.einsum("hqk,khd->qhd", grad_scores, keys_rot, preferred_element_type=jnp.float32)
            / score_scale
        )
        grad_keys_rot = (
            jnp.einsum("hqk,qhd->khd", grad_scores, query_block, preferred_element_type=jnp.float32)
            / score_scale
        )
    grad_queries_n = rotate(grad_query_blocks[0], cos_table, -sin_table)
    grad_keys_n = rotate(grad_keys_rot, cos_table, -sin_table)
    query_gain_part = jnp.sum(grad_queries_n * query_unit, axis=(0, 1))
    key_gain_part = jnp.sum(grad_keys_n * key_unit, axis=(0, 1))
    grad_queries_raw = (
        norm_back(grad_queries_n, gain_query, query_unit, query_inverse)
        .astype(jnp.bfloat16)
        .reshape(token_rows, local_heads * HD)
    )
    grad_keys_raw = (
        norm_back(grad_keys_n, gain_key, key_unit, key_inverse)
        .astype(jnp.bfloat16)
        .reshape(token_rows, local_heads * HD)
    )
    grad_values_low = grad_values.astype(jnp.bfloat16).reshape(token_rows, local_heads * HD)
    query_grad = jnp.dot(normed_one.T, grad_queries_raw, preferred_element_type=jnp.float32)
    key_grad = jnp.dot(normed_one.T, grad_keys_raw, preferred_element_type=jnp.float32)
    value_grad = jnp.dot(normed_one.T, grad_values_low, preferred_element_type=jnp.float32)
    normed_one_part = jnp.dot(grad_queries_raw, query_matrix.T, preferred_element_type=jnp.float32)
    normed_one_part = normed_one_part + jnp.dot(
        grad_keys_raw, key_matrix.T, preferred_element_type=jnp.float32
    )
    normed_one_part = normed_one_part + jnp.dot(
        grad_values_low, value_matrix.T, preferred_element_type=jnp.float32
    )
    grad_normed_one, query_gain_total, key_gain_total = (
        lax.psum(normed_one_part.astype(jnp.bfloat16), "tensor").astype(jnp.float32),
        lax.psum(query_gain_part.astype(jnp.bfloat16), "tensor").astype(jnp.float32),
        lax.psum(key_gain_part.astype(jnp.bfloat16), "tensor").astype(jnp.float32),
    )
    first_gain_grad = jnp.sum(grad_normed_one * unit_one, axis=0)
    input_grad = (grad_state + norm_back(grad_normed_one, gain_one, unit_one, inverse_one)).astype(
        jnp.bfloat16
    )
    shards = (
        lax.psum_scatter(
            query_grad.astype(jnp.bfloat16), "expert", scatter_dimension=0, tiled=True
        ).astype(jnp.float32),
        lax.psum_scatter(
            key_grad.astype(jnp.bfloat16), "expert", scatter_dimension=0, tiled=True
        ).astype(jnp.float32),
        lax.psum_scatter(
            value_grad.astype(jnp.bfloat16), "expert", scatter_dimension=0, tiled=True
        ).astype(jnp.float32),
        lax.psum_scatter(
            proj_grad.astype(jnp.bfloat16), "expert", scatter_dimension=1, tiled=True
        ).astype(jnp.float32),
        lax.psum_scatter(
            first_gain_grad.astype(jnp.bfloat16), "expert", scatter_dimension=0, tiled=True
        ).astype(jnp.float32),
        lax.psum_scatter(
            second_gain_grad.astype(jnp.bfloat16), "expert", scatter_dimension=0, tiled=True
        ).astype(jnp.float32),
        lax.psum_scatter(
            query_gain_total.astype(jnp.bfloat16), "expert", scatter_dimension=0, tiled=True
        ).astype(jnp.float32),
        lax.psum_scatter(
            key_gain_total.astype(jnp.bfloat16), "expert", scatter_dimension=0, tiled=True
        ).astype(jnp.float32),
        lax.psum_scatter(
            router_grad.astype(jnp.bfloat16), "expert", scatter_dimension=0, tiled=True
        ).astype(jnp.float32),
    )
    back_out, back_grad = (
        lax.all_to_all(
            output.reshape(1, token_rows, model_width),
            "expert",
            split_axis=1,
            concat_axis=0,
            tiled=True,
        ),
        lax.all_to_all(
            input_grad.reshape(1, token_rows, model_width),
            "expert",
            split_axis=1,
            concat_axis=0,
            tiled=True,
        ),
    )
    ordered_out = back_out[slot_of_seq]
    ordered_grad = back_grad[slot_of_seq]
    return (
        ordered_out,
        ordered_grad,
        shards[0],
        shards[1],
        shards[2],
        shards[3],
        shards[4],
        shards[5],
        shards[6],
        shards[7],
        shards[8],
        gate_grad,
        up_grad,
        down_grad,
    )


def solution(mesh):
    in_specs = (
        P(None, "expert", None),
        P(None, "expert", None),
        P(),
        P(),
        P("expert", None),
        P("expert", "tensor"),
        P("expert", "tensor"),
        P("expert", "tensor"),
        P("tensor", "expert"),
        P("expert"),
        P("expert"),
        P("expert"),
        P("expert"),
        P("expert", None),
        P("expert", None, "tensor"),
        P("expert", None, "tensor"),
        P("expert", "tensor", None),
    )
    out_specs = (
        P(None, "expert", None),
        P(None, "expert", None),
        P("expert", "tensor"),
        P("expert", "tensor"),
        P("expert", "tensor"),
        P("tensor", "expert"),
        P("expert"),
        P("expert"),
        P("expert"),
        P("expert"),
        P("expert", None),
        P("expert", None, "tensor"),
        P("expert", None, "tensor"),
        P("expert", "tensor", None),
    )
    few = mesh.shape["expert"] * mesh.shape["tensor"] <= 32
    return jax.shard_map(
        on_device if few else on_device_paired, mesh=mesh, in_specs=in_specs, out_specs=out_specs, check_vma=False
    )
```

```python
import functools
import math

import jax
import jax.numpy as jnp
from jax import lax
from jax.experimental import pallas as pl
from jax.experimental.pallas import tpu as pltpu
from jax.sharding import PartitionSpec as P

HD = 128
TOPK = 8


EPS = 1e-06
ROPE_BASE = 50000.0
NEG_FILL = -1e30


def norm_parts(values, gain):
    inverse = lax.rsqrt(jnp.mean(values * values, axis=-1, keepdims=True) + EPS)
    unit_rows = values * inverse
    return (unit_rows * gain, unit_rows, inverse)


def norm_back(grad_normed, gain, unit_rows, inverse):
    grad_unit = grad_normed * gain
    inner_mean = jnp.mean(grad_unit * unit_rows, axis=-1, keepdims=True)
    return inverse * (grad_unit - unit_rows * inner_mean)


def rope_tables(seq_count, width):
    halfway = width // 2
    frequency = jnp.power(ROPE_BASE, -jnp.arange(halfway, dtype=jnp.float32) * (2.0 / width))
    angles = jnp.arange(seq_count, dtype=jnp.float32)[:, None] * frequency[None, :]
    return (jnp.cos(angles)[:, None, :], jnp.sin(angles)[:, None, :])


def rotate(values, cos_table, sin_table):
    halfway = values.shape[-1] // 2
    former = values[..., :halfway]
    latter = values[..., halfway:]
    return jnp.concatenate(
        [former * cos_table - latter * sin_table, latter * cos_table + former * sin_table], axis=-1
    )


MESH = pl.DeviceIdType.MESH
UP, DOWN, ACROSS_X, ACROSS_Y, DIAG_X, DIAG_Y, PAIR = range(7)


def position():
    group, member = lax.axis_index("expert"), lax.axis_index("tensor")
    return lax.rem(group, 2), lax.div(member, 2), lax.div(group, 2), lax.rem(member, 2)


def device(x, y, z, c):
    return (z * 2 + x, y * 2 + c)


def greet(line, extra=0):
    x, y, z, c = position()
    barrier = pltpu.get_barrier_semaphore()

    def signal(to):
        pl.semaphore_signal(barrier, inc=1, device_id=to, device_id_type=MESH)

    signal(device(1 - x, y, z, c))
    signal(device(x, 1 - y, z, c))
    signal(device(x, y, z, 1 - c))
    pl.when(z > 0)(lambda: signal(device(x, y, z - 1, c)))
    pl.when(z < line - 1)(lambda: signal(device(x, y, z + 1, c)))
    near = 3 + (z > 0).astype(jnp.int32) + (z < line - 1).astype(jnp.int32)
    pl.semaphore_wait(barrier, near + extra)


def gather_steps(line, pair, ins, outs, send, recv, local, between=None):
    x, y, z, c = position()
    count = len(ins)
    deep = ins[0].shape[1]

    def place(i, xx, yy, zz, cc):
        first = 2 * yy + (4 * cc if pair else 0)
        return outs[i].at[pl.ds(first, 2), pl.ds((zz * 2 + xx) * deep, deep)]

    def copy(i, kind, block, to, own):
        slot = kind * line + block[2]
        return pltpu.make_async_remote_copy(
            src_ref=ins[i] if own else place(i, *block),
            dst_ref=place(i, *block),
            send_sem=send.at[i, slot],
            recv_sem=recv.at[i, slot],
            device_id=to,
            device_id_type=MESH,
        )

    x_side, y_side = device(1 - x, y, z, c), device(x, 1 - y, z, c)
    sibling = device(x, y, z, 1 - c)
    sends = []

    def push(kind, block, to, own=False, when=None):
        def start():
            for i in range(count):
                copy(i, kind, block, to, own).start()

        def finish():
            for i in range(count):
                copy(i, kind, block, to, own).wait_send()

        if when is None:
            start()
        else:
            pl.when(when)(start)
        sends.append((finish, when))

    def both(one, two):
        return two if one is None else one & two

    def arrive(kind, block, frm):
        for i in range(count):
            copy(i, kind, block, frm, False).wait_recv()

    mine = (x, y, z, c)
    below, above = device(x, y, z - 1, c), device(x, y, z + 1, c)
    push(UP, mine, above, True, z < line - 1)
    push(DOWN, mine, below, True, z > 0)
    push(ACROSS_X, mine, x_side, True)
    push(ACROSS_Y, mine, y_side, True)
    if pair:
        push(PAIR, mine, sibling, True)
    homes = [pltpu.make_async_copy(ins[i], place(i, *mine), local.at[i]) for i in range(count)]
    for home in homes:
        home.start()
    if between is not None:
        between()

    for step in range(line):
        signs = (0,) if step == 0 else (-1, 1)
        for sign in signs:
            zz = z + sign * step
            valid = None if step == 0 else (zz >= 0) & (zz < line)
            block = (x, y, zz, c)
            if step > 0:
                kind, frm = (UP, below) if sign < 0 else (DOWN, above)
                pl.when(valid)(functools.partial(arrive, kind, block, frm))
                if sign < 0:
                    push(UP, block, above, False, valid & (z < line - 1))
                else:
                    push(DOWN, block, below, False, valid & (z > 0))
                push(ACROSS_X, block, x_side, False, valid)
                push(ACROSS_Y, block, y_side, False, valid)
                if pair:
                    push(PAIR, block, sibling, False, valid)
        for sign in signs:
            zz = z + sign * step
            valid = None if step == 0 else (zz >= 0) & (zz < line)
            even = lax.rem(zz + line, 2) == 0
            if line % 2:
                even = ~even

            def take(kind, block, frm, valid=valid):
                go = functools.partial(arrive, kind, block, frm)
                if valid is None:
                    go()
                else:
                    pl.when(valid)(go)

            block = (1 - x, y, zz, c)
            take(ACROSS_X, block, x_side)
            push(DIAG_Y, block, y_side, False, both(valid, ~even))
            if pair:
                push(PAIR + 1, block, sibling, False, valid)
            block = (x, 1 - y, zz, c)
            take(ACROSS_Y, block, y_side)
            push(DIAG_X, block, x_side, False, both(valid, even))
            if pair:
                push(PAIR + 2, block, sibling, False, valid)
    for zz in range(line):
        block = (1 - x, 1 - y, zz, c)
        if zz % 2 == 0:
            arrive(DIAG_X, block, x_side)
        else:
            arrive(DIAG_Y, block, y_side)
        if pair:
            push(PAIR + 3, block, sibling)
    if pair:
        for zz in range(line):
            for way, (xx, yy) in enumerate(((x, y), (1 - x, y), (x, 1 - y), (1 - x, 1 - y))):
                arrive(PAIR + way, (xx, yy, zz, 1 - c), sibling)
    for home in homes:
        home.wait()
    for finish, when in sends:
        if when is None:
            finish()
        else:
            pl.when(when)(finish)


def gather_kernel(line, pair, count, *refs):
    ins, outs = refs[:count], refs[count : 2 * count]
    send, recv, local = refs[2 * count :]
    greet(line)
    gather_steps(line, pair, ins, outs, send, recv, local)


def gather_rows(arrays, line, pair, collective_id):
    count = len(arrays)
    kinds = PAIR + (4 if pair else 0)
    return pl.pallas_call(
        functools.partial(gather_kernel, line, pair, count),
        out_shape=[
            jax.ShapeDtypeStruct((8 if pair else 4, a.shape[1] * line * 2, a.shape[2]), a.dtype)
            for a in arrays
        ],
        in_specs=[pl.BlockSpec(memory_space=pltpu.VMEM)] * count,
        out_specs=[pl.BlockSpec(memory_space=pl.ANY)] * count,
        scratch_shapes=[
            pltpu.SemaphoreType.DMA((count, kinds * line)),
            pltpu.SemaphoreType.DMA((count, kinds * line)),
            pltpu.SemaphoreType.DMA((count,)),
        ],
        compiler_params=pltpu.CompilerParams(collective_id=collective_id, has_side_effects=True),
    )(*arrays)


def reduce_steps(line, pair, parts, outs, scratches, between=None):
    work = [
        reduce_phases(line, pair, part, out, *scratch)
        for part, out, scratch in zip(parts, outs, scratches)
    ]
    for phase in range(5):
        for phases in work:
            phases[phase]()
        if phase == 1 and between is not None:
            between()


def reduce_phases(line, pair, part, out, diag, side_x, side_y, rise, fall, twin, send, recv):
    x, y, z, c = position()
    deep = out.shape[1]
    columns = ((x, y), (1 - x, y), (x, 1 - y), (1 - x, 1 - y))
    x_side, y_side = device(1 - x, y, z, c), device(x, 1 - y, z, c)
    sibling = device(x, y, z, 1 - c)
    below, above = device(x, y, z - 1, c), device(x, y, z + 1, c)
    sends = []

    def slab(way, zz, cc):
        xx, yy = columns[way]
        first = 2 * yy + (4 * cc if pair else 0)
        return part.at[pl.ds(first, 2), pl.ds((zz * 2 + xx) * deep, deep)]

    def copy(kind, zz, src, dst, to):
        return pltpu.make_async_remote_copy(
            src_ref=src,
            dst_ref=dst.at[zz],
            send_sem=send.at[kind * line + zz],
            recv_sem=recv.at[kind * line + zz],
            device_id=to,
            device_id_type=MESH,
        )

    def push(kind, zz, src, dst, to):
        copy(kind, zz, src, dst, to).start()

    def landed(kind, zz, dst, frm):
        copy(kind, zz, dst.at[zz], dst, frm).wait_recv()

    def total(target, *terms):
        def some(n, carry):
            k, r = lax.div(n, deep // 16), pl.multiple_of(lax.rem(n, deep // 16) * 16, 16)
            value = terms[0][k, pl.ds(r, 16)].astype(jnp.float32)
            for term in terms[1:]:
                value = value + term[k, pl.ds(r, 16)].astype(jnp.float32)
            target[k, pl.ds(r, 16)] = value.astype(target.dtype)
            return carry

        lax.fori_loop(0, 2 * (deep // 16), some, 0)

    def base(way, zz):
        return twin.at[way, zz] if pair else slab(way, zz, c)

    def paired(way, zz):
        if pair:
            spot = twin.at[way]
            landed(PAIR + way, zz, spot, sibling)
            total(spot.at[zz], slab(way, zz, c), spot.at[zz])

    def halves():
        if pair:
            for way in (3, 1, 2, 0):
                for zz in range(line):
                    push(PAIR + way, zz, slab(way, zz, 1 - c), twin.at[way], sibling)

    def corner():
        for zz in range(line):
            paired(3, zz)
            if zz % 2 == 0:
                push(DIAG_X, zz, base(3, zz), diag, x_side)
            else:
                push(DIAG_Y, zz, base(3, zz), diag, y_side)

    def order(body):
        for step in range(line - 1, -1, -1):
            for sign in (0,) if step == 0 else (-1, 1):
                zz = z + sign * step
                go = functools.partial(body, zz, sign)
                if step == 0:
                    go()
                else:
                    pl.when((zz >= 0) & (zz < line))(go)

    def across(zz, sign):
        even = lax.rem(zz, 2) == 0
        paired(1, zz)
        paired(2, zz)

        @pl.when(even)
        def _():
            push(ACROSS_X, zz, base(1, zz), side_x, x_side)
            landed(DIAG_X, zz, diag, x_side)
            total(diag.at[zz], base(2, zz), diag.at[zz])
            push(ACROSS_Y, zz, diag.at[zz], side_y, y_side)

        @pl.when(~even)
        def _():
            push(ACROSS_Y, zz, base(2, zz), side_y, y_side)
            landed(DIAG_Y, zz, diag, y_side)
            total(diag.at[zz], base(1, zz), diag.at[zz])
            push(ACROSS_X, zz, diag.at[zz], side_x, x_side)

    def along(zz, sign):
        paired(0, zz)
        landed(ACROSS_X, zz, side_x, x_side)
        landed(ACROSS_Y, zz, side_y, y_side)
        spot = out if sign == 0 else side_x.at[zz]
        near = (base(0, zz), side_x.at[zz], side_y.at[zz])
        if sign > 0:
            @pl.when(z > 0)
            def _():
                landed(UP, zz, rise, below)
                total(spot, *near, rise.at[zz])

            @pl.when(z == 0)
            def _():
                total(spot, *near)

            push(UP, zz, spot, rise, above)
        elif sign < 0:
            @pl.when(z < line - 1)
            def _():
                landed(DOWN, zz, fall, above)
                total(spot, *near, fall.at[zz])

            @pl.when(z == line - 1)
            def _():
                total(spot, *near)

            push(DOWN, zz, spot, fall, below)
        else:
            @pl.when((z > 0) & (z < line - 1))
            def _():
                landed(UP, zz, rise, below)
                landed(DOWN, zz, fall, above)
                total(spot, *near, rise.at[zz], fall.at[zz])

            @pl.when(z == 0)
            def _():
                landed(DOWN, zz, fall, above)
                total(spot, *near, fall.at[zz])

            @pl.when(z == line - 1)
            def _():
                landed(UP, zz, rise, below)
                total(spot, *near, rise.at[zz])

    def sent(kind, zz, dst, to):
        copy(kind, zz, dst.at[zz], dst, to).wait_send()

    def drain():
        for zz in range(line):
            leave(zz)

    def leave(zz):
        if pair:
            for way in range(4):
                sent(PAIR + way, zz, twin.at[way], sibling)
        sent(DIAG_X if zz % 2 == 0 else DIAG_Y, zz, diag, x_side if zz % 2 == 0 else y_side)
        sent(ACROSS_X, zz, side_x, x_side)
        sent(ACROSS_Y, zz, side_y, y_side)
        pl.when(zz > z)(functools.partial(sent, UP, zz, rise, above))
        pl.when(zz < z)(functools.partial(sent, DOWN, zz, fall, below))

    return (
        halves,
        corner,
        functools.partial(order, across),
        functools.partial(order, along),
        drain,
    )


def reduce_kernel(line, pair, count, *refs):
    parts, outs, rest = refs[:count], refs[count : 2 * count], refs[2 * count :]
    greet(line)
    reduce_steps(line, pair, parts, outs, [rest[8 * i : 8 * i + 8] for i in range(count)])


def reduce_scratch(line, pair, deep, width, dtype):
    kinds = PAIR + (4 if pair else 0)
    block = (line, 2, deep, width)
    return [pltpu.VMEM(block, dtype)] * 5 + [
        pltpu.VMEM((4,) + block if pair else (8, 128), dtype),
        pltpu.SemaphoreType.DMA((kinds * line,)),
        pltpu.SemaphoreType.DMA((kinds * line,)),
    ]


def reduce_rows(parts, line, pair, collective_id):
    count, deep = len(parts), parts[0].shape[1] // (2 * line)
    scratch = []
    for part in parts:
        scratch += reduce_scratch(line, pair, deep, part.shape[2], part.dtype)
    return pl.pallas_call(
        functools.partial(reduce_kernel, line, pair, count),
        out_shape=[jax.ShapeDtypeStruct((2, deep, part.shape[2]), jnp.float32) for part in parts],
        in_specs=[pl.BlockSpec(memory_space=pltpu.VMEM)] * count,
        out_specs=[pl.BlockSpec(memory_space=pltpu.VMEM)] * count,
        scratch_shapes=scratch,
        compiler_params=pltpu.CompilerParams(
            collective_id=collective_id, has_side_effects=True, vmem_limit_bytes=60 << 20
        ),
    )(*parts)


def gathered_with_weights(line, rows, cut, proj_cut, small, *rest):
    all_rows, head_weight, head_proj, all_small, send, recv, local, wsend, wrecv, wlocal = rest
    x, y, z, c = position()
    group, groups = lax.axis_index("expert"), 2 * line
    member = lax.axis_index("tensor")
    deep, wide = cut.shape[1], proj_cut.shape[2]
    parts = cut.shape[0]
    sibling = device(x, y, z, 1 - c)
    barrier = pltpu.get_barrier_semaphore()
    for hop in range(1, groups):
        pl.semaphore_signal(
            barrier, inc=1, device_id=(lax.rem(group + hop, groups), member), device_id_type=MESH
        )
    pl.semaphore_signal(barrier, inc=1, device_id=sibling, device_id_type=MESH)
    pl.semaphore_signal(barrier, inc=1, device_id=device(x, 1 - y, z, c), device_id_type=MESH)
    pl.semaphore_wait(barrier, groups + 1)
    serves = lax.div(group, parts) == c

    def spots(origin):
        return (
            head_weight.at[pl.ds(origin * deep, deep)],
            head_proj.at[:, pl.ds(origin * wide, wide)],
        )

    def weight_copies(origin, sources, to, slot):
        return [
            pltpu.make_async_remote_copy(
                src_ref=source,
                dst_ref=spot,
                send_sem=wsend.at[which, slot],
                recv_sem=wrecv.at[which, origin],
                device_id=to,
                device_id_type=MESH,
            )
            for which, (source, spot) in enumerate(zip(sources, spots(origin)))
        ]

    def small_copy(origin, to, slot):
        return pltpu.make_async_remote_copy(
            src_ref=small,
            dst_ref=all_small.at[:, pl.ds(origin * small.shape[1], small.shape[1])],
            send_sem=wsend.at[2, slot],
            recv_sem=wrecv.at[2, origin],
            device_id=to,
            device_id_type=MESH,
        )

    def outgoing(n):
        return weight_copies(group, (cut.at[n], proj_cut.at[n]), (c * parts + n, member), n)

    own = lax.rem(group, parts)
    home = [
        pltpu.make_async_copy(source, spot, wlocal.at[which])
        for which, (source, spot) in enumerate(zip((cut.at[own], proj_cut.at[own]), spots(group)))
    ]
    small_home = pltpu.make_async_copy(
        small, all_small.at[:, pl.ds(group * small.shape[1], small.shape[1])], wlocal.at[2]
    )
    own_to_sibling = weight_copies(group, (cut.at[own], proj_cut.at[own]), sibling, parts)

    def everything(copies, act):
        for one in copies:
            getattr(one, act)()

    def begin():
        small_home.start()
        for hop in range(1, groups):
            small_copy(group, (lax.rem(group + hop, groups), member), hop).start()
        for n in range(parts):
            pl.when(c * parts + n != group)(functools.partial(everything, outgoing(n), "start"))

        @pl.when(serves)
        def _():
            everything(home, "start")
            everything(own_to_sibling, "start")

    gather_steps(line, False, (rows,), (all_rows,), send, recv, local, begin)
    for hop in range(1, groups):
        origin = lax.rem(group + hop, groups)
        copies = weight_copies(origin, spots(origin), sibling, parts + hop)
        everything(copies, "wait_recv")
        pl.when(serves)(functools.partial(everything, copies, "start"))
    pl.when(~serves)(functools.partial(everything, own_to_sibling, "wait_recv"))
    for hop in range(1, groups):
        small_copy(lax.rem(group + hop, groups), sibling, hop).wait_recv()
    small_home.wait()
    for n in range(parts):
        pl.when(c * parts + n != group)(functools.partial(everything, outgoing(n), "wait_send"))
    for hop in range(1, groups):
        small_copy(group, (lax.rem(group + hop, groups), member), hop).wait_send()

    @pl.when(serves)
    def _():
        everything(home, "wait")
        everything(own_to_sibling, "wait_send")
        for hop in range(1, groups):
            origin = lax.rem(group + hop, groups)
            everything(weight_copies(origin, spots(origin), sibling, parts + hop), "wait_send")


def gather_with_weights(rows, cut, proj_cut, small, line, collective_id):
    groups = 2 * line
    vmem = pl.BlockSpec(memory_space=pltpu.VMEM)
    anywhere = pl.BlockSpec(memory_space=pl.ANY)
    slots = cut.shape[0] + groups
    return pl.pallas_call(
        functools.partial(gathered_with_weights, line),
        out_shape=[
            jax.ShapeDtypeStruct((4, rows.shape[1] * groups, rows.shape[2]), rows.dtype),
            jax.ShapeDtypeStruct((groups * cut.shape[1], cut.shape[2]), cut.dtype),
            jax.ShapeDtypeStruct((proj_cut.shape[1], groups * proj_cut.shape[2]), cut.dtype),
            jax.ShapeDtypeStruct((small.shape[0], groups * small.shape[1]), small.dtype),
        ],
        in_specs=[vmem] * 4,
        out_specs=[anywhere] * 4,
        scratch_shapes=[
            pltpu.SemaphoreType.DMA((1, PAIR * line)),
            pltpu.SemaphoreType.DMA((1, PAIR * line)),
            pltpu.SemaphoreType.DMA((1,)),
            pltpu.SemaphoreType.DMA((3, slots)),
            pltpu.SemaphoreType.DMA((3, groups)),
            pltpu.SemaphoreType.DMA((3,)),
        ],
        compiler_params=pltpu.CompilerParams(collective_id=collective_id, has_side_effects=True),
    )(rows, cut, proj_cut, small)


def spread_copies(own, full, send, recv):
    x, y, z, c = position()
    y_side, sibling = device(x, 1 - y, z, c), device(x, y, z, 1 - c)

    def spot(yy, cc):
        return full.at[pl.ds(4 * cc + 2 * yy, 2)]

    def copy(slot, source, yy, to):
        return pltpu.make_async_remote_copy(
            src_ref=source,
            dst_ref=spot(yy, c),
            send_sem=send.at[slot],
            recv_sem=recv.at[slot],
            device_id=to,
            device_id_type=MESH,
        )

    def incoming(slot, yy, cc, frm):
        return pltpu.make_async_remote_copy(
            src_ref=spot(yy, cc),
            dst_ref=spot(yy, cc),
            send_sem=send.at[slot],
            recv_sem=recv.at[slot],
            device_id=frm,
            device_id_type=MESH,
        )

    first = [copy(0, own, y, y_side), copy(1, own, y, sibling)]
    onward = copy(2, spot(1 - y, c), 1 - y, sibling)
    home = pltpu.make_async_copy(own, spot(y, c), send.at[3])

    def begin():
        home.start()
        for one in first:
            one.start()

    def finish():
        incoming(0, 1 - y, c, y_side).wait_recv()
        onward.start()
        incoming(1, y, 1 - c, sibling).wait_recv()
        incoming(2, 1 - y, 1 - c, sibling).wait_recv()
        home.wait()
        for one in first + [onward]:
            one.wait_send()

    return begin, finish


def gathered_and_spread(line, rows, own, all_rows, full, send, recv, local, ssend, srecv):
    greet(line)
    begin, finish = spread_copies(own, full, ssend, srecv)
    gather_steps(line, False, (rows,), (all_rows,), send, recv, local, begin)
    finish()


def gather_and_spread(rows, own, line, collective_id):
    groups = 2 * line
    return pl.pallas_call(
        functools.partial(gathered_and_spread, line),
        out_shape=[
            jax.ShapeDtypeStruct((4, rows.shape[1] * groups, rows.shape[2]), rows.dtype),
            jax.ShapeDtypeStruct((8,) + own.shape[1:], own.dtype),
        ],
        in_specs=[pl.BlockSpec(memory_space=pltpu.VMEM)] * 2,
        out_specs=[pl.BlockSpec(memory_space=pl.ANY)] * 2,
        scratch_shapes=[
            pltpu.SemaphoreType.DMA((1, PAIR * line)),
            pltpu.SemaphoreType.DMA((1, PAIR * line)),
            pltpu.SemaphoreType.DMA((1,)),
            pltpu.SemaphoreType.DMA((4,)),
            pltpu.SemaphoreType.DMA((4,)),
        ],
        compiler_params=pltpu.CompilerParams(collective_id=collective_id, has_side_effects=True),
    )(rows, own)


def reduced_with_weights(line, part, grad, proj_grad, out, cuts, proj_cuts, *rest):
    scratch, (other, proj_other, wsend, wrecv, wlocal) = rest[:8], rest[8:]
    x, y, z, c = position()
    group = lax.axis_index("expert")
    parts = cuts.shape[0]
    deep, wide = cuts.shape[1], proj_cuts.shape[2]
    sibling = device(x, y, z, 1 - c)
    side = lax.div(group, parts)
    barrier = pltpu.get_barrier_semaphore()
    for n in range(parts):
        peer = c * parts + n

        @pl.when((peer != group) | (side != c))
        def _():
            pl.semaphore_signal(
                barrier, inc=1, device_id=(peer, y * 2 + side), device_id_type=MESH
            )

    greet(line, parts - (side == c).astype(jnp.int32))
    half, proj_half = parts * deep, parts * wide
    to_sibling = [
        pltpu.make_async_remote_copy(
            src_ref=source,
            dst_ref=target,
            send_sem=wsend.at[which, parts],
            recv_sem=wrecv.at[which, parts],
            device_id=sibling,
            device_id_type=MESH,
        )
        for which, (source, target) in enumerate(
            (
                (grad.at[pl.ds((1 - c) * half, half)], other),
                (proj_grad.at[:, pl.ds((1 - c) * proj_half, proj_half)], proj_other),
            )
        )
    ]
    for one in to_sibling:
        one.start()

    def outgoing(n):
        return [
            pltpu.make_async_remote_copy(
                src_ref=source,
                dst_ref=target.at[lax.rem(group, parts)],
                send_sem=wsend.at[which, n],
                recv_sem=wrecv.at[which, lax.rem(group, parts)],
                device_id=(c * parts + n, y * 2 + side),
                device_id_type=MESH,
            )
            for which, (source, target) in enumerate(
                (
                    (other.at[pl.ds(n * deep, deep)], cuts),
                    (proj_other.at[:, pl.ds(n * wide, wide)], proj_cuts),
                )
            )
        ]

    def incoming(n):
        return [
            pltpu.make_async_remote_copy(
                src_ref=target.at[n],
                dst_ref=target.at[n],
                send_sem=wsend.at[which, n],
                recv_sem=wrecv.at[which, n],
                device_id=(c * parts + n, y * 2 + side),
                device_id_type=MESH,
            )
            for which, target in enumerate((cuts, proj_cuts))
        ]

    own = lax.rem(group, parts)
    home = [
        pltpu.make_async_copy(source, target, wlocal.at[which])
        for which, (source, target) in enumerate(
            (
                (other.at[pl.ds(own * deep, deep)], cuts.at[own]),
                (proj_other.at[:, pl.ds(own * wide, wide)], proj_cuts.at[own]),
            )
        )
    ]

    def remote(n):
        return (c * parts + n != group) | (side != c)

    def between():
        for one in to_sibling:
            one.wait_recv()

        def add(n, carry):
            r = pl.multiple_of(n * 16, 16)
            other[pl.ds(r, 16)] = (
                other[pl.ds(r, 16)].astype(jnp.float32)
                + grad[pl.ds(pl.multiple_of(c * half + n * 16, 16), 16)].astype(jnp.float32)
            ).astype(other.dtype)
            return carry

        lax.fori_loop(0, half // 16, add, 0)

        def add_proj(n, carry):
            r = pl.multiple_of(n * 16, 16)
            mine = proj_grad[pl.ds(r, 16), pl.ds(pl.multiple_of(c * proj_half, 128), proj_half)]
            proj_other[pl.ds(r, 16)] = (
                proj_other[pl.ds(r, 16)].astype(jnp.float32) + mine.astype(jnp.float32)
            ).astype(other.dtype)
            return carry

        lax.fori_loop(0, proj_other.shape[0] // 16, add_proj, 0)

        for n in range(parts):
            @pl.when(remote(n))
            def _():
                for one in outgoing(n):
                    one.start()

        @pl.when(side == c)
        def _():
            for one in home:
                one.start()

    reduce_steps(line, False, (part,), (out,), (scratch,), between)
    for n in range(parts):
        @pl.when(remote(n))
        def _():
            for one in incoming(n):
                one.wait_recv()
            for one in outgoing(n):
                one.wait_send()

    for one in to_sibling:
        one.wait_send()

    @pl.when(side == c)
    def _():
        for one in home:
            one.wait()


def reduce_with_weights(part, grad, proj_grad, line, collective_id):
    groups, parts = 2 * line, line
    deep, width = part.shape[1] // groups, part.shape[2]
    vmem = pl.BlockSpec(memory_space=pltpu.VMEM)
    cut = (parts, grad.shape[0] // groups, grad.shape[1])
    proj_cut = (parts, proj_grad.shape[0], proj_grad.shape[1] // groups)
    return pl.pallas_call(
        functools.partial(reduced_with_weights, line),
        out_shape=[
            jax.ShapeDtypeStruct((2, deep, width), jnp.float32),
            jax.ShapeDtypeStruct(cut, grad.dtype),
            jax.ShapeDtypeStruct(proj_cut, grad.dtype),
        ],
        in_specs=[vmem] * 3,
        out_specs=[vmem] * 3,
        scratch_shapes=reduce_scratch(line, False, deep, width, part.dtype)
        + [
            pltpu.VMEM((grad.shape[0] // 2, grad.shape[1]), grad.dtype),
            pltpu.VMEM((proj_grad.shape[0], proj_grad.shape[1] // 2), grad.dtype),
            pltpu.SemaphoreType.DMA((2, parts + 1)),
            pltpu.SemaphoreType.DMA((2, parts + 1)),
            pltpu.SemaphoreType.DMA((2,)),
        ],
        compiler_params=pltpu.CompilerParams(
            collective_id=collective_id, has_side_effects=True, vmem_limit_bytes=60 << 20
        ),
    )(part, grad, proj_grad)


def finished(line, own, small, full, total, ssend, srecv, held, tensor_held, send, recv):
    x, y, z, c = position()
    group, groups, member = lax.axis_index("expert"), 2 * line, lax.axis_index("tensor")
    barrier = pltpu.get_barrier_semaphore()
    for hop in range(1, groups):
        pl.semaphore_signal(
            barrier, inc=1, device_id=(lax.rem(group + hop, groups), member), device_id_type=MESH
        )
    for hop in range(1, 4):
        pl.semaphore_signal(
            barrier, inc=1, device_id=(group, lax.rem(member + hop, 4)), device_id_type=MESH
        )
    pl.semaphore_wait(barrier, groups + 2)
    wide = total.shape[1]

    def outgoing(hop):
        to = lax.rem(group + hop, groups)
        return pltpu.make_async_remote_copy(
            src_ref=small.at[:, pl.ds(to * wide, wide)],
            dst_ref=held.at[hop],
            send_sem=send.at[hop],
            recv_sem=recv.at[hop],
            device_id=(to, member),
            device_id_type=MESH,
        )

    def onward(hop):
        return pltpu.make_async_remote_copy(
            src_ref=held.at[0],
            dst_ref=tensor_held.at[hop],
            send_sem=send.at[groups + hop],
            recv_sem=recv.at[groups + hop],
            device_id=(group, lax.rem(member + hop, 4)),
            device_id_type=MESH,
        )

    for hop in range(1, groups):
        outgoing(hop).start()
    begin, finish = spread_copies(own, full, ssend, srecv)
    begin()
    value = small[:, pl.ds(pl.multiple_of(group * wide, 128), wide)]
    for hop in range(1, groups):
        outgoing(hop).wait_recv()
        value = value + held[hop]
    held[0] = value
    for hop in range(1, 4):
        onward(hop).start()
    finish()
    for hop in range(1, 4):
        onward(hop).wait_recv()
        value = value + tensor_held[hop]
    total[...] = value
    for hop in range(1, groups):
        outgoing(hop).wait_send()
    for hop in range(1, 4):
        onward(hop).wait_send()


def finish_rows(own, small, line, collective_id):
    groups = 2 * line
    vmem = pl.BlockSpec(memory_space=pltpu.VMEM)
    wide = small.shape[1] // groups
    return pl.pallas_call(
        functools.partial(finished, line),
        out_shape=[
            jax.ShapeDtypeStruct((8,) + own.shape[1:], own.dtype),
            jax.ShapeDtypeStruct((small.shape[0], wide), jnp.float32),
        ],
        in_specs=[vmem] * 2,
        out_specs=[vmem] * 2,
        scratch_shapes=[
            pltpu.SemaphoreType.DMA((4,)),
            pltpu.SemaphoreType.DMA((4,)),
            pltpu.VMEM((groups, small.shape[0], wide), jnp.float32),
            pltpu.VMEM((4, small.shape[0], wide), jnp.float32),
            pltpu.SemaphoreType.DMA((groups + 4,)),
            pltpu.SemaphoreType.DMA((groups + 4,)),
        ],
        compiler_params=pltpu.CompilerParams(collective_id=collective_id, has_side_effects=True),
    )(own, small)


def dot(left, right, over=((1,), (0,))):
    return lax.dot_general(left, right, (over, ((), ())), preferred_element_type=jnp.float32)


def on_device(
    inputs,
    cotangent,
    lengths,
    permutation,
    routes,
    query_weight,
    key_weight,
    value_weight,
    proj_weight,
    first_gain,
    second_gain,
    query_gain,
    key_gain,
    router_weight,
    gate_weight,
    up_weight,
    down_weight,
):
    sequences, deep, model_width = inputs.shape
    groups = lax.axis_size("expert")
    line = groups // 2
    rows = deep * groups
    expert_count = router_weight.shape[1]
    local_experts, _, hidden_width = gate_weight.shape
    group, member = lax.axis_index("expert"), lax.axis_index("tensor")
    y, c = member // 2, member % 2
    first_own = 4 * c + 2 * y
    low = jnp.bfloat16
    score_scale = math.sqrt(HD)

    own_in = lax.dynamic_slice_in_dim(inputs, first_own, 2)
    own_cot = lax.dynamic_slice_in_dim(cotangent, first_own, 2)
    cut = (
        jnp.stack([query_weight, key_weight, value_weight], axis=0)
        .astype(low)
        .reshape(3, -1, line, HD)
        .transpose(2, 1, 0, 3)
        .reshape(line, -1, 3 * HD)
    )
    proj_cut = proj_weight.astype(low).reshape(line, HD, -1)
    named = jnp.sum(
        (routes[:, :, None] == jnp.arange(expert_count, dtype=jnp.int32)).astype(jnp.float32), axis=1
    )
    width = first_gain.shape[0]
    gain_rows = jnp.zeros((16, width), jnp.float32)
    gain_rows = gain_rows.at[0].set(first_gain).at[1].set(second_gain)
    share = query_gain.shape[0]
    gain_rows = gain_rows.at[2, :share].set(query_gain).at[2, share : 2 * share].set(key_gain)
    small = jnp.concatenate([gain_rows, router_weight.T, named.T], axis=0).astype(low)
    all_in, head_weight, head_proj, all_small = gather_with_weights(
        own_in, cut, proj_cut, small, line, 1
    )
    gain_one = all_small[0].astype(jnp.float32)
    gain_two = all_small[1].astype(jnp.float32)
    shares = all_small[2].reshape(groups, width).astype(jnp.float32)
    gain_query = shares[:, :share].reshape(HD)
    gain_key = shares[:, share : 2 * share].reshape(HD)
    router_rows = all_small[16 : 16 + expert_count]
    named_all = all_small[16 + expert_count :]

    normed_one = norm_parts(all_in.reshape(4 * rows, model_width).astype(jnp.float32), gain_one)[0]
    normed_one = normed_one.astype(low)
    projected = dot(normed_one, head_weight)
    queries_raw = projected[:, :HD].reshape(4, rows, HD)
    keys_raw = projected[:, HD : 2 * HD].reshape(4, rows, HD)
    values = projected[:, 2 * HD :].astype(low).reshape(4, rows, HD)
    cos_table, sin_table = rope_tables(rows, HD)
    cos_table, sin_table = cos_table[:, 0], sin_table[:, 0]
    query_normed, query_unit, query_inverse = norm_parts(queries_raw, gain_query)
    key_normed, key_unit, key_inverse = norm_parts(keys_raw, gain_key)
    queries = rotate(query_normed, cos_table, sin_table).astype(low)
    keys_rot = rotate(key_normed, cos_table, sin_table).astype(low)
    my_lengths = lax.dynamic_slice_in_dim(lengths, 4 * c, 4)
    usable = jnp.arange(rows)[None, :] < my_lengths[:, None]
    scores = (
        jnp.einsum("sqd,skd->sqk", queries, keys_rot, preferred_element_type=jnp.float32)
        / score_scale
    )
    scores = jnp.where(usable[:, None, :], scores, NEG_FILL)
    exponent = jnp.exp(scores - jnp.max(scores, axis=-1, keepdims=True))
    softmax_f = exponent / jnp.sum(exponent, axis=-1, keepdims=True)
    probs = softmax_f.astype(low)
    context = jnp.einsum("sqk,skd->sqd", probs, values, preferred_element_type=jnp.float32)
    context = context.astype(low).reshape(4 * rows, HD)
    attn_part = dot(context, head_proj).astype(low).reshape(4, rows, model_width)
    (attn_total,) = reduce_rows((attn_part,), line, False, 2)

    source = own_in.astype(jnp.float32)
    residual = source + attn_total
    normed_two_f, unit_two, inverse_two = norm_parts(residual, gain_two)
    normed_two = normed_two_f.astype(low)
    flat_two = normed_two.reshape(2 * deep, model_width)
    logits = dot(flat_two, router_rows, ((1,), (1,)))
    slot_of_seq = jnp.argmax(
        permutation[None, :] == jnp.arange(sequences, dtype=jnp.int32)[:, None], axis=1
    ).astype(jnp.int32)
    own_slots = lax.dynamic_slice_in_dim(slot_of_seq, first_own, 2)
    own_named = jnp.concatenate(
        [
            lax.dynamic_slice_in_dim(named_all, own_slots[k] * rows + group * deep, deep, axis=1)
            for k in range(2)
        ],
        axis=1,
    ).T.astype(jnp.float32)
    gates = jax.nn.softmax(jnp.where(own_named > 0.5, logits, NEG_FILL), axis=-1)
    lanes = 128
    gate_rows = jnp.pad(gates, ((0, 0), (0, lanes - expert_count))).reshape(2, deep, lanes)
    all_rows, all_grad, all_gates = gather_rows([normed_two, own_cot, gate_rows], line, True, 3)
    tokens = sequences * rows
    all_rows = all_rows.reshape(tokens, model_width)
    all_grad = all_grad.reshape(tokens, model_width)
    all_gates = all_gates.reshape(tokens, lanes)
    gate_matrix = gate_weight.astype(low)
    up_matrix = up_weight.astype(low)
    down_matrix = down_weight.astype(low)
    out_part = 0.0
    rows_part = 0.0
    gate_part = 0.0
    weight_grads = []
    lane_ids = jnp.arange(lanes, dtype=jnp.int32)[None, :]
    for number in range(local_experts):
        here = (lane_ids == group * local_experts + number).astype(jnp.float32)
        gate_column = jnp.sum(all_gates * here, axis=-1, keepdims=True)
        gate_pre = dot(all_rows, gate_matrix[number])
        up_pre = dot(all_rows, up_matrix[number])
        grad_plain = dot(all_grad, down_matrix[number], ((1,), (1,)))
        sigmoid_gate = jax.nn.sigmoid(gate_pre)
        silu_gate = gate_pre * sigmoid_gate
        hidden = silu_gate * up_pre
        gate_part = gate_part + here * jnp.sum(hidden * grad_plain, axis=-1, keepdims=True)
        gated = (gate_column * hidden).astype(low)
        grad_hidden = gate_column * grad_plain
        grad_gate_pre = (
            grad_hidden * up_pre * sigmoid_gate * (1.0 + gate_pre * (1.0 - sigmoid_gate))
        ).astype(low)
        grad_up_pre = (grad_hidden * silu_gate).astype(low)
        out_part = out_part + dot(gated, down_matrix[number])
        rows_part = (
            rows_part
            + dot(grad_gate_pre, gate_matrix[number], ((1,), (1,)))
            + dot(grad_up_pre, up_matrix[number], ((1,), (1,)))
        )
        weight_grads.append(
            (
                dot(all_rows, grad_gate_pre, ((0,), (0,))),
                dot(all_rows, grad_up_pre, ((0,), (0,))),
                dot(gated, all_grad, ((0,), (0,))),
            )
        )
    gate_grad, up_grad, down_grad = (
        jnp.stack([grads[which] for grads in weight_grads]) for which in range(3)
    )
    moe_total, grad_normed_two, gate_total = reduce_rows(
        (
            out_part.astype(low).reshape(sequences, rows, model_width),
            rows_part.astype(low).reshape(sequences, rows, model_width),
            gate_part.reshape(sequences, rows, lanes),
        ),
        line,
        True,
        4,
    )

    own_out = (residual + moe_total).astype(low)
    gate_total = gate_total.reshape(2 * deep, lanes)[:, :expert_count]
    grad_logits = (
        gates * (gate_total - jnp.sum(gates * gate_total, axis=-1, keepdims=True))
    ).astype(low)
    grad_normed_two = grad_normed_two + dot(grad_logits, router_rows).reshape(2, deep, model_width)
    router_part = dot(grad_logits, flat_two, ((0,), (0,)))
    second_part = jnp.sum(grad_normed_two * unit_two, axis=(0, 1))
    grad_state = own_cot.astype(jnp.float32) + norm_back(
        grad_normed_two, gain_two, unit_two, inverse_two
    )
    all_state, output = gather_and_spread(grad_state.astype(low), own_out, line, 5)

    all_state = all_state.reshape(4 * rows, model_width)
    proj_grad = dot(context, all_state, ((0,), (0,))).astype(low)
    grad_context = dot(all_state, head_proj, ((1,), (1,))).astype(low).reshape(4, rows, HD)
    grad_values = jnp.einsum("sqk,sqd->skd", probs, grad_context, preferred_element_type=jnp.float32)
    grad_probs = jnp.einsum("sqd,skd->sqk", grad_context, values, preferred_element_type=jnp.float32)
    grad_scores = (
        softmax_f * (grad_probs - jnp.sum(grad_probs * softmax_f, axis=-1, keepdims=True))
    ).astype(low)
    grad_queries = (
        jnp.einsum("sqk,skd->sqd", grad_scores, keys_rot, preferred_element_type=jnp.float32)
        / score_scale
    )
    grad_keys = (
        jnp.einsum("sqk,sqd->skd", grad_scores, queries, preferred_element_type=jnp.float32)
        / score_scale
    )
    grad_queries = rotate(grad_queries, cos_table, -sin_table)
    grad_keys = rotate(grad_keys, cos_table, -sin_table)
    query_gain_part = jnp.sum(grad_queries * query_unit, axis=(0, 1))
    key_gain_part = jnp.sum(grad_keys * key_unit, axis=(0, 1))
    grad_projected = jnp.concatenate(
        [
            norm_back(grad_queries, gain_query, query_unit, query_inverse).astype(low),
            norm_back(grad_keys, gain_key, key_unit, key_inverse).astype(low),
            grad_values.astype(low),
        ],
        axis=-1,
    ).reshape(4 * rows, 3 * HD)
    head_grad = dot(normed_one, grad_projected, ((0,), (0,))).astype(low)
    one_part = dot(grad_projected, head_weight, ((1,), (1,))).astype(low)
    grad_normed_one, cuts, proj_cuts = reduce_with_weights(
        one_part.reshape(4, rows, model_width), head_grad, proj_grad, line, 6
    )

    _, unit_one, inverse_one = norm_parts(source, gain_one)
    first_part = jnp.sum(grad_normed_one * unit_one, axis=(0, 1))
    own_grad = (grad_state + norm_back(grad_normed_one, gain_one, unit_one, inverse_one)).astype(low)

    def by_share(values):
        return jnp.pad(values.reshape(groups, share), ((0, 0), (0, width - share))).reshape(1, -1)

    small_grads = jnp.concatenate(
        [
            first_part[None],
            second_part[None],
            by_share(query_gain_part),
            by_share(key_gain_part),
            jnp.zeros((4, model_width), jnp.float32),
            router_part,
        ],
        axis=0,
    )
    input_grad, small_total = finish_rows(own_grad, small_grads, line, 7)
    owned = cuts.reshape(line, -1, 3, HD).transpose(2, 1, 0, 3).reshape(3, -1, line * HD)
    owned = owned.astype(jnp.float32)
    return (
        output,
        input_grad,
        owned[0],
        owned[1],
        owned[2],
        proj_cuts.reshape(line * HD, -1).astype(jnp.float32),
        small_total[0],
        small_total[1],
        small_total[2, :share],
        small_total[3, :share],
        small_total[8:].T,
        gate_grad,
        up_grad,
        down_grad,
    )


def on_device_paired(
    inputs,
    cotangent,
    lengths,
    permutation,
    routes,
    query_weight,
    key_weight,
    value_weight,
    proj_weight,
    first_gain,
    second_gain,
    query_gain,
    key_gain,
    router_weight,
    gate_weight,
    up_weight,
    down_weight,
):
    model_width = inputs.shape[2]
    local_heads = query_weight.shape[1] // HD
    expert_count = router_weight.shape[1]
    groups_count = lax.axis_size("expert")
    local_experts = gate_weight.shape[0]
    slot_index = lax.axis_index("expert")
    seq_ids = jnp.arange(permutation.shape[0], dtype=jnp.int32)
    my_sequence = jnp.sum(jnp.where(seq_ids == slot_index, permutation, 0))
    my_length = jnp.sum(jnp.where(seq_ids == my_sequence, lengths, 0))
    slot_of_seq = jnp.sum(
        jnp.where(permutation[None, :] == seq_ids[:, None], seq_ids[None, :], 0), axis=1
    )
    dealt_in, dealt_grad = (
        lax.all_to_all(inputs[permutation], "expert", split_axis=0, concat_axis=1, tiled=True),
        lax.all_to_all(cotangent[permutation], "expert", split_axis=0, concat_axis=1, tiled=True),
    )
    token_rows = dealt_in.shape[1]
    capacity = token_rows * TOPK * 33 // (32 * expert_count)
    block_rows = min(512, token_rows)
    score_scale = math.sqrt(HD)
    gathered = (
        lax.all_gather(query_weight.astype(jnp.bfloat16), "expert", axis=0, tiled=True),
        lax.all_gather(key_weight.astype(jnp.bfloat16), "expert", axis=0, tiled=True),
        lax.all_gather(value_weight.astype(jnp.bfloat16), "expert", axis=0, tiled=True),
        lax.all_gather(proj_weight.astype(jnp.bfloat16), "expert", axis=1, tiled=True),
        lax.all_gather(first_gain.astype(jnp.bfloat16), "expert", axis=0, tiled=True),
        lax.all_gather(second_gain.astype(jnp.bfloat16), "expert", axis=0, tiled=True),
        lax.all_gather(query_gain.astype(jnp.bfloat16), "expert", axis=0, tiled=True),
        lax.all_gather(key_gain.astype(jnp.bfloat16), "expert", axis=0, tiled=True),
        lax.all_gather(router_weight.astype(jnp.bfloat16), "expert", axis=0, tiled=True),
    )
    query_matrix = gathered[0]
    key_matrix = gathered[1]
    value_matrix = gathered[2]
    proj_matrix = gathered[3]
    gain_one = gathered[4].astype(jnp.float32)
    gain_two = gathered[5].astype(jnp.float32)
    gain_query = gathered[6].astype(jnp.float32)
    gain_key = gathered[7].astype(jnp.float32)
    router_matrix = gathered[8]
    gate_matrix = gate_weight.astype(jnp.bfloat16)
    up_matrix = up_weight.astype(jnp.bfloat16)
    down_matrix = down_weight.astype(jnp.bfloat16)
    source = dealt_in.reshape(token_rows, model_width).astype(jnp.float32)
    normed_one_f, unit_one, inverse_one = norm_parts(source, gain_one)
    normed_one = normed_one_f.astype(jnp.bfloat16)
    queries_raw = jnp.dot(normed_one, query_matrix, preferred_element_type=jnp.float32).reshape(
        token_rows, local_heads, HD
    )
    keys_raw = jnp.dot(normed_one, key_matrix, preferred_element_type=jnp.float32).reshape(
        token_rows, local_heads, HD
    )
    values = (
        jnp.dot(normed_one, value_matrix, preferred_element_type=jnp.float32)
        .astype(jnp.bfloat16)
        .reshape(token_rows, local_heads, HD)
    )
    cos_table, sin_table = rope_tables(token_rows, HD)
    query_normed, query_unit, query_inverse = norm_parts(queries_raw, gain_query)
    key_normed, key_unit, key_inverse = norm_parts(keys_raw, gain_key)
    queries = rotate(query_normed, cos_table, sin_table).astype(jnp.bfloat16)
    keys_rot = rotate(key_normed, cos_table, sin_table).astype(jnp.bfloat16)
    usable = jnp.arange(token_rows) < my_length

    def block_scores():
        scores = (
            jnp.einsum("qhd,khd->hqk", queries, keys_rot, preferred_element_type=jnp.float32)
            / score_scale
        )
        return (queries, jnp.where(usable[None, None, :], scores, NEG_FILL))

    query_block, scores = block_scores()
    maximum = jnp.max(scores, axis=-1, keepdims=True)
    exponent = jnp.exp(scores - maximum)
    row_total = jnp.sum(exponent, axis=-1, keepdims=True)
    softmax_rows = (exponent / row_total).astype(jnp.bfloat16)
    context_blocks = jnp.einsum(
        "hqk,khd->qhd", softmax_rows, values, preferred_element_type=jnp.float32
    ).astype(jnp.bfloat16)
    lse_blocks = [maximum + jnp.log(row_total)]
    context = context_blocks.reshape(token_rows, local_heads * HD)
    attn_part = jnp.dot(context, proj_matrix, preferred_element_type=jnp.float32)
    attn_total = lax.psum(attn_part, "tensor")
    residual = source + attn_total
    normed_two_f, unit_two, inverse_two = norm_parts(residual, gain_two)
    normed_two = normed_two_f.astype(jnp.bfloat16)
    logits = jnp.dot(normed_two, router_matrix, preferred_element_type=jnp.float32)
    choose = (
        routes[:, :, None] == jnp.arange(expert_count, dtype=jnp.int32)[None, None, :]
    ).astype(jnp.float32)
    chosen = jnp.sum(choose * logits[:, None, :], axis=-1)
    gate_probs = jax.nn.softmax(chosen, axis=-1)
    flat_routes = routes.reshape(-1)
    route_hits = (
        flat_routes[:, None] == jnp.arange(expert_count, dtype=jnp.int32)[None, :]
    ).astype(jnp.int32)
    rank_ids = jnp.sum(jnp.cumsum(route_hits, axis=0) * route_hits, axis=1) - 1
    slot_ids = flat_routes * capacity + rank_ids
    pair_tokens = jnp.arange(flat_routes.shape[0], dtype=jnp.int32) // TOPK
    send_rows = (
        jnp.zeros((expert_count * capacity, model_width), jnp.bfloat16)
        .at[slot_ids]
        .set(normed_two[pair_tokens])
    )
    send_rows = send_rows.reshape(groups_count, local_experts, capacity, model_width)
    received = lax.all_to_all(send_rows, "expert", split_axis=0, concat_axis=0, tiled=True)
    gate_pre = jnp.einsum(
        "secd,edf->secf", received, gate_matrix, preferred_element_type=jnp.float32
    )
    up_pre = jnp.einsum("secd,edf->secf", received, up_matrix, preferred_element_type=jnp.float32)
    hidden = (jax.nn.silu(gate_pre) * up_pre).astype(jnp.bfloat16)
    result = jnp.einsum(
        "secf,efd->secd", hidden, down_matrix, preferred_element_type=jnp.float32
    ).astype(jnp.bfloat16)
    returned = lax.all_to_all(result, "expert", split_axis=0, concat_axis=0, tiled=True)
    picked = returned.reshape(expert_count * capacity, model_width)[slot_ids].reshape(
        token_rows, TOPK, model_width
    )
    combined = jnp.sum(gate_probs[:, :, None] * picked.astype(jnp.float32), axis=1)
    moe_total = lax.psum(combined.astype(jnp.bfloat16), "tensor").astype(jnp.float32)
    output = (residual + moe_total).astype(jnp.bfloat16)
    grad_out = dealt_grad.reshape(token_rows, model_width).astype(jnp.float32)
    gate_grad_part = jnp.sum(grad_out[:, None, :] * picked.astype(jnp.float32), axis=-1)
    routed_grad = (
        (gate_probs[:, :, None] * grad_out[:, None, :])
        .astype(jnp.bfloat16)
        .reshape(token_rows * TOPK, model_width)
    )
    grad_send = (
        jnp.zeros((expert_count * capacity, model_width), jnp.bfloat16)
        .at[slot_ids]
        .set(routed_grad)
    )
    grad_send = grad_send.reshape(groups_count, local_experts, capacity, model_width)
    grad_rows, rows_in = (
        lax.all_to_all(grad_send, "expert", split_axis=0, concat_axis=0, tiled=True),
        lax.all_to_all(send_rows, "expert", split_axis=0, concat_axis=0, tiled=True),
    )
    gate_pre = jnp.einsum(
        "secd,edf->secf", rows_in, gate_matrix, preferred_element_type=jnp.float32
    )
    up_pre = jnp.einsum("secd,edf->secf", rows_in, up_matrix, preferred_element_type=jnp.float32)
    grad_hidden = jnp.einsum(
        "secd,efd->secf", grad_rows, down_matrix, preferred_element_type=jnp.float32
    )
    sigmoid_gate = jax.nn.sigmoid(gate_pre)
    silu_gate = gate_pre * sigmoid_gate
    grad_gate_pre = (
        grad_hidden * up_pre * sigmoid_gate * (1.0 + gate_pre * (1.0 - sigmoid_gate))
    ).astype(jnp.bfloat16)
    grad_up_pre = (grad_hidden * silu_gate).astype(jnp.bfloat16)
    hidden = (silu_gate * up_pre).astype(jnp.bfloat16)
    rows_grad = (
        jnp.einsum("secf,edf->secd", grad_gate_pre, gate_matrix, preferred_element_type=jnp.float32)
        + jnp.einsum("secf,edf->secd", grad_up_pre, up_matrix, preferred_element_type=jnp.float32)
    ).astype(jnp.bfloat16)
    down_grad = jnp.einsum("secf,secd->efd", hidden, grad_rows, preferred_element_type=jnp.float32)
    gate_grad = jnp.einsum(
        "secd,secf->edf", rows_in, grad_gate_pre, preferred_element_type=jnp.float32
    )
    up_grad = jnp.einsum("secd,secf->edf", rows_in, grad_up_pre, preferred_element_type=jnp.float32)
    returned_grad = lax.all_to_all(rows_grad, "expert", split_axis=0, concat_axis=0, tiled=True)
    returned_pairs = returned_grad.reshape(expert_count * capacity, model_width)[slot_ids].reshape(
        token_rows, TOPK, model_width
    )
    normed_two_part = jnp.sum(returned_pairs.astype(jnp.float32), axis=1)
    grad_normed_two, gate_grad_total = lax.psum((normed_two_part, gate_grad_part), "tensor")
    grad_chosen = gate_probs * (
        gate_grad_total - jnp.sum(gate_probs * gate_grad_total, axis=-1, keepdims=True)
    )
    grad_logits = jnp.sum(choose * grad_chosen[:, :, None], axis=1).astype(jnp.bfloat16)
    grad_normed_two = grad_normed_two + jnp.dot(
        grad_logits, router_matrix.T, preferred_element_type=jnp.float32
    )
    router_grad = jnp.dot(normed_two.T, grad_logits, preferred_element_type=jnp.float32)
    second_gain_grad = jnp.sum(grad_normed_two * unit_two, axis=0)
    grad_state = grad_out + norm_back(grad_normed_two, gain_two, unit_two, inverse_two)
    grad_context_in = grad_state.astype(jnp.bfloat16)
    proj_grad = jnp.dot(context.T, grad_context_in, preferred_element_type=jnp.float32)
    grad_context = (
        jnp.dot(grad_context_in, proj_matrix.T, preferred_element_type=jnp.float32)
        .astype(jnp.bfloat16)
        .reshape(token_rows, local_heads, HD)
    )
    grad_values = jnp.zeros((token_rows, local_heads, HD), jnp.float32)
    grad_keys_rot = jnp.zeros((token_rows, local_heads, HD), jnp.float32)
    grad_query_blocks = []
    for number, start_row in enumerate(range(0, token_rows, block_rows)):
        query_block, scores = block_scores()
        softmax_f = jnp.exp(scores - lse_blocks[number])
        grad_values = jnp.einsum(
            "hqk,qhd->khd",
            softmax_f.astype(jnp.bfloat16),
            grad_context,
            preferred_element_type=jnp.float32,
        )
        grad_probs = jnp.einsum(
            "qhd,khd->hqk", grad_context, values, preferred_element_type=jnp.float32
        )
        grad_scores = (
            softmax_f * (grad_probs - jnp.sum(grad_probs * softmax_f, axis=-1, keepdims=True))
        ).astype(jnp.bfloat16)
        grad_query_blocks.append(
            jnp.einsum("hqk,khd->qhd", grad_scores, keys_rot, preferred_element_type=jnp.float32)
            / score_scale
        )
        grad_keys_rot = (
            jnp.einsum("hqk,qhd->khd", grad_scores, query_block, preferred_element_type=jnp.float32)
            / score_scale
        )
    grad_queries_n = rotate(grad_query_blocks[0], cos_table, -sin_table)
    grad_keys_n = rotate(grad_keys_rot, cos_table, -sin_table)
    query_gain_part = jnp.sum(grad_queries_n * query_unit, axis=(0, 1))
    key_gain_part = jnp.sum(grad_keys_n * key_unit, axis=(0, 1))
    grad_queries_raw = (
        norm_back(grad_queries_n, gain_query, query_unit, query_inverse)
        .astype(jnp.bfloat16)
        .reshape(token_rows, local_heads * HD)
    )
    grad_keys_raw = (
        norm_back(grad_keys_n, gain_key, key_unit, key_inverse)
        .astype(jnp.bfloat16)
        .reshape(token_rows, local_heads * HD)
    )
    grad_values_low = grad_values.astype(jnp.bfloat16).reshape(token_rows, local_heads * HD)
    query_grad = jnp.dot(normed_one.T, grad_queries_raw, preferred_element_type=jnp.float32)
    key_grad = jnp.dot(normed_one.T, grad_keys_raw, preferred_element_type=jnp.float32)
    value_grad = jnp.dot(normed_one.T, grad_values_low, preferred_element_type=jnp.float32)
    normed_one_part = jnp.dot(grad_queries_raw, query_matrix.T, preferred_element_type=jnp.float32)
    normed_one_part = normed_one_part + jnp.dot(
        grad_keys_raw, key_matrix.T, preferred_element_type=jnp.float32
    )
    normed_one_part = normed_one_part + jnp.dot(
        grad_values_low, value_matrix.T, preferred_element_type=jnp.float32
    )
    grad_normed_one, query_gain_total, key_gain_total = (
        lax.psum(normed_one_part.astype(jnp.bfloat16), "tensor").astype(jnp.float32),
        lax.psum(query_gain_part.astype(jnp.bfloat16), "tensor").astype(jnp.float32),
        lax.psum(key_gain_part.astype(jnp.bfloat16), "tensor").astype(jnp.float32),
    )
    first_gain_grad = jnp.sum(grad_normed_one * unit_one, axis=0)
    input_grad = (grad_state + norm_back(grad_normed_one, gain_one, unit_one, inverse_one)).astype(
        jnp.bfloat16
    )
    shards = (
        lax.psum_scatter(
            query_grad.astype(jnp.bfloat16), "expert", scatter_dimension=0, tiled=True
        ).astype(jnp.float32),
        lax.psum_scatter(
            key_grad.astype(jnp.bfloat16), "expert", scatter_dimension=0, tiled=True
        ).astype(jnp.float32),
        lax.psum_scatter(
            value_grad.astype(jnp.bfloat16), "expert", scatter_dimension=0, tiled=True
        ).astype(jnp.float32),
        lax.psum_scatter(
            proj_grad.astype(jnp.bfloat16), "expert", scatter_dimension=1, tiled=True
        ).astype(jnp.float32),
        lax.psum_scatter(
            first_gain_grad.astype(jnp.bfloat16), "expert", scatter_dimension=0, tiled=True
        ).astype(jnp.float32),
        lax.psum_scatter(
            second_gain_grad.astype(jnp.bfloat16), "expert", scatter_dimension=0, tiled=True
        ).astype(jnp.float32),
        lax.psum_scatter(
            query_gain_total.astype(jnp.bfloat16), "expert", scatter_dimension=0, tiled=True
        ).astype(jnp.float32),
        lax.psum_scatter(
            key_gain_total.astype(jnp.bfloat16), "expert", scatter_dimension=0, tiled=True
        ).astype(jnp.float32),
        lax.psum_scatter(
            router_grad.astype(jnp.bfloat16), "expert", scatter_dimension=0, tiled=True
        ).astype(jnp.float32),
    )
    back_out, back_grad = (
        lax.all_to_all(
            output.reshape(1, token_rows, model_width),
            "expert",
            split_axis=1,
            concat_axis=0,
            tiled=True,
        ),
        lax.all_to_all(
            input_grad.reshape(1, token_rows, model_width),
            "expert",
            split_axis=1,
            concat_axis=0,
            tiled=True,
        ),
    )
    ordered_out = back_out[slot_of_seq]
    ordered_grad = back_grad[slot_of_seq]
    return (
        ordered_out,
        ordered_grad,
        shards[0],
        shards[1],
        shards[2],
        shards[3],
        shards[4],
        shards[5],
        shards[6],
        shards[7],
        shards[8],
        gate_grad,
        up_grad,
        down_grad,
    )


def solution(mesh):
    in_specs = (
        P(None, "expert", None),
        P(None, "expert", None),
        P(),
        P(),
        P("expert", None),
        P("expert", "tensor"),
        P("expert", "tensor"),
        P("expert", "tensor"),
        P("tensor", "expert"),
        P("expert"),
        P("expert"),
        P("expert"),
        P("expert"),
        P("expert", None),
        P("expert", None, "tensor"),
        P("expert", None, "tensor"),
        P("expert", "tensor", None),
    )
    out_specs = (
        P(None, "expert", None),
        P(None, "expert", None),
        P("expert", "tensor"),
        P("expert", "tensor"),
        P("expert", "tensor"),
        P("tensor", "expert"),
        P("expert"),
        P("expert"),
        P("expert"),
        P("expert"),
        P("expert", None),
        P("expert", None, "tensor"),
        P("expert", None, "tensor"),
        P("expert", "tensor", None),
    )
    chips = mesh.shape["expert"] * mesh.shape["tensor"] // 2

    def whole(*arrays):
        heads, sequences = arrays[5].shape[1] // HD, arrays[0].shape[0]
        fits = heads == chips and sequences == 8 and mesh.shape["tensor"] == 4
        return jax.shard_map(
            on_device if fits else on_device_paired,
            mesh=mesh,
            in_specs=in_specs,
            out_specs=out_specs,
            check_vma=False,
        )(*arrays)

    return whole
```

```python
import functools
import math

import jax
import jax.numpy as jnp
from jax import lax
from jax.experimental import pallas as pl
from jax.experimental.pallas import tpu as pltpu
from jax.sharding import PartitionSpec as P

HD = 128
TOPK = 8


EPS = 1e-06
ROPE_BASE = 50000.0
NEG_FILL = -1e30


def norm_parts(values, gain):
    inverse = lax.rsqrt(jnp.mean(values * values, axis=-1, keepdims=True) + EPS)
    unit_rows = values * inverse
    return (unit_rows * gain, unit_rows, inverse)


def norm_back(grad_normed, gain, unit_rows, inverse):
    grad_unit = grad_normed * gain
    inner_mean = jnp.mean(grad_unit * unit_rows, axis=-1, keepdims=True)
    return inverse * (grad_unit - unit_rows * inner_mean)


def rope_tables(seq_count, width):
    halfway = width // 2
    frequency = jnp.power(ROPE_BASE, -jnp.arange(halfway, dtype=jnp.float32) * (2.0 / width))
    angles = jnp.arange(seq_count, dtype=jnp.float32)[:, None] * frequency[None, :]
    return (jnp.cos(angles)[:, None, :], jnp.sin(angles)[:, None, :])


def rotate(values, cos_table, sin_table):
    halfway = values.shape[-1] // 2
    former = values[..., :halfway]
    latter = values[..., halfway:]
    return jnp.concatenate(
        [former * cos_table - latter * sin_table, latter * cos_table + former * sin_table], axis=-1
    )


MESH = pl.DeviceIdType.MESH
UP, DOWN, ACROSS_X, ACROSS_Y, DIAG_X, DIAG_Y, PAIR = range(7)


def position():
    group, member = lax.axis_index("expert"), lax.axis_index("tensor")
    return lax.rem(group, 2), lax.div(member, 2), lax.div(group, 2), lax.rem(member, 2)


def device(x, y, z, c):
    return (z * 2 + x, y * 2 + c)


def greet(line, extra=0):
    x, y, z, c = position()
    barrier = pltpu.get_barrier_semaphore()

    def signal(to):
        pl.semaphore_signal(barrier, inc=1, device_id=to, device_id_type=MESH)

    signal(device(1 - x, y, z, c))
    signal(device(x, 1 - y, z, c))
    signal(device(x, y, z, 1 - c))
    pl.when(z > 0)(lambda: signal(device(x, y, z - 1, c)))
    pl.when(z < line - 1)(lambda: signal(device(x, y, z + 1, c)))
    near = 3 + (z > 0).astype(jnp.int32) + (z < line - 1).astype(jnp.int32)
    pl.semaphore_wait(barrier, near + extra)


def gather_steps(line, pair, ins, outs, send, recv, local, between=None):
    x, y, z, c = position()
    count = len(ins)
    deep = ins[0].shape[1]

    def place(i, xx, yy, zz, cc):
        if pair:
            return outs[i].at[(zz * 2 + xx) * 4 + yy * 2 + cc]
        return outs[i].at[pl.ds(2 * yy, 2), pl.ds((zz * 2 + xx) * deep, deep)]

    def copy(i, kind, block, to, own):
        slot = kind * line + block[2]
        return pltpu.make_async_remote_copy(
            src_ref=ins[i] if own else place(i, *block),
            dst_ref=place(i, *block),
            send_sem=send.at[i, slot],
            recv_sem=recv.at[i, slot],
            device_id=to,
            device_id_type=MESH,
        )

    x_side, y_side = device(1 - x, y, z, c), device(x, 1 - y, z, c)
    sibling = device(x, y, z, 1 - c)
    sends = []

    def push(kind, block, to, own=False, when=None):
        def start():
            for i in range(count):
                copy(i, kind, block, to, own).start()

        def finish():
            for i in range(count):
                copy(i, kind, block, to, own).wait_send()

        if when is None:
            start()
        else:
            pl.when(when)(start)
        sends.append((finish, when))

    def both(one, two):
        return two if one is None else one & two

    def arrive(kind, block, frm):
        for i in range(count):
            copy(i, kind, block, frm, False).wait_recv()

    mine = (x, y, z, c)
    below, above = device(x, y, z - 1, c), device(x, y, z + 1, c)
    push(UP, mine, above, True, z < line - 1)
    push(DOWN, mine, below, True, z > 0)
    push(ACROSS_X, mine, x_side, True)
    push(ACROSS_Y, mine, y_side, True)
    if pair:
        push(PAIR, mine, sibling, True)
    homes = [pltpu.make_async_copy(ins[i], place(i, *mine), local.at[i]) for i in range(count)]
    for home in homes:
        home.start()
    if between is not None:
        between()

    for step in range(line):
        signs = (0,) if step == 0 else (-1, 1)
        for sign in signs:
            zz = z + sign * step
            valid = None if step == 0 else (zz >= 0) & (zz < line)
            block = (x, y, zz, c)
            if step > 0:
                kind, frm = (UP, below) if sign < 0 else (DOWN, above)
                pl.when(valid)(functools.partial(arrive, kind, block, frm))
                if sign < 0:
                    push(UP, block, above, False, valid & (z < line - 1))
                else:
                    push(DOWN, block, below, False, valid & (z > 0))
                push(ACROSS_X, block, x_side, False, valid)
                push(ACROSS_Y, block, y_side, False, valid)
                if pair:
                    push(PAIR, block, sibling, False, valid)
        for sign in signs:
            zz = z + sign * step
            valid = None if step == 0 else (zz >= 0) & (zz < line)
            even = lax.rem(zz + line, 2) == 0
            if line % 2:
                even = ~even

            def take(kind, block, frm, valid=valid):
                go = functools.partial(arrive, kind, block, frm)
                if valid is None:
                    go()
                else:
                    pl.when(valid)(go)

            block = (1 - x, y, zz, c)
            take(ACROSS_X, block, x_side)
            push(DIAG_Y, block, y_side, False, both(valid, ~even))
            if pair:
                push(PAIR + 1, block, sibling, False, valid)
            block = (x, 1 - y, zz, c)
            take(ACROSS_Y, block, y_side)
            push(DIAG_X, block, x_side, False, both(valid, even))
            if pair:
                push(PAIR + 2, block, sibling, False, valid)
    for zz in range(line):
        block = (1 - x, 1 - y, zz, c)
        if zz % 2 == 0:
            arrive(DIAG_X, block, x_side)
        else:
            arrive(DIAG_Y, block, y_side)
        if pair:
            push(PAIR + 3, block, sibling)
    if pair:
        for zz in range(line):
            for way, (xx, yy) in enumerate(((x, y), (1 - x, y), (x, 1 - y), (1 - x, 1 - y))):
                arrive(PAIR + way, (xx, yy, zz, 1 - c), sibling)
    for home in homes:
        home.wait()
    for finish, when in sends:
        if when is None:
            finish()
        else:
            pl.when(when)(finish)


def gather_kernel(line, pair, count, *refs):
    ins, outs = refs[:count], refs[count : 2 * count]
    send, recv, local = refs[2 * count :]
    greet(line)
    gather_steps(line, pair, ins, outs, send, recv, local)


def gather_rows(arrays, line, pair, collective_id):
    count = len(arrays)
    kinds = PAIR + (4 if pair else 0)
    return pl.pallas_call(
        functools.partial(gather_kernel, line, pair, count),
        out_shape=[
            jax.ShapeDtypeStruct(
                (line * 8,) + a.shape if pair else (4, a.shape[1] * line * 2, a.shape[2]), a.dtype
            )
            for a in arrays
        ],
        in_specs=[pl.BlockSpec(memory_space=pltpu.VMEM)] * count,
        out_specs=[pl.BlockSpec(memory_space=pl.ANY)] * count,
        scratch_shapes=[
            pltpu.SemaphoreType.DMA((count, kinds * line)),
            pltpu.SemaphoreType.DMA((count, kinds * line)),
            pltpu.SemaphoreType.DMA((count,)),
        ],
        compiler_params=pltpu.CompilerParams(collective_id=collective_id, has_side_effects=True),
    )(*arrays)


def column(way):
    x, y, _, _ = position()
    over_x, over_y = way % 2, way // 2
    return x + over_x * (1 - 2 * x), y + over_y * (1 - 2 * y)


def reduce_steps(line, pair, parts, outs, scratches, between=None):
    work = [
        reduce_phases(line, pair, sequence_slab(part, pair, out.shape[1]), out, *scratch)
        for part, out, scratch in zip(parts, outs, scratches)
    ]
    for phase in ("halves", "corner", "across", "along", "drain"):
        for phases in work:
            phases[phase]()
        if phase == "corner" and between is not None:
            between()


def sequence_slab(part, pair, deep):
    def slab(xx, yy, zz, cc):
        first = 2 * yy + (4 * cc if pair else 0)
        return part.at[pl.ds(first, 2), pl.ds((zz * 2 + xx) * deep, deep)]

    return slab


def reduce_phases(line, pair, spot_of, out, diag, side_x, side_y, rise, fall, twin, send, recv):
    x, y, z, c = position()
    deep = out.shape[1]
    x_side, y_side = device(1 - x, y, z, c), device(x, 1 - y, z, c)
    sibling = device(x, y, z, 1 - c)
    below, above = device(x, y, z - 1, c), device(x, y, z + 1, c)

    def slab(way, zz, cc):
        return spot_of(*column(way), zz, cc)

    def copy(kind, zz, src, dst, to):
        return pltpu.make_async_remote_copy(
            src_ref=src,
            dst_ref=dst.at[zz],
            send_sem=send.at[kind * line + zz],
            recv_sem=recv.at[kind * line + zz],
            device_id=to,
            device_id_type=MESH,
        )

    def push(kind, zz, src, dst, to):
        copy(kind, zz, src, dst, to).start()

    def landed(kind, zz, dst, frm):
        copy(kind, zz, dst.at[zz], dst, frm).wait_recv()

    def total(target, *terms):
        def some(n, carry):
            k, r = lax.div(n, deep // 16), pl.multiple_of(lax.rem(n, deep // 16) * 16, 16)
            value = terms[0][k, pl.ds(r, 16)].astype(jnp.float32)
            for term in terms[1:]:
                value = value + term[k, pl.ds(r, 16)].astype(jnp.float32)
            target[k, pl.ds(r, 16)] = value.astype(target.dtype)
            return carry

        lax.fori_loop(0, 2 * (deep // 16), some, 0)

    def base(way, zz):
        return twin.at[way, zz] if pair else slab(way, zz, c)

    def paired(way, zz):
        if pair:
            spot = twin.at[way]
            landed(PAIR + way, zz, spot, sibling)
            total(spot.at[zz], slab(way, zz, c), spot.at[zz])

    def half(way, zz):
        push(PAIR + way, zz, slab(way, zz, 1 - c), twin.at[way], sibling)

    def halves():
        if pair:
            for way in (3, 1, 2, 0):
                for zz in range(line):
                    half(way, zz)

    def corner_of(zz):
        paired(3, zz)
        pl.when(lax.rem(zz, 2) == 0)(lambda: push(DIAG_X, zz, base(3, zz), diag, x_side))
        pl.when(lax.rem(zz, 2) == 1)(lambda: push(DIAG_Y, zz, base(3, zz), diag, y_side))

    def corner():
        for zz in range(line):
            corner_of(jnp.int32(zz))

    def direct(way, zz):
        paired(way, zz)
        if way == 1:
            pl.when(lax.rem(zz, 2) == 0)(lambda: push(ACROSS_X, zz, base(1, zz), side_x, x_side))
        else:
            pl.when(lax.rem(zz, 2) == 1)(lambda: push(ACROSS_Y, zz, base(2, zz), side_y, y_side))

    def dependent(zz):
        @pl.when(lax.rem(zz, 2) == 0)
        def _():
            landed(DIAG_X, zz, diag, x_side)
            total(diag.at[zz], base(2, zz), diag.at[zz])
            push(ACROSS_Y, zz, diag.at[zz], side_y, y_side)

        @pl.when(lax.rem(zz, 2) == 1)
        def _():
            landed(DIAG_Y, zz, diag, y_side)
            total(diag.at[zz], base(1, zz), diag.at[zz])
            push(ACROSS_X, zz, diag.at[zz], side_x, x_side)

    def order(body):
        for step in range(line - 1, -1, -1):
            for sign in (0,) if step == 0 else (-1, 1):
                zz = z + sign * step
                go = functools.partial(body, zz, sign)
                if step == 0:
                    go()
                else:
                    pl.when((zz >= 0) & (zz < line))(go)

    def across(zz, sign):
        direct(1, zz)
        direct(2, zz)
        dependent(zz)

    def along(zz, sign):
        paired(0, zz)
        landed(ACROSS_X, zz, side_x, x_side)
        landed(ACROSS_Y, zz, side_y, y_side)
        spot = out if sign == 0 else side_x.at[zz]
        near = (base(0, zz), side_x.at[zz], side_y.at[zz])
        if sign > 0:
            @pl.when(z > 0)
            def _():
                landed(UP, zz, rise, below)
                total(spot, *near, rise.at[zz])

            @pl.when(z == 0)
            def _():
                total(spot, *near)

            push(UP, zz, spot, rise, above)
        elif sign < 0:
            @pl.when(z < line - 1)
            def _():
                landed(DOWN, zz, fall, above)
                total(spot, *near, fall.at[zz])

            @pl.when(z == line - 1)
            def _():
                total(spot, *near)

            push(DOWN, zz, spot, fall, below)
        else:
            @pl.when((z > 0) & (z < line - 1))
            def _():
                landed(UP, zz, rise, below)
                landed(DOWN, zz, fall, above)
                total(spot, *near, rise.at[zz], fall.at[zz])

            @pl.when(z == 0)
            def _():
                landed(DOWN, zz, fall, above)
                total(spot, *near, fall.at[zz])

            @pl.when(z == line - 1)
            def _():
                landed(UP, zz, rise, below)
                total(spot, *near, rise.at[zz])

    def sent(kind, zz, dst, to):
        copy(kind, zz, dst.at[zz], dst, to).wait_send()

    def drain():
        for zz in range(line):
            leave(zz)

    def leave(zz):
        if pair:
            for way in range(4):
                sent(PAIR + way, zz, twin.at[way], sibling)
        sent(DIAG_X if zz % 2 == 0 else DIAG_Y, zz, diag, x_side if zz % 2 == 0 else y_side)
        sent(ACROSS_X, zz, side_x, x_side)
        sent(ACROSS_Y, zz, side_y, y_side)
        pl.when(zz > z)(functools.partial(sent, UP, zz, rise, above))
        pl.when(zz < z)(functools.partial(sent, DOWN, zz, fall, below))

    return dict(
        half=half,
        halves=halves,
        corner_of=corner_of,
        corner=corner,
        direct=direct,
        dependent=dependent,
        across=functools.partial(order, across),
        along=functools.partial(order, along),
        along_of=along,
        drain=drain,
    )


def reduce_kernel(line, pair, count, *refs):
    parts, outs, rest = refs[:count], refs[count : 2 * count], refs[2 * count :]
    greet(line)
    reduce_steps(line, pair, parts, outs, [rest[8 * i : 8 * i + 8] for i in range(count)])


def reduce_scratch(line, pair, deep, width, dtype):
    kinds = PAIR + (4 if pair else 0)
    block = (line, 2, deep, width)
    return [pltpu.VMEM(block, dtype)] * 5 + [
        pltpu.VMEM((4,) + block if pair else (8, 128), dtype),
        pltpu.SemaphoreType.DMA((kinds * line,)),
        pltpu.SemaphoreType.DMA((kinds * line,)),
    ]


def reduce_rows(parts, line, pair, collective_id):
    count, deep = len(parts), parts[0].shape[1] // (2 * line)
    scratch = []
    for part in parts:
        scratch += reduce_scratch(line, pair, deep, part.shape[2], part.dtype)
    return pl.pallas_call(
        functools.partial(reduce_kernel, line, pair, count),
        out_shape=[jax.ShapeDtypeStruct((2, deep, part.shape[2]), jnp.float32) for part in parts],
        in_specs=[pl.BlockSpec(memory_space=pltpu.VMEM)] * count,
        out_specs=[pl.BlockSpec(memory_space=pltpu.VMEM)] * count,
        scratch_shapes=scratch,
        compiler_params=pltpu.CompilerParams(
            collective_id=collective_id, has_side_effects=True, vmem_limit_bytes=60 << 20
        ),
    )(*parts)


def gathered_with_weights(line, rows, cut, proj_cut, small, *rest):
    all_rows, head_weight, head_proj, all_small, send, recv, local, wsend, wrecv, wlocal = rest
    x, y, z, c = position()
    group, groups = lax.axis_index("expert"), 2 * line
    member = lax.axis_index("tensor")
    deep, wide = cut.shape[1], proj_cut.shape[2]
    parts = cut.shape[0]
    sibling = device(x, y, z, 1 - c)
    barrier = pltpu.get_barrier_semaphore()
    for hop in range(1, groups):
        pl.semaphore_signal(
            barrier, inc=1, device_id=(lax.rem(group + hop, groups), member), device_id_type=MESH
        )
    pl.semaphore_signal(barrier, inc=1, device_id=sibling, device_id_type=MESH)
    pl.semaphore_signal(barrier, inc=1, device_id=device(x, 1 - y, z, c), device_id_type=MESH)
    pl.semaphore_wait(barrier, groups + 1)
    serves = lax.div(group, parts) == c

    def spots(origin):
        return (
            head_weight.at[pl.ds(origin * deep, deep)],
            head_proj.at[:, pl.ds(origin * wide, wide)],
        )

    def weight_copies(origin, sources, to, slot):
        return [
            pltpu.make_async_remote_copy(
                src_ref=source,
                dst_ref=spot,
                send_sem=wsend.at[which, slot],
                recv_sem=wrecv.at[which, origin],
                device_id=to,
                device_id_type=MESH,
            )
            for which, (source, spot) in enumerate(zip(sources, spots(origin)))
        ]

    def small_copy(origin, to, slot):
        return pltpu.make_async_remote_copy(
            src_ref=small,
            dst_ref=all_small.at[:, pl.ds(origin * small.shape[1], small.shape[1])],
            send_sem=wsend.at[2, slot],
            recv_sem=wrecv.at[2, origin],
            device_id=to,
            device_id_type=MESH,
        )

    def outgoing(n):
        return weight_copies(group, (cut.at[n], proj_cut.at[n]), (c * parts + n, member), n)

    own = lax.rem(group, parts)
    home = [
        pltpu.make_async_copy(source, spot, wlocal.at[which])
        for which, (source, spot) in enumerate(zip((cut.at[own], proj_cut.at[own]), spots(group)))
    ]
    small_home = pltpu.make_async_copy(
        small, all_small.at[:, pl.ds(group * small.shape[1], small.shape[1])], wlocal.at[2]
    )
    own_to_sibling = weight_copies(group, (cut.at[own], proj_cut.at[own]), sibling, parts)

    def everything(copies, act):
        for one in copies:
            getattr(one, act)()

    def begin():
        small_home.start()
        for hop in range(1, groups):
            small_copy(group, (lax.rem(group + hop, groups), member), hop).start()
        for n in range(parts):
            pl.when(c * parts + n != group)(functools.partial(everything, outgoing(n), "start"))

        @pl.when(serves)
        def _():
            everything(home, "start")
            everything(own_to_sibling, "start")

    gather_steps(line, False, (rows,), (all_rows,), send, recv, local, begin)
    for hop in range(1, groups):
        origin = lax.rem(group + hop, groups)
        copies = weight_copies(origin, spots(origin), sibling, parts + hop)
        everything(copies, "wait_recv")
        pl.when(serves)(functools.partial(everything, copies, "start"))
    pl.when(~serves)(functools.partial(everything, own_to_sibling, "wait_recv"))
    for hop in range(1, groups):
        small_copy(lax.rem(group + hop, groups), sibling, hop).wait_recv()
    small_home.wait()
    for n in range(parts):
        pl.when(c * parts + n != group)(functools.partial(everything, outgoing(n), "wait_send"))
    for hop in range(1, groups):
        small_copy(group, (lax.rem(group + hop, groups), member), hop).wait_send()

    @pl.when(serves)
    def _():
        everything(home, "wait")
        everything(own_to_sibling, "wait_send")
        for hop in range(1, groups):
            origin = lax.rem(group + hop, groups)
            everything(weight_copies(origin, spots(origin), sibling, parts + hop), "wait_send")


def gather_with_weights(rows, cut, proj_cut, small, line, collective_id):
    groups = 2 * line
    vmem = pl.BlockSpec(memory_space=pltpu.VMEM)
    anywhere = pl.BlockSpec(memory_space=pl.ANY)
    slots = cut.shape[0] + groups
    return pl.pallas_call(
        functools.partial(gathered_with_weights, line),
        out_shape=[
            jax.ShapeDtypeStruct((4, rows.shape[1] * groups, rows.shape[2]), rows.dtype),
            jax.ShapeDtypeStruct((groups * cut.shape[1], cut.shape[2]), cut.dtype),
            jax.ShapeDtypeStruct((proj_cut.shape[1], groups * proj_cut.shape[2]), cut.dtype),
            jax.ShapeDtypeStruct((small.shape[0], groups * small.shape[1]), small.dtype),
        ],
        in_specs=[vmem] * 4,
        out_specs=[anywhere] * 4,
        scratch_shapes=[
            pltpu.SemaphoreType.DMA((1, PAIR * line)),
            pltpu.SemaphoreType.DMA((1, PAIR * line)),
            pltpu.SemaphoreType.DMA((1,)),
            pltpu.SemaphoreType.DMA((3, slots)),
            pltpu.SemaphoreType.DMA((3, groups)),
            pltpu.SemaphoreType.DMA((3,)),
        ],
        compiler_params=pltpu.CompilerParams(collective_id=collective_id, has_side_effects=True),
    )(rows, cut, proj_cut, small)


def spread_copies(own, full, send, recv):
    x, y, z, c = position()
    y_side, sibling = device(x, 1 - y, z, c), device(x, y, z, 1 - c)

    def spot(yy, cc):
        return full.at[pl.ds(4 * cc + 2 * yy, 2)]

    def copy(slot, source, yy, to):
        return pltpu.make_async_remote_copy(
            src_ref=source,
            dst_ref=spot(yy, c),
            send_sem=send.at[slot],
            recv_sem=recv.at[slot],
            device_id=to,
            device_id_type=MESH,
        )

    def incoming(slot, yy, cc, frm):
        return pltpu.make_async_remote_copy(
            src_ref=spot(yy, cc),
            dst_ref=spot(yy, cc),
            send_sem=send.at[slot],
            recv_sem=recv.at[slot],
            device_id=frm,
            device_id_type=MESH,
        )

    first = [copy(0, own, y, y_side), copy(1, own, y, sibling)]
    onward = copy(2, spot(1 - y, c), 1 - y, sibling)
    home = pltpu.make_async_copy(own, spot(y, c), send.at[3])

    def begin():
        home.start()
        for one in first:
            one.start()

    def finish():
        incoming(0, 1 - y, c, y_side).wait_recv()
        onward.start()
        incoming(1, y, 1 - c, sibling).wait_recv()
        incoming(2, 1 - y, 1 - c, sibling).wait_recv()
        home.wait()
        for one in first + [onward]:
            one.wait_send()

    return begin, finish


def gathered_and_spread(line, rows, own, all_rows, full, send, recv, local, ssend, srecv):
    greet(line)
    begin, finish = spread_copies(own, full, ssend, srecv)
    gather_steps(line, False, (rows,), (all_rows,), send, recv, local, begin)
    finish()


def gather_and_spread(rows, own, line, collective_id):
    groups = 2 * line
    return pl.pallas_call(
        functools.partial(gathered_and_spread, line),
        out_shape=[
            jax.ShapeDtypeStruct((4, rows.shape[1] * groups, rows.shape[2]), rows.dtype),
            jax.ShapeDtypeStruct((8,) + own.shape[1:], own.dtype),
        ],
        in_specs=[pl.BlockSpec(memory_space=pltpu.VMEM)] * 2,
        out_specs=[pl.BlockSpec(memory_space=pl.ANY)] * 2,
        scratch_shapes=[
            pltpu.SemaphoreType.DMA((1, PAIR * line)),
            pltpu.SemaphoreType.DMA((1, PAIR * line)),
            pltpu.SemaphoreType.DMA((1,)),
            pltpu.SemaphoreType.DMA((4,)),
            pltpu.SemaphoreType.DMA((4,)),
        ],
        compiler_params=pltpu.CompilerParams(collective_id=collective_id, has_side_effects=True),
    )(rows, own)


def reduced_with_weights(line, part, grad, proj_grad, out, cuts, proj_cuts, *rest):
    scratch, (other, proj_other, wsend, wrecv, wlocal) = rest[:8], rest[8:]
    x, y, z, c = position()
    group = lax.axis_index("expert")
    parts = cuts.shape[0]
    deep, wide = cuts.shape[1], proj_cuts.shape[2]
    sibling = device(x, y, z, 1 - c)
    side = lax.div(group, parts)
    barrier = pltpu.get_barrier_semaphore()
    for n in range(parts):
        peer = c * parts + n

        @pl.when((peer != group) | (side != c))
        def _():
            pl.semaphore_signal(
                barrier, inc=1, device_id=(peer, y * 2 + side), device_id_type=MESH
            )

    greet(line, parts - (side == c).astype(jnp.int32))
    half, proj_half = parts * deep, parts * wide
    to_sibling = [
        pltpu.make_async_remote_copy(
            src_ref=source,
            dst_ref=target,
            send_sem=wsend.at[which, parts],
            recv_sem=wrecv.at[which, parts],
            device_id=sibling,
            device_id_type=MESH,
        )
        for which, (source, target) in enumerate(
            (
                (grad.at[pl.ds((1 - c) * half, half)], other),
                (proj_grad.at[:, pl.ds((1 - c) * proj_half, proj_half)], proj_other),
            )
        )
    ]
    for one in to_sibling:
        one.start()

    def outgoing(n):
        return [
            pltpu.make_async_remote_copy(
                src_ref=source,
                dst_ref=target.at[lax.rem(group, parts)],
                send_sem=wsend.at[which, n],
                recv_sem=wrecv.at[which, lax.rem(group, parts)],
                device_id=(c * parts + n, y * 2 + side),
                device_id_type=MESH,
            )
            for which, (source, target) in enumerate(
                (
                    (other.at[pl.ds(n * deep, deep)], cuts),
                    (proj_other.at[:, pl.ds(n * wide, wide)], proj_cuts),
                )
            )
        ]

    def incoming(n):
        return [
            pltpu.make_async_remote_copy(
                src_ref=target.at[n],
                dst_ref=target.at[n],
                send_sem=wsend.at[which, n],
                recv_sem=wrecv.at[which, n],
                device_id=(c * parts + n, y * 2 + side),
                device_id_type=MESH,
            )
            for which, target in enumerate((cuts, proj_cuts))
        ]

    own = lax.rem(group, parts)
    home = [
        pltpu.make_async_copy(source, target, wlocal.at[which])
        for which, (source, target) in enumerate(
            (
                (other.at[pl.ds(own * deep, deep)], cuts.at[own]),
                (proj_other.at[:, pl.ds(own * wide, wide)], proj_cuts.at[own]),
            )
        )
    ]

    def remote(n):
        return (c * parts + n != group) | (side != c)

    def between():
        for one in to_sibling:
            one.wait_recv()

        def add(n, carry):
            r = pl.multiple_of(n * 16, 16)
            other[pl.ds(r, 16)] = (
                other[pl.ds(r, 16)].astype(jnp.float32)
                + grad[pl.ds(pl.multiple_of(c * half + n * 16, 16), 16)].astype(jnp.float32)
            ).astype(other.dtype)
            return carry

        lax.fori_loop(0, half // 16, add, 0)

        def add_proj(n, carry):
            r = pl.multiple_of(n * 16, 16)
            mine = proj_grad[pl.ds(r, 16), pl.ds(pl.multiple_of(c * proj_half, 128), proj_half)]
            proj_other[pl.ds(r, 16)] = (
                proj_other[pl.ds(r, 16)].astype(jnp.float32) + mine.astype(jnp.float32)
            ).astype(other.dtype)
            return carry

        lax.fori_loop(0, proj_other.shape[0] // 16, add_proj, 0)

        for n in range(parts):
            @pl.when(remote(n))
            def _():
                for one in outgoing(n):
                    one.start()

        @pl.when(side == c)
        def _():
            for one in home:
                one.start()

    reduce_steps(line, False, (part,), (out,), (scratch,), between)
    for n in range(parts):
        @pl.when(remote(n))
        def _():
            for one in incoming(n):
                one.wait_recv()
            for one in outgoing(n):
                one.wait_send()

    for one in to_sibling:
        one.wait_send()

    @pl.when(side == c)
    def _():
        for one in home:
            one.wait()


def reduce_with_weights(part, grad, proj_grad, line, collective_id):
    groups, parts = 2 * line, line
    deep, width = part.shape[1] // groups, part.shape[2]
    vmem = pl.BlockSpec(memory_space=pltpu.VMEM)
    cut = (parts, grad.shape[0] // groups, grad.shape[1])
    proj_cut = (parts, proj_grad.shape[0], proj_grad.shape[1] // groups)
    return pl.pallas_call(
        functools.partial(reduced_with_weights, line),
        out_shape=[
            jax.ShapeDtypeStruct((2, deep, width), jnp.float32),
            jax.ShapeDtypeStruct(cut, grad.dtype),
            jax.ShapeDtypeStruct(proj_cut, grad.dtype),
        ],
        in_specs=[vmem] * 3,
        out_specs=[vmem] * 3,
        scratch_shapes=reduce_scratch(line, False, deep, width, part.dtype)
        + [
            pltpu.VMEM((grad.shape[0] // 2, grad.shape[1]), grad.dtype),
            pltpu.VMEM((proj_grad.shape[0], proj_grad.shape[1] // 2), grad.dtype),
            pltpu.SemaphoreType.DMA((2, parts + 1)),
            pltpu.SemaphoreType.DMA((2, parts + 1)),
            pltpu.SemaphoreType.DMA((2,)),
        ],
        compiler_params=pltpu.CompilerParams(
            collective_id=collective_id, has_side_effects=True, vmem_limit_bytes=60 << 20
        ),
    )(part, grad, proj_grad)


def finished(line, own, small, full, total, ssend, srecv, held, tensor_held, send, recv):
    x, y, z, c = position()
    group, groups, member = lax.axis_index("expert"), 2 * line, lax.axis_index("tensor")
    barrier = pltpu.get_barrier_semaphore()
    for hop in range(1, groups):
        pl.semaphore_signal(
            barrier, inc=1, device_id=(lax.rem(group + hop, groups), member), device_id_type=MESH
        )
    for hop in range(1, 4):
        pl.semaphore_signal(
            barrier, inc=1, device_id=(group, lax.rem(member + hop, 4)), device_id_type=MESH
        )
    pl.semaphore_wait(barrier, groups + 2)
    wide = total.shape[1]

    def outgoing(hop):
        to = lax.rem(group + hop, groups)
        return pltpu.make_async_remote_copy(
            src_ref=small.at[:, pl.ds(to * wide, wide)],
            dst_ref=held.at[hop],
            send_sem=send.at[hop],
            recv_sem=recv.at[hop],
            device_id=(to, member),
            device_id_type=MESH,
        )

    def onward(hop):
        return pltpu.make_async_remote_copy(
            src_ref=held.at[0],
            dst_ref=tensor_held.at[hop],
            send_sem=send.at[groups + hop],
            recv_sem=recv.at[groups + hop],
            device_id=(group, lax.rem(member + hop, 4)),
            device_id_type=MESH,
        )

    for hop in range(1, groups):
        outgoing(hop).start()
    begin, finish = spread_copies(own, full, ssend, srecv)
    begin()
    value = small[:, pl.ds(pl.multiple_of(group * wide, 128), wide)]
    for hop in range(1, groups):
        outgoing(hop).wait_recv()
        value = value + held[hop]
    held[0] = value
    for hop in range(1, 4):
        onward(hop).start()
    finish()
    for hop in range(1, 4):
        onward(hop).wait_recv()
        value = value + tensor_held[hop]
    total[...] = value
    for hop in range(1, groups):
        outgoing(hop).wait_send()
    for hop in range(1, 4):
        onward(hop).wait_send()


def finish_rows(own, small, line, collective_id):
    groups = 2 * line
    vmem = pl.BlockSpec(memory_space=pltpu.VMEM)
    wide = small.shape[1] // groups
    return pl.pallas_call(
        functools.partial(finished, line),
        out_shape=[
            jax.ShapeDtypeStruct((8,) + own.shape[1:], own.dtype),
            jax.ShapeDtypeStruct((small.shape[0], wide), jnp.float32),
        ],
        in_specs=[vmem] * 2,
        out_specs=[vmem] * 2,
        scratch_shapes=[
            pltpu.SemaphoreType.DMA((4,)),
            pltpu.SemaphoreType.DMA((4,)),
            pltpu.VMEM((groups, small.shape[0], wide), jnp.float32),
            pltpu.VMEM((4, small.shape[0], wide), jnp.float32),
            pltpu.SemaphoreType.DMA((groups + 4,)),
            pltpu.SemaphoreType.DMA((groups + 4,)),
        ],
        compiler_params=pltpu.CompilerParams(collective_id=collective_id, has_side_effects=True),
    )(own, small)


def experts_and_sums(
    line, experts, rows, grads, gates, both, down, out, row_grad, gated_o, pre_o, *rest
):
    works, rest = [rest[8 * i : 8 * i + 8] for i in range(2)], rest[16:]
    part_out, part_rows, row_buf, grad_buf, gate_buf, gated_buf, pre_buf, load, store = rest
    x, y, z, c = position()
    group = lax.axis_index("expert")
    deep, width = rows.shape[2], rows.shape[3]
    hidden = down.shape[0]
    block = 2 * deep
    greet(line)

    def blocks_of(part):
        return lambda xx, yy, zz, cc: part.at[(zz * 2 + xx) * 4 + yy * 2 + cc]

    sums = [
        reduce_phases(line, True, blocks_of(part), target, *work)
        for part, target, work in zip((part_out, part_rows), (out, row_grad), works)
    ]
    steps = 4 * line // 2

    def chips(step):
        turn = lax.rem(step, 4)
        way = jnp.where(turn == 0, 3, jnp.where(turn == 3, 0, turn))
        return way, pair_of(lax.div(step, 4))

    def pair_of(number):
        far = [2 * number + j for j in range(2)]
        return [jnp.where(2 * z < line, line - 1 - k, k) for k in far]

    def first_block(step, j):
        way, zs = chips(step)
        xx, yy = column(way)
        return (zs[j] * 2 + xx) * 4 + yy * 2

    def loads(step, slot):
        return [
            pltpu.make_async_copy(
                source.at[pl.ds(first_block(step, j), 2)],
                target.at[slot, pl.ds(2 * j, 2)],
                load.at[slot, which, j],
            )
            for which, (source, target) in enumerate(
                ((rows, row_buf), (grads, grad_buf), (gates, gate_buf))
            )
            for j in range(2)
        ]

    def stores(step, slot):
        return [
            pltpu.make_async_copy(
                source.at[slot, pl.ds(2 * block * j, 2 * block)],
                target.at[pl.ds(first_block(step, j) * block, 2 * block)],
                store.at[slot, which, j],
            )
            for which, (source, target) in enumerate(((gated_buf, gated_o), (pre_buf, pre_o)))
            for j in range(2)
        ]

    def act(copies, what):
        for one in copies:
            getattr(one, what)()

    act(loads(0, 0), "start")
    experts_here = hidden // experts
    lane = lax.broadcasted_iota(jnp.int32, (4 * block, gates.shape[3]), 1)

    def body(step, carry):
        slot = lax.rem(step, 2)
        pl.when(step + 1 < steps)(lambda: act(loads(step + 1, 1 - slot), "start"))
        act(loads(step, slot), "wait")
        pl.when(step >= 2)(lambda: act(stores(step - 2, slot), "wait"))
        here = row_buf[slot].reshape(4 * block, width)
        grad_here = grad_buf[slot].reshape(4 * block, width)
        gate_here = gate_buf[slot].reshape(4 * block, gates.shape[3])
        pre = dot(here, both[...])
        plain = dot(grad_here, down[...], ((1,), (1,)))
        gate_term = jnp.zeros_like(gate_here)
        gated, grad_gate, grad_up = [], [], []
        for n in range(experts):
            mine = lane == group * experts + n
            gate = jnp.sum(jnp.where(mine, gate_here, 0.0), axis=-1, keepdims=True)
            gate_pre = pre[:, n * experts_here : (n + 1) * experts_here]
            up_pre = pre[:, hidden + n * experts_here : hidden + (n + 1) * experts_here]
            grad_plain = plain[:, n * experts_here : (n + 1) * experts_here]
            sigmoid = 1.0 / (1.0 + jnp.exp(-gate_pre))
            silu = gate_pre * sigmoid
            value = silu * up_pre
            sum_here = jnp.sum(value * grad_plain, axis=-1, keepdims=True)
            gate_term = jnp.where(mine, sum_here, gate_term)
            gated.append((gate * value).astype(jnp.bfloat16))
            grad_value = gate * grad_plain
            grad_gate.append(
                (grad_value * up_pre * sigmoid * (1.0 + gate_pre * (1.0 - sigmoid))).astype(
                    jnp.bfloat16
                )
            )
            grad_up.append((grad_value * silu).astype(jnp.bfloat16))
        gated_buf[slot] = jnp.concatenate(gated, axis=1)
        pre_buf[slot] = jnp.concatenate(grad_gate + grad_up, axis=1)
        act(stores(step, slot), "start")
        firsts = [first_block(step, j) for j in range(2)]

        def keep(part, value, n, tile):
            value = value.astype(part.dtype)
            for j in range(2):
                piece = value[2 * block * j : 2 * block * (j + 1)].reshape(2, 2, deep, tile)
                part[pl.ds(firsts[j], 2), :, :, n * tile : (n + 1) * tile] = piece

        tile = 512
        for n in range(width // tile):
            keep(part_out, dot(gated_buf[slot], down[:, n * tile : (n + 1) * tile]), n, tile)
        for n in range(width // tile):
            columns = both[n * tile : (n + 1) * tile]
            keep(part_rows, dot(pre_buf[slot], columns, ((1,), (1,))), n, tile)
        keep(part_rows, gate_term, width // gates.shape[3], gates.shape[3])
        way, zs = chips(step)
        for zz in zs:
            for one in sums:
                one["half"](way, zz)
        last_way, last = chips(step - 1)

        @pl.when((step > 0) & (last_way == 3))
        def _():
            for zz in last:
                for one in sums:
                    one["corner_of"](zz)

        for side in (1, 2):
            @pl.when((step > 0) & (last_way == side))
            def _():
                for zz in last:
                    for one in sums:
                        one["direct"](side, zz)

        @pl.when((step > 0) & (last_way == 0))
        def _():
            dependents(last)

        return carry

    def dependents(zs):
        for zz in zs:
            for one in sums:
                one["dependent"](zz)

    def along(zs):
        for zz in zs:
            for sign in (1, -1):
                @pl.when(sign * zz > sign * z)
                def _():
                    for one in sums:
                        one["along_of"](zz, sign)

    lax.fori_loop(0, steps, body, 0)
    for number in range(line // 2):
        if number == line // 2 - 1:
            dependents(pair_of(number))
        along(pair_of(number))
    for one in sums:
        one["along_of"](z, 0)
    for one in sums:
        one["drain"]()
    for step in (steps - 2, steps - 1):
        act(stores(step, step % 2), "wait")


def experts_to_rows(rows, grads, gates, both, down, experts, line, collective_id):
    count, _, deep, width = rows.shape
    lanes, hidden = gates.shape[3], down.shape[0]
    tokens, block = count * 2 * deep, 2 * deep
    vmem = pl.BlockSpec(memory_space=pltpu.VMEM)
    anywhere = pl.BlockSpec(memory_space=pl.ANY)
    scratch = []
    for wide in (width, width + lanes):
        scratch += reduce_scratch(line, True, deep, wide, rows.dtype)
    return pl.pallas_call(
        functools.partial(experts_and_sums, line, experts),
        out_shape=[
            jax.ShapeDtypeStruct((2, deep, width), jnp.float32),
            jax.ShapeDtypeStruct((2, deep, width + lanes), jnp.float32),
            jax.ShapeDtypeStruct((tokens, hidden), rows.dtype),
            jax.ShapeDtypeStruct((tokens, 2 * hidden), rows.dtype),
        ],
        in_specs=[anywhere] * 3 + [vmem] * 2,
        out_specs=[vmem] * 2 + [anywhere] * 2,
        scratch_shapes=scratch
        + [
            pltpu.VMEM((count, 2, deep, width), rows.dtype),
            pltpu.VMEM((count, 2, deep, width + lanes), rows.dtype),
            pltpu.VMEM((2, 4, 2, deep, width), rows.dtype),
            pltpu.VMEM((2, 4, 2, deep, width), rows.dtype),
            pltpu.VMEM((2, 4, 2, deep, lanes), gates.dtype),
            pltpu.VMEM((2, 4 * block, hidden), rows.dtype),
            pltpu.VMEM((2, 4 * block, 2 * hidden), rows.dtype),
            pltpu.SemaphoreType.DMA((2, 3, 2)),
            pltpu.SemaphoreType.DMA((2, 2, 2)),
        ],
        compiler_params=pltpu.CompilerParams(
            collective_id=collective_id, has_side_effects=True, vmem_limit_bytes=67043328
        ),
    )(rows, grads, gates, both, down)


def dot(left, right, over=((1,), (0,))):
    return lax.dot_general(left, right, (over, ((), ())), preferred_element_type=jnp.float32)


def on_device(
    inputs,
    cotangent,
    lengths,
    permutation,
    routes,
    query_weight,
    key_weight,
    value_weight,
    proj_weight,
    first_gain,
    second_gain,
    query_gain,
    key_gain,
    router_weight,
    gate_weight,
    up_weight,
    down_weight,
):
    sequences, deep, model_width = inputs.shape
    groups = lax.axis_size("expert")
    line = groups // 2
    rows = deep * groups
    expert_count = router_weight.shape[1]
    local_experts, _, hidden_width = gate_weight.shape
    group, member = lax.axis_index("expert"), lax.axis_index("tensor")
    y, c = member // 2, member % 2
    first_own = 4 * c + 2 * y
    low = jnp.bfloat16
    score_scale = math.sqrt(HD)

    own_in = lax.dynamic_slice_in_dim(inputs, first_own, 2)
    own_cot = lax.dynamic_slice_in_dim(cotangent, first_own, 2)
    cut = (
        jnp.stack([query_weight, key_weight, value_weight], axis=0)
        .astype(low)
        .reshape(3, -1, line, HD)
        .transpose(2, 1, 0, 3)
        .reshape(line, -1, 3 * HD)
    )
    proj_cut = proj_weight.astype(low).reshape(line, HD, -1)
    named = jnp.sum(
        (routes[:, :, None] == jnp.arange(expert_count, dtype=jnp.int32)).astype(jnp.float32), axis=1
    )
    width = first_gain.shape[0]
    gain_rows = jnp.zeros((16, width), jnp.float32)
    gain_rows = gain_rows.at[0].set(first_gain).at[1].set(second_gain)
    share = query_gain.shape[0]
    gain_rows = gain_rows.at[2, :share].set(query_gain).at[2, share : 2 * share].set(key_gain)
    small = jnp.concatenate([gain_rows, router_weight.T, named.T], axis=0).astype(low)
    all_in, head_weight, head_proj, all_small = gather_with_weights(
        own_in, cut, proj_cut, small, line, 1
    )
    gain_one = all_small[0].astype(jnp.float32)
    gain_two = all_small[1].astype(jnp.float32)
    shares = all_small[2].reshape(groups, width).astype(jnp.float32)
    gain_query = shares[:, :share].reshape(HD)
    gain_key = shares[:, share : 2 * share].reshape(HD)
    router_rows = all_small[16 : 16 + expert_count]
    named_all = all_small[16 + expert_count :]

    normed_one = norm_parts(all_in.reshape(4 * rows, model_width).astype(jnp.float32), gain_one)[0]
    normed_one = normed_one.astype(low)
    projected = dot(normed_one, head_weight)
    queries_raw = projected[:, :HD].reshape(4, rows, HD)
    keys_raw = projected[:, HD : 2 * HD].reshape(4, rows, HD)
    values = projected[:, 2 * HD :].astype(low).reshape(4, rows, HD)
    cos_table, sin_table = rope_tables(rows, HD)
    cos_table, sin_table = cos_table[:, 0], sin_table[:, 0]
    query_normed, query_unit, query_inverse = norm_parts(queries_raw, gain_query)
    key_normed, key_unit, key_inverse = norm_parts(keys_raw, gain_key)
    queries = rotate(query_normed, cos_table, sin_table).astype(low)
    keys_rot = rotate(key_normed, cos_table, sin_table).astype(low)
    my_lengths = lax.dynamic_slice_in_dim(lengths, 4 * c, 4)
    usable = jnp.arange(rows)[None, :] < my_lengths[:, None]
    scores = (
        jnp.einsum("sqd,skd->sqk", queries, keys_rot, preferred_element_type=jnp.float32)
        / score_scale
    )
    scores = jnp.where(usable[:, None, :], scores, NEG_FILL)
    exponent = jnp.exp(scores - jnp.max(scores, axis=-1, keepdims=True))
    softmax_f = exponent / jnp.sum(exponent, axis=-1, keepdims=True)
    probs = softmax_f.astype(low)
    context = jnp.einsum("sqk,skd->sqd", probs, values, preferred_element_type=jnp.float32)
    context = context.astype(low).reshape(4 * rows, HD)
    attn_part = dot(context, head_proj).astype(low).reshape(4, rows, model_width)
    (attn_total,) = reduce_rows((attn_part,), line, False, 2)

    source = own_in.astype(jnp.float32)
    residual = source + attn_total
    normed_two_f, unit_two, inverse_two = norm_parts(residual, gain_two)
    normed_two = normed_two_f.astype(low)
    flat_two = normed_two.reshape(2 * deep, model_width)
    logits = dot(flat_two, router_rows, ((1,), (1,)))
    slot_of_seq = jnp.argmax(
        permutation[None, :] == jnp.arange(sequences, dtype=jnp.int32)[:, None], axis=1
    ).astype(jnp.int32)
    own_slots = lax.dynamic_slice_in_dim(slot_of_seq, first_own, 2)
    own_named = jnp.concatenate(
        [
            lax.dynamic_slice_in_dim(named_all, own_slots[k] * rows + group * deep, deep, axis=1)
            for k in range(2)
        ],
        axis=1,
    ).T.astype(jnp.float32)
    gates = jax.nn.softmax(jnp.where(own_named > 0.5, logits, NEG_FILL), axis=-1)
    lanes = 128
    gate_rows = jnp.pad(gates, ((0, 0), (0, lanes - expert_count))).reshape(2, deep, lanes)
    all_rows, all_grad, all_gates = gather_rows([normed_two, own_cot, gate_rows], line, True, 3)
    tokens = sequences * rows
    wide = local_experts * hidden_width
    both_matrix = (
        jnp.concatenate([gate_weight, up_weight], axis=0)
        .astype(low)
        .transpose(1, 0, 2)
        .reshape(model_width, 2 * wide)
    )
    down_matrix = down_weight.astype(low).reshape(wide, model_width)
    moe_total, row_sums, gated, grad_pre = experts_to_rows(
        all_rows, all_grad, all_gates, both_matrix, down_matrix, local_experts, line, 4
    )
    grad_normed_two, gate_total = row_sums[..., :model_width], row_sums[..., model_width:]
    flat_rows = all_rows.reshape(tokens, model_width)
    flat_grad = all_grad.reshape(tokens, model_width)
    down_grad = dot(gated, flat_grad, ((0,), (0,))).reshape(local_experts, hidden_width, model_width)

    def by_expert(first):
        return jnp.stack(
            [
                dot(flat_rows, grad_pre[:, start : start + hidden_width], ((0,), (0,)))
                for start in range(first, first + wide, hidden_width)
            ]
        )

    gate_grad, up_grad = by_expert(0), by_expert(wide)

    own_out = (residual + moe_total).astype(low)
    gate_total = gate_total.reshape(2 * deep, lanes)[:, :expert_count]
    grad_logits = (
        gates * (gate_total - jnp.sum(gates * gate_total, axis=-1, keepdims=True))
    ).astype(low)
    grad_normed_two = grad_normed_two + dot(grad_logits, router_rows).reshape(2, deep, model_width)
    router_part = dot(grad_logits, flat_two, ((0,), (0,)))
    second_part = jnp.sum(grad_normed_two * unit_two, axis=(0, 1))
    grad_state = own_cot.astype(jnp.float32) + norm_back(
        grad_normed_two, gain_two, unit_two, inverse_two
    )
    all_state, output = gather_and_spread(grad_state.astype(low), own_out, line, 5)

    all_state = all_state.reshape(4 * rows, model_width)
    proj_grad = dot(context, all_state, ((0,), (0,))).astype(low)
    grad_context = dot(all_state, head_proj, ((1,), (1,))).astype(low).reshape(4, rows, HD)
    grad_values = jnp.einsum("sqk,sqd->skd", probs, grad_context, preferred_element_type=jnp.float32)
    grad_probs = jnp.einsum("sqd,skd->sqk", grad_context, values, preferred_element_type=jnp.float32)
    grad_scores = (
        softmax_f * (grad_probs - jnp.sum(grad_probs * softmax_f, axis=-1, keepdims=True))
    ).astype(low)
    grad_queries = (
        jnp.einsum("sqk,skd->sqd", grad_scores, keys_rot, preferred_element_type=jnp.float32)
        / score_scale
    )
    grad_keys = (
        jnp.einsum("sqk,sqd->skd", grad_scores, queries, preferred_element_type=jnp.float32)
        / score_scale
    )
    grad_queries = rotate(grad_queries, cos_table, -sin_table)
    grad_keys = rotate(grad_keys, cos_table, -sin_table)
    query_gain_part = jnp.sum(grad_queries * query_unit, axis=(0, 1))
    key_gain_part = jnp.sum(grad_keys * key_unit, axis=(0, 1))
    grad_projected = jnp.concatenate(
        [
            norm_back(grad_queries, gain_query, query_unit, query_inverse).astype(low),
            norm_back(grad_keys, gain_key, key_unit, key_inverse).astype(low),
            grad_values.astype(low),
        ],
        axis=-1,
    ).reshape(4 * rows, 3 * HD)
    head_grad = dot(normed_one, grad_projected, ((0,), (0,))).astype(low)
    one_part = dot(grad_projected, head_weight, ((1,), (1,))).astype(low)
    grad_normed_one, cuts, proj_cuts = reduce_with_weights(
        one_part.reshape(4, rows, model_width), head_grad, proj_grad, line, 6
    )

    _, unit_one, inverse_one = norm_parts(source, gain_one)
    first_part = jnp.sum(grad_normed_one * unit_one, axis=(0, 1))
    own_grad = (grad_state + norm_back(grad_normed_one, gain_one, unit_one, inverse_one)).astype(low)

    def by_share(values):
        return jnp.pad(values.reshape(groups, share), ((0, 0), (0, width - share))).reshape(1, -1)

    small_grads = jnp.concatenate(
        [
            first_part[None],
            second_part[None],
            by_share(query_gain_part),
            by_share(key_gain_part),
            jnp.zeros((4, model_width), jnp.float32),
            router_part,
        ],
        axis=0,
    )
    input_grad, small_total = finish_rows(own_grad, small_grads, line, 7)
    owned = cuts.reshape(line, -1, 3, HD).transpose(2, 1, 0, 3).reshape(3, -1, line * HD)
    owned = owned.astype(jnp.float32)
    return (
        output,
        input_grad,
        owned[0],
        owned[1],
        owned[2],
        proj_cuts.reshape(line * HD, -1).astype(jnp.float32),
        small_total[0],
        small_total[1],
        small_total[2, :share],
        small_total[3, :share],
        small_total[8:].T,
        gate_grad,
        up_grad,
        down_grad,
    )


def on_device_paired(
    inputs,
    cotangent,
    lengths,
    permutation,
    routes,
    query_weight,
    key_weight,
    value_weight,
    proj_weight,
    first_gain,
    second_gain,
    query_gain,
    key_gain,
    router_weight,
    gate_weight,
    up_weight,
    down_weight,
):
    model_width = inputs.shape[2]
    local_heads = query_weight.shape[1] // HD
    expert_count = router_weight.shape[1]
    groups_count = lax.axis_size("expert")
    local_experts = gate_weight.shape[0]
    slot_index = lax.axis_index("expert")
    seq_ids = jnp.arange(permutation.shape[0], dtype=jnp.int32)
    my_sequence = jnp.sum(jnp.where(seq_ids == slot_index, permutation, 0))
    my_length = jnp.sum(jnp.where(seq_ids == my_sequence, lengths, 0))
    slot_of_seq = jnp.sum(
        jnp.where(permutation[None, :] == seq_ids[:, None], seq_ids[None, :], 0), axis=1
    )
    dealt_in, dealt_grad = (
        lax.all_to_all(inputs[permutation], "expert", split_axis=0, concat_axis=1, tiled=True),
        lax.all_to_all(cotangent[permutation], "expert", split_axis=0, concat_axis=1, tiled=True),
    )
    token_rows = dealt_in.shape[1]
    capacity = token_rows * TOPK * 33 // (32 * expert_count)
    block_rows = min(512, token_rows)
    score_scale = math.sqrt(HD)
    gathered = (
        lax.all_gather(query_weight.astype(jnp.bfloat16), "expert", axis=0, tiled=True),
        lax.all_gather(key_weight.astype(jnp.bfloat16), "expert", axis=0, tiled=True),
        lax.all_gather(value_weight.astype(jnp.bfloat16), "expert", axis=0, tiled=True),
        lax.all_gather(proj_weight.astype(jnp.bfloat16), "expert", axis=1, tiled=True),
        lax.all_gather(first_gain.astype(jnp.bfloat16), "expert", axis=0, tiled=True),
        lax.all_gather(second_gain.astype(jnp.bfloat16), "expert", axis=0, tiled=True),
        lax.all_gather(query_gain.astype(jnp.bfloat16), "expert", axis=0, tiled=True),
        lax.all_gather(key_gain.astype(jnp.bfloat16), "expert", axis=0, tiled=True),
        lax.all_gather(router_weight.astype(jnp.bfloat16), "expert", axis=0, tiled=True),
    )
    query_matrix = gathered[0]
    key_matrix = gathered[1]
    value_matrix = gathered[2]
    proj_matrix = gathered[3]
    gain_one = gathered[4].astype(jnp.float32)
    gain_two = gathered[5].astype(jnp.float32)
    gain_query = gathered[6].astype(jnp.float32)
    gain_key = gathered[7].astype(jnp.float32)
    router_matrix = gathered[8]
    gate_matrix = gate_weight.astype(jnp.bfloat16)
    up_matrix = up_weight.astype(jnp.bfloat16)
    down_matrix = down_weight.astype(jnp.bfloat16)
    source = dealt_in.reshape(token_rows, model_width).astype(jnp.float32)
    normed_one_f, unit_one, inverse_one = norm_parts(source, gain_one)
    normed_one = normed_one_f.astype(jnp.bfloat16)
    queries_raw = jnp.dot(normed_one, query_matrix, preferred_element_type=jnp.float32).reshape(
        token_rows, local_heads, HD
    )
    keys_raw = jnp.dot(normed_one, key_matrix, preferred_element_type=jnp.float32).reshape(
        token_rows, local_heads, HD
    )
    values = (
        jnp.dot(normed_one, value_matrix, preferred_element_type=jnp.float32)
        .astype(jnp.bfloat16)
        .reshape(token_rows, local_heads, HD)
    )
    cos_table, sin_table = rope_tables(token_rows, HD)
    query_normed, query_unit, query_inverse = norm_parts(queries_raw, gain_query)
    key_normed, key_unit, key_inverse = norm_parts(keys_raw, gain_key)
    queries = rotate(query_normed, cos_table, sin_table).astype(jnp.bfloat16)
    keys_rot = rotate(key_normed, cos_table, sin_table).astype(jnp.bfloat16)
    usable = jnp.arange(token_rows) < my_length

    def block_scores():
        scores = (
            jnp.einsum("qhd,khd->hqk", queries, keys_rot, preferred_element_type=jnp.float32)
            / score_scale
        )
        return (queries, jnp.where(usable[None, None, :], scores, NEG_FILL))

    query_block, scores = block_scores()
    maximum = jnp.max(scores, axis=-1, keepdims=True)
    exponent = jnp.exp(scores - maximum)
    row_total = jnp.sum(exponent, axis=-1, keepdims=True)
    softmax_rows = (exponent / row_total).astype(jnp.bfloat16)
    context_blocks = jnp.einsum(
        "hqk,khd->qhd", softmax_rows, values, preferred_element_type=jnp.float32
    ).astype(jnp.bfloat16)
    lse_blocks = [maximum + jnp.log(row_total)]
    context = context_blocks.reshape(token_rows, local_heads * HD)
    attn_part = jnp.dot(context, proj_matrix, preferred_element_type=jnp.float32)
    attn_total = lax.psum(attn_part, "tensor")
    residual = source + attn_total
    normed_two_f, unit_two, inverse_two = norm_parts(residual, gain_two)
    normed_two = normed_two_f.astype(jnp.bfloat16)
    logits = jnp.dot(normed_two, router_matrix, preferred_element_type=jnp.float32)
    choose = (
        routes[:, :, None] == jnp.arange(expert_count, dtype=jnp.int32)[None, None, :]
    ).astype(jnp.float32)
    chosen = jnp.sum(choose * logits[:, None, :], axis=-1)
    gate_probs = jax.nn.softmax(chosen, axis=-1)
    flat_routes = routes.reshape(-1)
    route_hits = (
        flat_routes[:, None] == jnp.arange(expert_count, dtype=jnp.int32)[None, :]
    ).astype(jnp.int32)
    rank_ids = jnp.sum(jnp.cumsum(route_hits, axis=0) * route_hits, axis=1) - 1
    slot_ids = flat_routes * capacity + rank_ids
    pair_tokens = jnp.arange(flat_routes.shape[0], dtype=jnp.int32) // TOPK
    send_rows = (
        jnp.zeros((expert_count * capacity, model_width), jnp.bfloat16)
        .at[slot_ids]
        .set(normed_two[pair_tokens])
    )
    send_rows = send_rows.reshape(groups_count, local_experts, capacity, model_width)
    received = lax.all_to_all(send_rows, "expert", split_axis=0, concat_axis=0, tiled=True)
    gate_pre = jnp.einsum(
        "secd,edf->secf", received, gate_matrix, preferred_element_type=jnp.float32
    )
    up_pre = jnp.einsum("secd,edf->secf", received, up_matrix, preferred_element_type=jnp.float32)
    hidden = (jax.nn.silu(gate_pre) * up_pre).astype(jnp.bfloat16)
    result = jnp.einsum(
        "secf,efd->secd", hidden, down_matrix, preferred_element_type=jnp.float32
    ).astype(jnp.bfloat16)
    returned = lax.all_to_all(result, "expert", split_axis=0, concat_axis=0, tiled=True)
    picked = returned.reshape(expert_count * capacity, model_width)[slot_ids].reshape(
        token_rows, TOPK, model_width
    )
    combined = jnp.sum(gate_probs[:, :, None] * picked.astype(jnp.float32), axis=1)
    moe_total = lax.psum(combined.astype(jnp.bfloat16), "tensor").astype(jnp.float32)
    output = (residual + moe_total).astype(jnp.bfloat16)
    grad_out = dealt_grad.reshape(token_rows, model_width).astype(jnp.float32)
    gate_grad_part = jnp.sum(grad_out[:, None, :] * picked.astype(jnp.float32), axis=-1)
    routed_grad = (
        (gate_probs[:, :, None] * grad_out[:, None, :])
        .astype(jnp.bfloat16)
        .reshape(token_rows * TOPK, model_width)
    )
    grad_send = (
        jnp.zeros((expert_count * capacity, model_width), jnp.bfloat16)
        .at[slot_ids]
        .set(routed_grad)
    )
    grad_send = grad_send.reshape(groups_count, local_experts, capacity, model_width)
    grad_rows, rows_in = (
        lax.all_to_all(grad_send, "expert", split_axis=0, concat_axis=0, tiled=True),
        lax.all_to_all(send_rows, "expert", split_axis=0, concat_axis=0, tiled=True),
    )
    gate_pre = jnp.einsum(
        "secd,edf->secf", rows_in, gate_matrix, preferred_element_type=jnp.float32
    )
    up_pre = jnp.einsum("secd,edf->secf", rows_in, up_matrix, preferred_element_type=jnp.float32)
    grad_hidden = jnp.einsum(
        "secd,efd->secf", grad_rows, down_matrix, preferred_element_type=jnp.float32
    )
    sigmoid_gate = jax.nn.sigmoid(gate_pre)
    silu_gate = gate_pre * sigmoid_gate
    grad_gate_pre = (
        grad_hidden * up_pre * sigmoid_gate * (1.0 + gate_pre * (1.0 - sigmoid_gate))
    ).astype(jnp.bfloat16)
    grad_up_pre = (grad_hidden * silu_gate).astype(jnp.bfloat16)
    hidden = (silu_gate * up_pre).astype(jnp.bfloat16)
    rows_grad = (
        jnp.einsum("secf,edf->secd", grad_gate_pre, gate_matrix, preferred_element_type=jnp.float32)
        + jnp.einsum("secf,edf->secd", grad_up_pre, up_matrix, preferred_element_type=jnp.float32)
    ).astype(jnp.bfloat16)
    down_grad = jnp.einsum("secf,secd->efd", hidden, grad_rows, preferred_element_type=jnp.float32)
    gate_grad = jnp.einsum(
        "secd,secf->edf", rows_in, grad_gate_pre, preferred_element_type=jnp.float32
    )
    up_grad = jnp.einsum("secd,secf->edf", rows_in, grad_up_pre, preferred_element_type=jnp.float32)
    returned_grad = lax.all_to_all(rows_grad, "expert", split_axis=0, concat_axis=0, tiled=True)
    returned_pairs = returned_grad.reshape(expert_count * capacity, model_width)[slot_ids].reshape(
        token_rows, TOPK, model_width
    )
    normed_two_part = jnp.sum(returned_pairs.astype(jnp.float32), axis=1)
    grad_normed_two, gate_grad_total = lax.psum((normed_two_part, gate_grad_part), "tensor")
    grad_chosen = gate_probs * (
        gate_grad_total - jnp.sum(gate_probs * gate_grad_total, axis=-1, keepdims=True)
    )
    grad_logits = jnp.sum(choose * grad_chosen[:, :, None], axis=1).astype(jnp.bfloat16)
    grad_normed_two = grad_normed_two + jnp.dot(
        grad_logits, router_matrix.T, preferred_element_type=jnp.float32
    )
    router_grad = jnp.dot(normed_two.T, grad_logits, preferred_element_type=jnp.float32)
    second_gain_grad = jnp.sum(grad_normed_two * unit_two, axis=0)
    grad_state = grad_out + norm_back(grad_normed_two, gain_two, unit_two, inverse_two)
    grad_context_in = grad_state.astype(jnp.bfloat16)
    proj_grad = jnp.dot(context.T, grad_context_in, preferred_element_type=jnp.float32)
    grad_context = (
        jnp.dot(grad_context_in, proj_matrix.T, preferred_element_type=jnp.float32)
        .astype(jnp.bfloat16)
        .reshape(token_rows, local_heads, HD)
    )
    grad_values = jnp.zeros((token_rows, local_heads, HD), jnp.float32)
    grad_keys_rot = jnp.zeros((token_rows, local_heads, HD), jnp.float32)
    grad_query_blocks = []
    for number, start_row in enumerate(range(0, token_rows, block_rows)):
        query_block, scores = block_scores()
        softmax_f = jnp.exp(scores - lse_blocks[number])
        grad_values = jnp.einsum(
            "hqk,qhd->khd",
            softmax_f.astype(jnp.bfloat16),
            grad_context,
            preferred_element_type=jnp.float32,
        )
        grad_probs = jnp.einsum(
            "qhd,khd->hqk", grad_context, values, preferred_element_type=jnp.float32
        )
        grad_scores = (
            softmax_f * (grad_probs - jnp.sum(grad_probs * softmax_f, axis=-1, keepdims=True))
        ).astype(jnp.bfloat16)
        grad_query_blocks.append(
            jnp.einsum("hqk,khd->qhd", grad_scores, keys_rot, preferred_element_type=jnp.float32)
            / score_scale
        )
        grad_keys_rot = (
            jnp.einsum("hqk,qhd->khd", grad_scores, query_block, preferred_element_type=jnp.float32)
            / score_scale
        )
    grad_queries_n = rotate(grad_query_blocks[0], cos_table, -sin_table)
    grad_keys_n = rotate(grad_keys_rot, cos_table, -sin_table)
    query_gain_part = jnp.sum(grad_queries_n * query_unit, axis=(0, 1))
    key_gain_part = jnp.sum(grad_keys_n * key_unit, axis=(0, 1))
    grad_queries_raw = (
        norm_back(grad_queries_n, gain_query, query_unit, query_inverse)
        .astype(jnp.bfloat16)
        .reshape(token_rows, local_heads * HD)
    )
    grad_keys_raw = (
        norm_back(grad_keys_n, gain_key, key_unit, key_inverse)
        .astype(jnp.bfloat16)
        .reshape(token_rows, local_heads * HD)
    )
    grad_values_low = grad_values.astype(jnp.bfloat16).reshape(token_rows, local_heads * HD)
    query_grad = jnp.dot(normed_one.T, grad_queries_raw, preferred_element_type=jnp.float32)
    key_grad = jnp.dot(normed_one.T, grad_keys_raw, preferred_element_type=jnp.float32)
    value_grad = jnp.dot(normed_one.T, grad_values_low, preferred_element_type=jnp.float32)
    normed_one_part = jnp.dot(grad_queries_raw, query_matrix.T, preferred_element_type=jnp.float32)
    normed_one_part = normed_one_part + jnp.dot(
        grad_keys_raw, key_matrix.T, preferred_element_type=jnp.float32
    )
    normed_one_part = normed_one_part + jnp.dot(
        grad_values_low, value_matrix.T, preferred_element_type=jnp.float32
    )
    grad_normed_one, query_gain_total, key_gain_total = (
        lax.psum(normed_one_part.astype(jnp.bfloat16), "tensor").astype(jnp.float32),
        lax.psum(query_gain_part.astype(jnp.bfloat16), "tensor").astype(jnp.float32),
        lax.psum(key_gain_part.astype(jnp.bfloat16), "tensor").astype(jnp.float32),
    )
    first_gain_grad = jnp.sum(grad_normed_one * unit_one, axis=0)
    input_grad = (grad_state + norm_back(grad_normed_one, gain_one, unit_one, inverse_one)).astype(
        jnp.bfloat16
    )
    shards = (
        lax.psum_scatter(
            query_grad.astype(jnp.bfloat16), "expert", scatter_dimension=0, tiled=True
        ).astype(jnp.float32),
        lax.psum_scatter(
            key_grad.astype(jnp.bfloat16), "expert", scatter_dimension=0, tiled=True
        ).astype(jnp.float32),
        lax.psum_scatter(
            value_grad.astype(jnp.bfloat16), "expert", scatter_dimension=0, tiled=True
        ).astype(jnp.float32),
        lax.psum_scatter(
            proj_grad.astype(jnp.bfloat16), "expert", scatter_dimension=1, tiled=True
        ).astype(jnp.float32),
        lax.psum_scatter(
            first_gain_grad.astype(jnp.bfloat16), "expert", scatter_dimension=0, tiled=True
        ).astype(jnp.float32),
        lax.psum_scatter(
            second_gain_grad.astype(jnp.bfloat16), "expert", scatter_dimension=0, tiled=True
        ).astype(jnp.float32),
        lax.psum_scatter(
            query_gain_total.astype(jnp.bfloat16), "expert", scatter_dimension=0, tiled=True
        ).astype(jnp.float32),
        lax.psum_scatter(
            key_gain_total.astype(jnp.bfloat16), "expert", scatter_dimension=0, tiled=True
        ).astype(jnp.float32),
        lax.psum_scatter(
            router_grad.astype(jnp.bfloat16), "expert", scatter_dimension=0, tiled=True
        ).astype(jnp.float32),
    )
    back_out, back_grad = (
        lax.all_to_all(
            output.reshape(1, token_rows, model_width),
            "expert",
            split_axis=1,
            concat_axis=0,
            tiled=True,
        ),
        lax.all_to_all(
            input_grad.reshape(1, token_rows, model_width),
            "expert",
            split_axis=1,
            concat_axis=0,
            tiled=True,
        ),
    )
    ordered_out = back_out[slot_of_seq]
    ordered_grad = back_grad[slot_of_seq]
    return (
        ordered_out,
        ordered_grad,
        shards[0],
        shards[1],
        shards[2],
        shards[3],
        shards[4],
        shards[5],
        shards[6],
        shards[7],
        shards[8],
        gate_grad,
        up_grad,
        down_grad,
    )


def solution(mesh):
    in_specs = (
        P(None, "expert", None),
        P(None, "expert", None),
        P(),
        P(),
        P("expert", None),
        P("expert", "tensor"),
        P("expert", "tensor"),
        P("expert", "tensor"),
        P("tensor", "expert"),
        P("expert"),
        P("expert"),
        P("expert"),
        P("expert"),
        P("expert", None),
        P("expert", None, "tensor"),
        P("expert", None, "tensor"),
        P("expert", "tensor", None),
    )
    out_specs = (
        P(None, "expert", None),
        P(None, "expert", None),
        P("expert", "tensor"),
        P("expert", "tensor"),
        P("expert", "tensor"),
        P("tensor", "expert"),
        P("expert"),
        P("expert"),
        P("expert"),
        P("expert"),
        P("expert", None),
        P("expert", None, "tensor"),
        P("expert", None, "tensor"),
        P("expert", "tensor", None),
    )
    chips = mesh.shape["expert"] * mesh.shape["tensor"] // 2

    def whole(*arrays):
        heads, sequences = arrays[5].shape[1] // HD, arrays[0].shape[0]
        fits = heads == chips and sequences == 8 and mesh.shape["tensor"] == 4
        return jax.shard_map(
            on_device if fits else on_device_paired,
            mesh=mesh,
            in_specs=in_specs,
            out_specs=out_specs,
            check_vma=False,
        )(*arrays)

    return whole
```

```python
import functools
import math

import jax
import jax.numpy as jnp
from jax import lax
from jax.experimental import pallas as pl
from jax.experimental.pallas import tpu as pltpu
from jax.sharding import PartitionSpec as P

HD = 128
TOPK = 8


EPS = 1e-06
ROPE_BASE = 50000.0
NEG_FILL = -1e30


def norm_parts(values, gain):
    inverse = lax.rsqrt(jnp.mean(values * values, axis=-1, keepdims=True) + EPS)
    unit_rows = values * inverse
    return (unit_rows * gain, unit_rows, inverse)


def norm_back(grad_normed, gain, unit_rows, inverse):
    grad_unit = grad_normed * gain
    inner_mean = jnp.mean(grad_unit * unit_rows, axis=-1, keepdims=True)
    return inverse * (grad_unit - unit_rows * inner_mean)


def rope_tables(seq_count, width):
    halfway = width // 2
    frequency = jnp.power(ROPE_BASE, -jnp.arange(halfway, dtype=jnp.float32) * (2.0 / width))
    angles = jnp.arange(seq_count, dtype=jnp.float32)[:, None] * frequency[None, :]
    return (jnp.cos(angles)[:, None, :], jnp.sin(angles)[:, None, :])


def rotate(values, cos_table, sin_table):
    halfway = values.shape[-1] // 2
    former = values[..., :halfway]
    latter = values[..., halfway:]
    return jnp.concatenate(
        [former * cos_table - latter * sin_table, latter * cos_table + former * sin_table], axis=-1
    )


MESH = pl.DeviceIdType.MESH
UP, DOWN, ACROSS_X, ACROSS_Y, DIAG_X, DIAG_Y, PAIR = range(7)


def position():
    group, member = lax.axis_index("expert"), lax.axis_index("tensor")
    return lax.rem(group, 2), lax.div(member, 2), lax.div(group, 2), lax.rem(member, 2)


def device(x, y, z, c):
    return (z * 2 + x, y * 2 + c)


def greet(line, extra=0):
    x, y, z, c = position()
    barrier = pltpu.get_barrier_semaphore()

    def signal(to):
        pl.semaphore_signal(barrier, inc=1, device_id=to, device_id_type=MESH)

    signal(device(1 - x, y, z, c))
    signal(device(x, 1 - y, z, c))
    signal(device(x, y, z, 1 - c))
    pl.when(z > 0)(lambda: signal(device(x, y, z - 1, c)))
    pl.when(z < line - 1)(lambda: signal(device(x, y, z + 1, c)))
    near = 3 + (z > 0).astype(jnp.int32) + (z < line - 1).astype(jnp.int32)
    pl.semaphore_wait(barrier, near + extra)


def gather_steps(line, pair, ins, outs, send, recv, local, between=None, fill=None):
    x, y, z, c = position()
    count = len(ins)
    deep = ins[0].shape[1]

    def place(i, xx, yy, zz, cc):
        if pair:
            return outs[i].at[(zz * 2 + xx) * 4 + yy * 2 + cc]
        return outs[i].at[pl.ds(2 * yy, 2), pl.ds((zz * 2 + xx) * deep, deep)]

    def copy(i, kind, block, to, own):
        slot = kind * line + block[2]
        return pltpu.make_async_remote_copy(
            src_ref=ins[i] if own else place(i, *block),
            dst_ref=place(i, *block),
            send_sem=send.at[i, slot],
            recv_sem=recv.at[i, slot],
            device_id=to,
            device_id_type=MESH,
        )

    x_side, y_side = device(1 - x, y, z, c), device(x, 1 - y, z, c)
    sibling = device(x, y, z, 1 - c)
    mine = (x, y, z, c)
    below, above = device(x, y, z - 1, c), device(x, y, z + 1, c)
    moves = [(0, 0)] + [(step, sign) for step in range(1, line) for sign in (-1, 1)]
    spots = {}
    for step, sign in moves:
        zz = z + sign * step
        valid = (zz >= 0) & (zz < line)
        even = ((zz + 2 * line) & 1) == 0
        spots[step, sign] = dict(
            zz=zz,
            valid=valid if step else None,
            up=valid & (z < line - 1),
            down=valid & (z > 0),
            even=valid & even,
            odd=valid & ~even,
        )
    sends = {}

    def push(kind, block, to, own=False, when=None):
        def act(what):
            for i in range(count):
                getattr(copy(i, kind, block, to, own), what)()

        sends[kind, id(block[2])] = act, when
        guarded(when, functools.partial(act, "start"))

    def guarded(when, go):
        if when is None:
            go()
        else:
            pl.when(when)(go)

    def arrive(kind, block, frm):
        for i in range(count):
            copy(i, kind, block, frm, False).wait_recv()

    push(UP, mine, above, True, spots[0, 0]["up"])
    push(DOWN, mine, below, True, spots[0, 0]["down"])
    push(ACROSS_X, mine, x_side, True)
    push(ACROSS_Y, mine, y_side, True)
    if pair:
        push(PAIR, mine, sibling, True)
    homes = [pltpu.make_async_copy(ins[i], place(i, *mine), local.at[i]) for i in range(count)]
    for home in homes:
        home.start()
    if between is not None:
        between()

    def take_step(step):
        signs = (0,) if step == 0 else (-1, 1)
        for sign in signs:
            spot = spots[step, sign]
            valid, block = spot["valid"], (x, y, spot["zz"], c)
            if step > 0:
                kind, frm = (UP, below) if sign < 0 else (DOWN, above)
                guarded(valid, functools.partial(arrive, kind, block, frm))
                if sign < 0:
                    push(UP, block, above, False, spot["up"])
                else:
                    push(DOWN, block, below, False, spot["down"])
                push(ACROSS_X, block, x_side, False, valid)
                push(ACROSS_Y, block, y_side, False, valid)
                if pair:
                    push(PAIR, block, sibling, False, valid)
        for sign in signs:
            spot = spots[step, sign]
            valid = spot["valid"]
            block = (1 - x, y, spot["zz"], c)
            guarded(valid, functools.partial(arrive, ACROSS_X, block, x_side))
            push(DIAG_Y, block, y_side, False, spot["odd"])
            if pair:
                push(PAIR + 1, block, sibling, False, valid)
            block = (x, 1 - y, spot["zz"], c)
            guarded(valid, functools.partial(arrive, ACROSS_Y, block, y_side))
            push(DIAG_X, block, x_side, False, spot["even"])
            if pair:
                push(PAIR + 2, block, sibling, False, valid)

    for step in range(line):
        if fill is not None:
            fill(step)
        take_step(step)
    other = (1 - x, 1 - y)
    for zz in range(line):
        block = (*other, zz, c)
        if zz % 2 == 0:
            arrive(DIAG_X, block, x_side)
        else:
            arrive(DIAG_Y, block, y_side)
        if pair:
            push(PAIR + 3, block, sibling)
    if pair:
        for zz in range(line):
            for way, (xx, yy) in enumerate(((x, y), (1 - x, y), (x, 1 - y), (1 - x, 1 - y))):
                arrive(PAIR + way, (xx, yy, zz, 1 - c), sibling)
    for home in homes:
        home.wait()
    for act, when in sends.values():
        guarded(when, functools.partial(act, "wait_send"))


def column(way):
    x, y, _, _ = position()
    over_x, over_y = way % 2, way // 2
    return x + over_x * (1 - 2 * x), y + over_y * (1 - 2 * y)


def reduce_steps(line, pair, parts, outs, scratches, between=None):
    work = [
        reduce_phases(line, pair, sequence_slab(part, pair, out.shape[1]), out, *scratch)
        for part, out, scratch in zip(parts, outs, scratches)
    ]
    for phase in ("halves", "corner", "across", "along", "drain"):
        for phases in work:
            phases[phase]()
        if phase == "corner" and between is not None:
            between()


def sequence_slab(part, pair, deep):
    def slab(xx, yy, zz, cc):
        first = 2 * yy + (4 * cc if pair else 0)
        return part.at[pl.ds(first, 2), pl.ds((zz * 2 + xx) * deep, deep)]

    return slab


def reduce_phases(line, pair, spot_of, out, diag, side_x, side_y, rise, fall, twin, send, recv):
    x, y, z, c = position()
    deep = out.shape[1]
    x_side, y_side = device(1 - x, y, z, c), device(x, 1 - y, z, c)
    sibling = device(x, y, z, 1 - c)
    below, above = device(x, y, z - 1, c), device(x, y, z + 1, c)

    def slab(way, zz, cc):
        return spot_of(*column(way), zz, cc)

    def copy(kind, zz, src, dst, to):
        return pltpu.make_async_remote_copy(
            src_ref=src,
            dst_ref=dst.at[zz],
            send_sem=send.at[kind * line + zz],
            recv_sem=recv.at[kind * line + zz],
            device_id=to,
            device_id_type=MESH,
        )

    def push(kind, zz, src, dst, to):
        copy(kind, zz, src, dst, to).start()

    def landed(kind, zz, dst, frm):
        copy(kind, zz, dst.at[zz], dst, frm).wait_recv()

    def total(target, *terms):
        def some(n, carry):
            k, r = lax.div(n, deep // 16), pl.multiple_of(lax.rem(n, deep // 16) * 16, 16)
            value = terms[0][k, pl.ds(r, 16)].astype(jnp.float32)
            for term in terms[1:]:
                value = value + term[k, pl.ds(r, 16)].astype(jnp.float32)
            target[k, pl.ds(r, 16)] = value.astype(target.dtype)
            return carry

        lax.fori_loop(0, 2 * (deep // 16), some, 0)

    def base(way, zz):
        return twin.at[way, zz] if pair else slab(way, zz, c)

    def paired(way, zz):
        if pair:
            spot = twin.at[way]
            landed(PAIR + way, zz, spot, sibling)
            total(spot.at[zz], slab(way, zz, c), spot.at[zz])

    def half(way, zz):
        push(PAIR + way, zz, slab(way, zz, 1 - c), twin.at[way], sibling)

    def halves():
        if pair:
            for way in (3, 1, 2, 0):
                for zz in range(line):
                    half(way, zz)

    def corner_of(zz):
        paired(3, zz)
        pl.when(lax.rem(zz, 2) == 0)(lambda: push(DIAG_X, zz, base(3, zz), diag, x_side))
        pl.when(lax.rem(zz, 2) == 1)(lambda: push(DIAG_Y, zz, base(3, zz), diag, y_side))

    def corner():
        for zz in range(line):
            corner_of(jnp.int32(zz))

    def direct(way, zz):
        paired(way, zz)
        if way == 1:
            pl.when(lax.rem(zz, 2) == 0)(lambda: push(ACROSS_X, zz, base(1, zz), side_x, x_side))
        else:
            pl.when(lax.rem(zz, 2) == 1)(lambda: push(ACROSS_Y, zz, base(2, zz), side_y, y_side))

    def dependent(zz):
        @pl.when(lax.rem(zz, 2) == 0)
        def _():
            landed(DIAG_X, zz, diag, x_side)
            total(diag.at[zz], base(2, zz), diag.at[zz])
            push(ACROSS_Y, zz, diag.at[zz], side_y, y_side)

        @pl.when(lax.rem(zz, 2) == 1)
        def _():
            landed(DIAG_Y, zz, diag, y_side)
            total(diag.at[zz], base(1, zz), diag.at[zz])
            push(ACROSS_X, zz, diag.at[zz], side_x, x_side)

    def order(body):
        for step in range(line - 1, -1, -1):
            for sign in (0,) if step == 0 else (-1, 1):
                zz = z + sign * step
                go = functools.partial(body, zz, sign)
                if step == 0:
                    go()
                else:
                    pl.when((zz >= 0) & (zz < line))(go)

    def across(zz, sign):
        direct(1, zz)
        direct(2, zz)
        dependent(zz)

    def along(zz, sign):
        paired(0, zz)
        landed(ACROSS_X, zz, side_x, x_side)
        landed(ACROSS_Y, zz, side_y, y_side)
        spot = out if sign == 0 else side_x.at[zz]
        near = (base(0, zz), side_x.at[zz], side_y.at[zz])
        if sign > 0:
            @pl.when(z > 0)
            def _():
                landed(UP, zz, rise, below)
                total(spot, *near, rise.at[zz])

            @pl.when(z == 0)
            def _():
                total(spot, *near)

            push(UP, zz, spot, rise, above)
        elif sign < 0:
            @pl.when(z < line - 1)
            def _():
                landed(DOWN, zz, fall, above)
                total(spot, *near, fall.at[zz])

            @pl.when(z == line - 1)
            def _():
                total(spot, *near)

            push(DOWN, zz, spot, fall, below)
        else:
            @pl.when((z > 0) & (z < line - 1))
            def _():
                landed(UP, zz, rise, below)
                landed(DOWN, zz, fall, above)
                total(spot, *near, rise.at[zz], fall.at[zz])

            @pl.when(z == 0)
            def _():
                landed(DOWN, zz, fall, above)
                total(spot, *near, fall.at[zz])

            @pl.when(z == line - 1)
            def _():
                landed(UP, zz, rise, below)
                total(spot, *near, rise.at[zz])

    def sent(kind, zz, dst, to):
        copy(kind, zz, dst.at[zz], dst, to).wait_send()

    def drain():
        for zz in range(line):
            leave(zz)

    def leave(zz):
        if pair:
            for way in range(4):
                sent(PAIR + way, zz, twin.at[way], sibling)
        sent(DIAG_X if zz % 2 == 0 else DIAG_Y, zz, diag, x_side if zz % 2 == 0 else y_side)
        sent(ACROSS_X, zz, side_x, x_side)
        sent(ACROSS_Y, zz, side_y, y_side)
        pl.when(zz > z)(functools.partial(sent, UP, zz, rise, above))
        pl.when(zz < z)(functools.partial(sent, DOWN, zz, fall, below))

    return dict(
        half=half,
        halves=halves,
        corner_of=corner_of,
        corner=corner,
        direct=direct,
        dependent=dependent,
        across=functools.partial(order, across),
        along=functools.partial(order, along),
        along_of=along,
        drain=drain,
    )


def reduce_kernel(line, pair, count, *refs):
    parts, outs, rest = refs[:count], refs[count : 2 * count], refs[2 * count :]
    greet(line)
    reduce_steps(line, pair, parts, outs, [rest[8 * i : 8 * i + 8] for i in range(count)])


def reduce_scratch(line, pair, deep, width, dtype):
    kinds = PAIR + (4 if pair else 0)
    block = (line, 2, deep, width)
    return [pltpu.VMEM(block, dtype)] * 5 + [
        pltpu.VMEM((4,) + block if pair else (8, 128), dtype),
        pltpu.SemaphoreType.DMA((kinds * line,)),
        pltpu.SemaphoreType.DMA((kinds * line,)),
    ]


def reduce_rows(parts, line, pair, collective_id):
    count, deep = len(parts), parts[0].shape[1] // (2 * line)
    scratch = []
    for part in parts:
        scratch += reduce_scratch(line, pair, deep, part.shape[2], part.dtype)
    return pl.pallas_call(
        functools.partial(reduce_kernel, line, pair, count),
        out_shape=[jax.ShapeDtypeStruct((2, deep, part.shape[2]), jnp.float32) for part in parts],
        in_specs=[pl.BlockSpec(memory_space=pltpu.VMEM)] * count,
        out_specs=[pl.BlockSpec(memory_space=pltpu.VMEM)] * count,
        scratch_shapes=scratch,
        compiler_params=pltpu.CompilerParams(
            collective_id=collective_id, has_side_effects=True, vmem_limit_bytes=60 << 20
        ),
    )(*parts)


def gathered_with_weights(line, rows, cut, proj_cut, small, *rest):
    all_rows, head_weight, head_proj, all_small, send, recv, local, wsend, wrecv, wlocal = rest
    x, y, z, c = position()
    group, groups = lax.axis_index("expert"), 2 * line
    member = lax.axis_index("tensor")
    deep, wide = cut.shape[1], proj_cut.shape[2]
    parts = cut.shape[0]
    sibling = device(x, y, z, 1 - c)
    barrier = pltpu.get_barrier_semaphore()
    for hop in range(1, groups):
        pl.semaphore_signal(
            barrier, inc=1, device_id=(lax.rem(group + hop, groups), member), device_id_type=MESH
        )
    pl.semaphore_signal(barrier, inc=1, device_id=sibling, device_id_type=MESH)
    pl.semaphore_signal(barrier, inc=1, device_id=device(x, 1 - y, z, c), device_id_type=MESH)
    pl.semaphore_wait(barrier, groups + 1)
    serves = lax.div(group, parts) == c

    def spots(origin):
        return (
            head_weight.at[pl.ds(origin * deep, deep)],
            head_proj.at[:, pl.ds(origin * wide, wide)],
        )

    def weight_copies(origin, sources, to, slot):
        return [
            pltpu.make_async_remote_copy(
                src_ref=source,
                dst_ref=spot,
                send_sem=wsend.at[which, slot],
                recv_sem=wrecv.at[which, origin],
                device_id=to,
                device_id_type=MESH,
            )
            for which, (source, spot) in enumerate(zip(sources, spots(origin)))
        ]

    def small_copy(origin, to, slot):
        return pltpu.make_async_remote_copy(
            src_ref=small,
            dst_ref=all_small.at[:, pl.ds(origin * small.shape[1], small.shape[1])],
            send_sem=wsend.at[2, slot],
            recv_sem=wrecv.at[2, origin],
            device_id=to,
            device_id_type=MESH,
        )

    def outgoing(n):
        return weight_copies(group, (cut.at[n], proj_cut.at[n]), (c * parts + n, member), n)

    own = lax.rem(group, parts)
    home = [
        pltpu.make_async_copy(source, spot, wlocal.at[which])
        for which, (source, spot) in enumerate(zip((cut.at[own], proj_cut.at[own]), spots(group)))
    ]
    small_home = pltpu.make_async_copy(
        small, all_small.at[:, pl.ds(group * small.shape[1], small.shape[1])], wlocal.at[2]
    )
    own_to_sibling = weight_copies(group, (cut.at[own], proj_cut.at[own]), sibling, parts)

    def everything(copies, act):
        for one in copies:
            getattr(one, act)()

    def begin():
        small_home.start()
        for hop in range(1, groups):
            small_copy(group, (lax.rem(group + hop, groups), member), hop).start()
        for n in range(parts):
            pl.when(c * parts + n != group)(functools.partial(everything, outgoing(n), "start"))

        @pl.when(serves)
        def _():
            everything(home, "start")
            everything(own_to_sibling, "start")

    gather_steps(line, False, (rows,), (all_rows,), send, recv, local, begin)
    for hop in range(1, groups):
        origin = lax.rem(group + hop, groups)
        copies = weight_copies(origin, spots(origin), sibling, parts + hop)
        everything(copies, "wait_recv")
        pl.when(serves)(functools.partial(everything, copies, "start"))
    pl.when(~serves)(functools.partial(everything, own_to_sibling, "wait_recv"))
    for hop in range(1, groups):
        small_copy(lax.rem(group + hop, groups), sibling, hop).wait_recv()
    small_home.wait()
    for n in range(parts):
        pl.when(c * parts + n != group)(functools.partial(everything, outgoing(n), "wait_send"))
    for hop in range(1, groups):
        small_copy(group, (lax.rem(group + hop, groups), member), hop).wait_send()

    @pl.when(serves)
    def _():
        everything(home, "wait")
        everything(own_to_sibling, "wait_send")
        for hop in range(1, groups):
            origin = lax.rem(group + hop, groups)
            everything(weight_copies(origin, spots(origin), sibling, parts + hop), "wait_send")


def gather_with_weights(rows, cut, proj_cut, small, line, collective_id):
    groups = 2 * line
    vmem = pl.BlockSpec(memory_space=pltpu.VMEM)
    anywhere = pl.BlockSpec(memory_space=pl.ANY)
    slots = cut.shape[0] + groups
    return pl.pallas_call(
        functools.partial(gathered_with_weights, line),
        out_shape=[
            jax.ShapeDtypeStruct((4, rows.shape[1] * groups, rows.shape[2]), rows.dtype),
            jax.ShapeDtypeStruct((groups * cut.shape[1], cut.shape[2]), cut.dtype),
            jax.ShapeDtypeStruct((proj_cut.shape[1], groups * proj_cut.shape[2]), cut.dtype),
            jax.ShapeDtypeStruct((small.shape[0], groups * small.shape[1]), small.dtype),
        ],
        in_specs=[vmem] * 4,
        out_specs=[anywhere] * 4,
        scratch_shapes=[
            pltpu.SemaphoreType.DMA((1, PAIR * line)),
            pltpu.SemaphoreType.DMA((1, PAIR * line)),
            pltpu.SemaphoreType.DMA((1,)),
            pltpu.SemaphoreType.DMA((3, slots)),
            pltpu.SemaphoreType.DMA((3, groups)),
            pltpu.SemaphoreType.DMA((3,)),
        ],
        compiler_params=pltpu.CompilerParams(collective_id=collective_id, has_side_effects=True),
    )(rows, cut, proj_cut, small)


def spread_copies(own, full, send, recv):
    x, y, z, c = position()
    y_side, sibling = device(x, 1 - y, z, c), device(x, y, z, 1 - c)

    def spot(yy, cc):
        return full.at[pl.ds(4 * cc + 2 * yy, 2)]

    def copy(slot, source, yy, to):
        return pltpu.make_async_remote_copy(
            src_ref=source,
            dst_ref=spot(yy, c),
            send_sem=send.at[slot],
            recv_sem=recv.at[slot],
            device_id=to,
            device_id_type=MESH,
        )

    def incoming(slot, yy, cc, frm):
        return pltpu.make_async_remote_copy(
            src_ref=spot(yy, cc),
            dst_ref=spot(yy, cc),
            send_sem=send.at[slot],
            recv_sem=recv.at[slot],
            device_id=frm,
            device_id_type=MESH,
        )

    first = [copy(0, own, y, y_side), copy(1, own, y, sibling)]
    onward = copy(2, spot(1 - y, c), 1 - y, sibling)
    home = pltpu.make_async_copy(own, spot(y, c), send.at[3])

    def begin():
        home.start()
        for one in first:
            one.start()

    def finish():
        incoming(0, 1 - y, c, y_side).wait_recv()
        onward.start()
        incoming(1, y, 1 - c, sibling).wait_recv()
        incoming(2, 1 - y, 1 - c, sibling).wait_recv()
        home.wait()
        for one in first + [onward]:
            one.wait_send()

    return begin, finish


def weight_gradients(rows, grads, pre, gated, gate_o, up_o, down_o, *scratch):
    row_buf, grad_buf, pre_buf, gated_buf, gate_buf, up_buf, down_buf, load, once, store = scratch
    tile = row_buf.shape[2]
    tiles = rows.shape[1] // tile
    experts, _, wide = gate_o.shape

    def act(copies, what):
        for one in copies:
            getattr(one, what)()

    def loads(n, slot):
        return [
            pltpu.make_async_copy(
                source.at[:, pl.ds(n * tile, tile)], target.at[slot], load.at[slot, which]
            )
            for which, (source, target) in enumerate(((rows, row_buf), (grads, grad_buf)))
        ]

    def stores(n, slot):
        return [
            pltpu.make_async_copy(source.at[slot], target, store.at[slot, which])
            for which, (source, target) in enumerate(
                (
                    (gate_buf, gate_o.at[:, pl.ds(n * tile, tile)]),
                    (up_buf, up_o.at[:, pl.ds(n * tile, tile)]),
                    (down_buf, down_o.at[:, :, pl.ds(n * tile, tile)]),
                )
            )
        ]

    whole = [
        pltpu.make_async_copy(pre, pre_buf, once.at[0]),
        pltpu.make_async_copy(gated, gated_buf, once.at[1]),
    ]

    def begin():
        act(loads(0, 0), "start")
        act(whole, "start")

    def one(n):
        slot = lax.rem(n, 2)
        pl.when(n == 0)(functools.partial(act, whole, "wait"))
        pl.when(n + 1 < tiles)(lambda: act(loads(n + 1, 1 - slot), "start"))
        act(loads(n, slot), "wait")
        pl.when(n >= 2)(lambda: act(stores(n - 2, slot), "wait"))
        product = dot(row_buf[slot], pre_buf[...], ((0,), (0,)))
        for e in range(experts):
            gate_buf[slot, e] = product[:, e * wide : (e + 1) * wide]
            up_buf[slot, e] = product[:, (experts + e) * wide : (experts + e + 1) * wide]
        product = dot(gated_buf[...], grad_buf[slot], ((0,), (0,)))
        down_buf[slot] = product.reshape(experts, wide, tile)
        act(stores(n, slot), "start")

    def finish():
        for n in (tiles - 2, tiles - 1):
            act(stores(n, n % 2), "wait")

    return tiles, begin, one, finish


def gathered_and_spread(line, rows, own, *refs):
    operands, (all_rows, full), grads_o, rest = refs[:4], refs[4:6], refs[6:9], refs[9:]
    (send, recv, local, ssend, srecv), scratch = rest[:5], rest[5:]
    tiles, start, one, end = weight_gradients(*operands, *grads_o, *scratch)
    start()
    greet(line)
    begin, finish = spread_copies(own, full, ssend, srecv)
    each = tiles // line

    def fill(i):
        def some(n, carry):
            one(i * each + n)
            return carry

        lax.fori_loop(0, each, some, 0)

    gather_steps(line, False, (rows,), (all_rows,), send, recv, local, begin, fill)
    finish()
    end()


def gather_and_spread(rows, own, operands, shapes, line, collective_id):
    groups, tile = 2 * line, 256
    tokens, both = operands[2].shape
    hidden = operands[3].shape[1]
    experts, _, wide = shapes[0]
    kind = operands[0].dtype
    vmem, anywhere = pl.BlockSpec(memory_space=pltpu.VMEM), pl.BlockSpec(memory_space=pl.ANY)
    return pl.pallas_call(
        functools.partial(gathered_and_spread, line),
        out_shape=[
            jax.ShapeDtypeStruct((4, rows.shape[1] * groups, rows.shape[2]), rows.dtype),
            jax.ShapeDtypeStruct((8,) + own.shape[1:], own.dtype),
        ]
        + [jax.ShapeDtypeStruct(shape, jnp.float32) for shape in shapes],
        in_specs=[vmem] * 2 + [anywhere] * 4,
        out_specs=[anywhere] * 5,
        scratch_shapes=[
            pltpu.SemaphoreType.DMA((1, PAIR * line)),
            pltpu.SemaphoreType.DMA((1, PAIR * line)),
            pltpu.SemaphoreType.DMA((1,)),
            pltpu.SemaphoreType.DMA((4,)),
            pltpu.SemaphoreType.DMA((4,)),
            pltpu.VMEM((2, tokens, tile), kind),
            pltpu.VMEM((2, tokens, tile), kind),
            pltpu.VMEM((tokens, both), kind),
            pltpu.VMEM((tokens, hidden), kind),
            pltpu.VMEM((2, experts, tile, wide), jnp.float32),
            pltpu.VMEM((2, experts, tile, wide), jnp.float32),
            pltpu.VMEM((2, experts, wide, tile), jnp.float32),
            pltpu.SemaphoreType.DMA((2, 2)),
            pltpu.SemaphoreType.DMA((2,)),
            pltpu.SemaphoreType.DMA((2, 3)),
        ],
        compiler_params=pltpu.CompilerParams(
            collective_id=collective_id, has_side_effects=True, vmem_limit_bytes=60 << 20
        ),
    )(rows, own, *operands)


def gathered_with_casts(line, count, *refs):
    ins, masters = refs[:count], refs[count : count + 3]
    outs, (both, down) = refs[count + 3 : 2 * count + 3], refs[2 * count + 3 : 2 * count + 5]
    send, recv, local, gate_buf, up_buf, down_buf, load = refs[2 * count + 5 :]
    experts, width, wide = gate_buf.shape
    tile, down_tile = width // line, experts * wide // line
    per_expert = wide // down_tile

    def loads(i):
        spot = (i // per_expert, pl.ds((i % per_expert) * down_tile, down_tile))
        return [
            pltpu.make_async_copy(source.at[where], target.at[where], load.at[which, i])
            for which, (source, target, where) in enumerate(
                (
                    (masters[0], gate_buf, (slice(None), pl.ds(i * tile, tile))),
                    (masters[1], up_buf, (slice(None), pl.ds(i * tile, tile))),
                    (masters[2], down_buf, spot),
                )
            )
        ]

    for i in range(line):
        for one in loads(i):
            one.start()
    greet(line)

    def fill(i):
        for one in loads(i):
            one.wait()
        here = pl.ds(i * tile, tile)
        for e in range(experts):
            both[here, e * wide : (e + 1) * wide] = gate_buf[e, here].astype(both.dtype)
            both[here, (experts + e) * wide : (experts + e + 1) * wide] = up_buf[e, here].astype(
                both.dtype
            )
        start = (i % per_expert) * down_tile
        down[pl.ds(i * down_tile, down_tile)] = down_buf[
            i // per_expert, pl.ds(start, down_tile)
        ].astype(down.dtype)

    gather_steps(line, True, ins, outs, send, recv, local, None, fill)


def gather_with_casts(arrays, masters, line, collective_id):
    count, kinds = len(arrays), PAIR + 4
    experts, width, wide = masters[0].shape
    vmem, anywhere = pl.BlockSpec(memory_space=pltpu.VMEM), pl.BlockSpec(memory_space=pl.ANY)
    return pl.pallas_call(
        functools.partial(gathered_with_casts, line, count),
        out_shape=[jax.ShapeDtypeStruct((line * 8,) + a.shape, a.dtype) for a in arrays]
        + [
            jax.ShapeDtypeStruct((width, 2 * experts * wide), jnp.bfloat16),
            jax.ShapeDtypeStruct((experts * wide, width), jnp.bfloat16),
        ],
        in_specs=[vmem] * count + [anywhere] * 3,
        out_specs=[anywhere] * count + [vmem] * 2,
        scratch_shapes=[
            pltpu.SemaphoreType.DMA((count, kinds * line)),
            pltpu.SemaphoreType.DMA((count, kinds * line)),
            pltpu.SemaphoreType.DMA((count,)),
            pltpu.VMEM((experts, width, wide), jnp.float32),
            pltpu.VMEM((experts, width, wide), jnp.float32),
            pltpu.VMEM((experts, wide, width), jnp.float32),
            pltpu.SemaphoreType.DMA((3, line)),
        ],
        compiler_params=pltpu.CompilerParams(
            collective_id=collective_id, has_side_effects=True, vmem_limit_bytes=60 << 20
        ),
    )(*arrays, *masters)


def reduced_with_weights(line, part, grad, proj_grad, out, cuts, proj_cuts, *rest):
    scratch, (other, proj_other, wsend, wrecv, wlocal) = rest[:8], rest[8:]
    x, y, z, c = position()
    group = lax.axis_index("expert")
    parts = cuts.shape[0]
    deep, wide = cuts.shape[1], proj_cuts.shape[2]
    sibling = device(x, y, z, 1 - c)
    side = lax.div(group, parts)
    barrier = pltpu.get_barrier_semaphore()
    for n in range(parts):
        peer = c * parts + n

        @pl.when((peer != group) | (side != c))
        def _():
            pl.semaphore_signal(
                barrier, inc=1, device_id=(peer, y * 2 + side), device_id_type=MESH
            )

    greet(line, parts - (side == c).astype(jnp.int32))
    half, proj_half = parts * deep, parts * wide
    to_sibling = [
        pltpu.make_async_remote_copy(
            src_ref=source,
            dst_ref=target,
            send_sem=wsend.at[which, parts],
            recv_sem=wrecv.at[which, parts],
            device_id=sibling,
            device_id_type=MESH,
        )
        for which, (source, target) in enumerate(
            (
                (grad.at[pl.ds((1 - c) * half, half)], other),
                (proj_grad.at[:, pl.ds((1 - c) * proj_half, proj_half)], proj_other),
            )
        )
    ]
    for one in to_sibling:
        one.start()

    def outgoing(n):
        return [
            pltpu.make_async_remote_copy(
                src_ref=source,
                dst_ref=target.at[lax.rem(group, parts)],
                send_sem=wsend.at[which, n],
                recv_sem=wrecv.at[which, lax.rem(group, parts)],
                device_id=(c * parts + n, y * 2 + side),
                device_id_type=MESH,
            )
            for which, (source, target) in enumerate(
                (
                    (other.at[pl.ds(n * deep, deep)], cuts),
                    (proj_other.at[:, pl.ds(n * wide, wide)], proj_cuts),
                )
            )
        ]

    def incoming(n):
        return [
            pltpu.make_async_remote_copy(
                src_ref=target.at[n],
                dst_ref=target.at[n],
                send_sem=wsend.at[which, n],
                recv_sem=wrecv.at[which, n],
                device_id=(c * parts + n, y * 2 + side),
                device_id_type=MESH,
            )
            for which, target in enumerate((cuts, proj_cuts))
        ]

    own = lax.rem(group, parts)
    home = [
        pltpu.make_async_copy(source, target, wlocal.at[which])
        for which, (source, target) in enumerate(
            (
                (other.at[pl.ds(own * deep, deep)], cuts.at[own]),
                (proj_other.at[:, pl.ds(own * wide, wide)], proj_cuts.at[own]),
            )
        )
    ]

    def remote(n):
        return (c * parts + n != group) | (side != c)

    def between():
        for one in to_sibling:
            one.wait_recv()

        def add(n, carry):
            r = pl.multiple_of(n * 16, 16)
            other[pl.ds(r, 16)] = (
                other[pl.ds(r, 16)].astype(jnp.float32)
                + grad[pl.ds(pl.multiple_of(c * half + n * 16, 16), 16)].astype(jnp.float32)
            ).astype(other.dtype)
            return carry

        lax.fori_loop(0, half // 16, add, 0)

        def add_proj(n, carry):
            r = pl.multiple_of(n * 16, 16)
            mine = proj_grad[pl.ds(r, 16), pl.ds(pl.multiple_of(c * proj_half, 128), proj_half)]
            proj_other[pl.ds(r, 16)] = (
                proj_other[pl.ds(r, 16)].astype(jnp.float32) + mine.astype(jnp.float32)
            ).astype(other.dtype)
            return carry

        lax.fori_loop(0, proj_other.shape[0] // 16, add_proj, 0)

        for n in range(parts):
            @pl.when(remote(n))
            def _():
                for one in outgoing(n):
                    one.start()

        @pl.when(side == c)
        def _():
            for one in home:
                one.start()

    reduce_steps(line, False, (part,), (out,), (scratch,), between)
    for n in range(parts):
        @pl.when(remote(n))
        def _():
            for one in incoming(n):
                one.wait_recv()
            for one in outgoing(n):
                one.wait_send()

    for one in to_sibling:
        one.wait_send()

    @pl.when(side == c)
    def _():
        for one in home:
            one.wait()


def reduce_with_weights(part, grad, proj_grad, line, collective_id):
    groups, parts = 2 * line, line
    deep, width = part.shape[1] // groups, part.shape[2]
    vmem = pl.BlockSpec(memory_space=pltpu.VMEM)
    cut = (parts, grad.shape[0] // groups, grad.shape[1])
    proj_cut = (parts, proj_grad.shape[0], proj_grad.shape[1] // groups)
    return pl.pallas_call(
        functools.partial(reduced_with_weights, line),
        out_shape=[
            jax.ShapeDtypeStruct((2, deep, width), jnp.float32),
            jax.ShapeDtypeStruct(cut, grad.dtype),
            jax.ShapeDtypeStruct(proj_cut, grad.dtype),
        ],
        in_specs=[vmem] * 3,
        out_specs=[vmem] * 3,
        scratch_shapes=reduce_scratch(line, False, deep, width, part.dtype)
        + [
            pltpu.VMEM((grad.shape[0] // 2, grad.shape[1]), grad.dtype),
            pltpu.VMEM((proj_grad.shape[0], proj_grad.shape[1] // 2), grad.dtype),
            pltpu.SemaphoreType.DMA((2, parts + 1)),
            pltpu.SemaphoreType.DMA((2, parts + 1)),
            pltpu.SemaphoreType.DMA((2,)),
        ],
        compiler_params=pltpu.CompilerParams(
            collective_id=collective_id, has_side_effects=True, vmem_limit_bytes=60 << 20
        ),
    )(part, grad, proj_grad)


def finished(line, own, small, full, total, ssend, srecv, held, tensor_held, send, recv):
    x, y, z, c = position()
    group, groups, member = lax.axis_index("expert"), 2 * line, lax.axis_index("tensor")
    barrier = pltpu.get_barrier_semaphore()
    for hop in range(1, groups):
        pl.semaphore_signal(
            barrier, inc=1, device_id=(lax.rem(group + hop, groups), member), device_id_type=MESH
        )
    for hop in range(1, 4):
        pl.semaphore_signal(
            barrier, inc=1, device_id=(group, lax.rem(member + hop, 4)), device_id_type=MESH
        )
    pl.semaphore_wait(barrier, groups + 2)
    wide = total.shape[1]

    def outgoing(hop):
        to = lax.rem(group + hop, groups)
        return pltpu.make_async_remote_copy(
            src_ref=small.at[:, pl.ds(to * wide, wide)],
            dst_ref=held.at[hop],
            send_sem=send.at[hop],
            recv_sem=recv.at[hop],
            device_id=(to, member),
            device_id_type=MESH,
        )

    def onward(hop):
        return pltpu.make_async_remote_copy(
            src_ref=held.at[0],
            dst_ref=tensor_held.at[hop],
            send_sem=send.at[groups + hop],
            recv_sem=recv.at[groups + hop],
            device_id=(group, lax.rem(member + hop, 4)),
            device_id_type=MESH,
        )

    for hop in range(1, groups):
        outgoing(hop).start()
    begin, finish = spread_copies(own, full, ssend, srecv)
    begin()
    value = small[:, pl.ds(pl.multiple_of(group * wide, 128), wide)]
    for hop in range(1, groups):
        outgoing(hop).wait_recv()
        value = value + held[hop]
    held[0] = value
    for hop in range(1, 4):
        onward(hop).start()
    finish()
    for hop in range(1, 4):
        onward(hop).wait_recv()
        value = value + tensor_held[hop]
    total[...] = value
    for hop in range(1, groups):
        outgoing(hop).wait_send()
    for hop in range(1, 4):
        onward(hop).wait_send()


def finish_rows(own, small, line, collective_id):
    groups = 2 * line
    vmem = pl.BlockSpec(memory_space=pltpu.VMEM)
    wide = small.shape[1] // groups
    return pl.pallas_call(
        functools.partial(finished, line),
        out_shape=[
            jax.ShapeDtypeStruct((8,) + own.shape[1:], own.dtype),
            jax.ShapeDtypeStruct((small.shape[0], wide), jnp.float32),
        ],
        in_specs=[vmem] * 2,
        out_specs=[vmem] * 2,
        scratch_shapes=[
            pltpu.SemaphoreType.DMA((4,)),
            pltpu.SemaphoreType.DMA((4,)),
            pltpu.VMEM((groups, small.shape[0], wide), jnp.float32),
            pltpu.VMEM((4, small.shape[0], wide), jnp.float32),
            pltpu.SemaphoreType.DMA((groups + 4,)),
            pltpu.SemaphoreType.DMA((groups + 4,)),
        ],
        compiler_params=pltpu.CompilerParams(collective_id=collective_id, has_side_effects=True),
    )(own, small)


def experts_and_sums(
    line, experts, rows, grads, gates, both, down, out, row_grad, gated_o, pre_o, *rest
):
    works, rest = [rest[8 * i : 8 * i + 8] for i in range(2)], rest[16:]
    part_out, part_rows, row_buf, grad_buf, gate_buf, gated_buf, pre_buf, load, store = rest
    x, y, z, c = position()
    group = lax.axis_index("expert")
    deep, width = rows.shape[2], rows.shape[3]
    hidden = down.shape[0]
    block = 2 * deep
    greet(line)

    def blocks_of(part):
        return lambda xx, yy, zz, cc: part.at[(zz * 2 + xx) * 4 + yy * 2 + cc]

    sums = [
        reduce_phases(line, True, blocks_of(part), target, *work)
        for part, target, work in zip((part_out, part_rows), (out, row_grad), works)
    ]
    steps = 4 * line // 2

    def chips(step):
        turn = lax.rem(step, 4)
        way = jnp.where(turn == 0, 3, jnp.where(turn == 3, 0, turn))
        return way, pair_of(lax.div(step, 4))

    def pair_of(number):
        far = [2 * number + j for j in range(2)]
        return [jnp.where(2 * z < line, line - 1 - k, k) for k in far]

    def first_block(step, j):
        way, zs = chips(step)
        xx, yy = column(way)
        return (zs[j] * 2 + xx) * 4 + yy * 2

    def loads(step, slot):
        return [
            pltpu.make_async_copy(
                source.at[pl.ds(first_block(step, j), 2)],
                target.at[slot, pl.ds(2 * j, 2)],
                load.at[slot, which, j],
            )
            for which, (source, target) in enumerate(
                ((rows, row_buf), (grads, grad_buf), (gates, gate_buf))
            )
            for j in range(2)
        ]

    def stores(step, slot):
        return [
            pltpu.make_async_copy(
                source.at[slot, pl.ds(2 * block * j, 2 * block)],
                target.at[pl.ds(first_block(step, j) * block, 2 * block)],
                store.at[slot, which, j],
            )
            for which, (source, target) in enumerate(((gated_buf, gated_o), (pre_buf, pre_o)))
            for j in range(2)
        ]

    def act(copies, what):
        for one in copies:
            getattr(one, what)()

    act(loads(0, 0), "start")
    experts_here = hidden // experts
    lane = lax.broadcasted_iota(jnp.int32, (4 * block, gates.shape[3]), 1)

    def body(step, carry):
        slot = lax.rem(step, 2)
        pl.when(step + 1 < steps)(lambda: act(loads(step + 1, 1 - slot), "start"))
        act(loads(step, slot), "wait")
        pl.when(step >= 2)(lambda: act(stores(step - 2, slot), "wait"))
        here = row_buf[slot].reshape(4 * block, width)
        grad_here = grad_buf[slot].reshape(4 * block, width)
        gate_here = gate_buf[slot].reshape(4 * block, gates.shape[3])
        pre = dot(here, both[...])
        plain = dot(grad_here, down[...], ((1,), (1,)))
        gate_term = jnp.zeros_like(gate_here)
        gated, grad_gate, grad_up = [], [], []
        for n in range(experts):
            mine = lane == group * experts + n
            gate = jnp.sum(jnp.where(mine, gate_here, 0.0), axis=-1, keepdims=True)
            gate_pre = pre[:, n * experts_here : (n + 1) * experts_here]
            up_pre = pre[:, hidden + n * experts_here : hidden + (n + 1) * experts_here]
            grad_plain = plain[:, n * experts_here : (n + 1) * experts_here]
            sigmoid = 1.0 / (1.0 + jnp.exp(-gate_pre))
            silu = gate_pre * sigmoid
            value = silu * up_pre
            sum_here = jnp.sum(value * grad_plain, axis=-1, keepdims=True)
            gate_term = jnp.where(mine, sum_here, gate_term)
            gated.append((gate * value).astype(jnp.bfloat16))
            grad_value = gate * grad_plain
            grad_gate.append(
                (grad_value * up_pre * sigmoid * (1.0 + gate_pre * (1.0 - sigmoid))).astype(
                    jnp.bfloat16
                )
            )
            grad_up.append((grad_value * silu).astype(jnp.bfloat16))
        gated_buf[slot] = jnp.concatenate(gated, axis=1)
        pre_buf[slot] = jnp.concatenate(grad_gate + grad_up, axis=1)
        act(stores(step, slot), "start")
        firsts = [first_block(step, j) for j in range(2)]

        def keep(part, value, n, tile):
            value = value.astype(part.dtype)
            for j in range(2):
                piece = value[2 * block * j : 2 * block * (j + 1)].reshape(2, 2, deep, tile)
                part[pl.ds(firsts[j], 2), :, :, n * tile : (n + 1) * tile] = piece

        tile = 512
        for n in range(width // tile):
            keep(part_out, dot(gated_buf[slot], down[:, n * tile : (n + 1) * tile]), n, tile)
        for n in range(width // tile):
            columns = both[n * tile : (n + 1) * tile]
            keep(part_rows, dot(pre_buf[slot], columns, ((1,), (1,))), n, tile)
        keep(part_rows, gate_term, width // gates.shape[3], gates.shape[3])
        way, zs = chips(step)
        for zz in zs:
            for one in sums:
                one["half"](way, zz)
        last_way, last = chips(step - 1)

        @pl.when((step > 0) & (last_way == 3))
        def _():
            for zz in last:
                for one in sums:
                    one["corner_of"](zz)

        for side in (1, 2):
            @pl.when((step > 0) & (last_way == side))
            def _():
                for zz in last:
                    for one in sums:
                        one["direct"](side, zz)

        @pl.when((step > 0) & (last_way == 0))
        def _():
            dependents(last)

        return carry

    def dependents(zs):
        for zz in zs:
            for one in sums:
                one["dependent"](zz)

    def along(zs):
        for zz in zs:
            for sign in (1, -1):
                @pl.when(sign * zz > sign * z)
                def _():
                    for one in sums:
                        one["along_of"](zz, sign)

    lax.fori_loop(0, steps, body, 0)
    for number in range(line // 2):
        if number == line // 2 - 1:
            dependents(pair_of(number))
        along(pair_of(number))
    for one in sums:
        one["along_of"](z, 0)
    for one in sums:
        one["drain"]()
    for step in (steps - 2, steps - 1):
        act(stores(step, step % 2), "wait")


def experts_to_rows(rows, grads, gates, both, down, experts, line, collective_id):
    count, _, deep, width = rows.shape
    lanes, hidden = gates.shape[3], down.shape[0]
    tokens, block = count * 2 * deep, 2 * deep
    vmem = pl.BlockSpec(memory_space=pltpu.VMEM)
    anywhere = pl.BlockSpec(memory_space=pl.ANY)
    scratch = []
    for wide in (width, width + lanes):
        scratch += reduce_scratch(line, True, deep, wide, rows.dtype)
    return pl.pallas_call(
        functools.partial(experts_and_sums, line, experts),
        out_shape=[
            jax.ShapeDtypeStruct((2, deep, width), jnp.float32),
            jax.ShapeDtypeStruct((2, deep, width + lanes), jnp.float32),
            jax.ShapeDtypeStruct((tokens, hidden), rows.dtype),
            jax.ShapeDtypeStruct((tokens, 2 * hidden), rows.dtype),
        ],
        in_specs=[anywhere] * 3 + [vmem] * 2,
        out_specs=[vmem] * 2 + [anywhere] * 2,
        scratch_shapes=scratch
        + [
            pltpu.VMEM((count, 2, deep, width), rows.dtype),
            pltpu.VMEM((count, 2, deep, width + lanes), rows.dtype),
            pltpu.VMEM((2, 4, 2, deep, width), rows.dtype),
            pltpu.VMEM((2, 4, 2, deep, width), rows.dtype),
            pltpu.VMEM((2, 4, 2, deep, lanes), gates.dtype),
            pltpu.VMEM((2, 4 * block, hidden), rows.dtype),
            pltpu.VMEM((2, 4 * block, 2 * hidden), rows.dtype),
            pltpu.SemaphoreType.DMA((2, 3, 2)),
            pltpu.SemaphoreType.DMA((2, 2, 2)),
        ],
        compiler_params=pltpu.CompilerParams(
            collective_id=collective_id, has_side_effects=True, vmem_limit_bytes=67043328
        ),
    )(rows, grads, gates, both, down)


def dot(left, right, over=((1,), (0,))):
    return lax.dot_general(left, right, (over, ((), ())), preferred_element_type=jnp.float32)


def on_device(
    inputs,
    cotangent,
    lengths,
    permutation,
    routes,
    query_weight,
    key_weight,
    value_weight,
    proj_weight,
    first_gain,
    second_gain,
    query_gain,
    key_gain,
    router_weight,
    gate_weight,
    up_weight,
    down_weight,
):
    sequences, deep, model_width = inputs.shape
    groups = lax.axis_size("expert")
    line = groups // 2
    rows = deep * groups
    expert_count = router_weight.shape[1]
    local_experts, _, hidden_width = gate_weight.shape
    group, member = lax.axis_index("expert"), lax.axis_index("tensor")
    y, c = member // 2, member % 2
    first_own = 4 * c + 2 * y
    low = jnp.bfloat16
    score_scale = math.sqrt(HD)

    own_in = lax.dynamic_slice_in_dim(inputs, first_own, 2)
    own_cot = lax.dynamic_slice_in_dim(cotangent, first_own, 2)
    cut = (
        jnp.stack([query_weight, key_weight, value_weight], axis=0)
        .astype(low)
        .reshape(3, -1, line, HD)
        .transpose(2, 1, 0, 3)
        .reshape(line, -1, 3 * HD)
    )
    proj_cut = proj_weight.astype(low).reshape(line, HD, -1)
    named = jnp.sum(
        (routes[:, :, None] == jnp.arange(expert_count, dtype=jnp.int32)).astype(jnp.float32), axis=1
    )
    width = first_gain.shape[0]
    gain_rows = jnp.zeros((16, width), jnp.float32)
    gain_rows = gain_rows.at[0].set(first_gain).at[1].set(second_gain)
    share = query_gain.shape[0]
    gain_rows = gain_rows.at[2, :share].set(query_gain).at[2, share : 2 * share].set(key_gain)
    small = jnp.concatenate([gain_rows, router_weight.T, named.T], axis=0).astype(low)
    all_in, head_weight, head_proj, all_small = gather_with_weights(
        own_in, cut, proj_cut, small, line, 1
    )
    gain_one = all_small[0].astype(jnp.float32)
    gain_two = all_small[1].astype(jnp.float32)
    shares = all_small[2].reshape(groups, width).astype(jnp.float32)
    gain_query = shares[:, :share].reshape(HD)
    gain_key = shares[:, share : 2 * share].reshape(HD)
    router_rows = all_small[16 : 16 + expert_count]
    named_all = all_small[16 + expert_count :]

    normed_one = norm_parts(all_in.reshape(4 * rows, model_width).astype(jnp.float32), gain_one)[0]
    normed_one = normed_one.astype(low)
    projected = dot(normed_one, head_weight)
    queries_raw = projected[:, :HD].reshape(4, rows, HD)
    keys_raw = projected[:, HD : 2 * HD].reshape(4, rows, HD)
    values = projected[:, 2 * HD :].astype(low).reshape(4, rows, HD)
    cos_table, sin_table = rope_tables(rows, HD)
    cos_table, sin_table = cos_table[:, 0], sin_table[:, 0]
    query_normed, query_unit, query_inverse = norm_parts(queries_raw, gain_query)
    key_normed, key_unit, key_inverse = norm_parts(keys_raw, gain_key)
    queries = rotate(query_normed, cos_table, sin_table).astype(low)
    keys_rot = rotate(key_normed, cos_table, sin_table).astype(low)
    my_lengths = lax.dynamic_slice_in_dim(lengths, 4 * c, 4)
    usable = jnp.arange(rows)[None, :] < my_lengths[:, None]
    scores = (
        jnp.einsum("sqd,skd->sqk", queries, keys_rot, preferred_element_type=jnp.float32)
        / score_scale
    )
    scores = jnp.where(usable[:, None, :], scores, NEG_FILL)
    exponent = jnp.exp(scores - jnp.max(scores, axis=-1, keepdims=True))
    softmax_f = exponent / jnp.sum(exponent, axis=-1, keepdims=True)
    probs = softmax_f.astype(low)
    context = jnp.einsum("sqk,skd->sqd", probs, values, preferred_element_type=jnp.float32)
    context = context.astype(low).reshape(4 * rows, HD)
    attn_part = dot(context, head_proj).astype(low).reshape(4, rows, model_width)
    (attn_total,) = reduce_rows((attn_part,), line, False, 2)

    source = own_in.astype(jnp.float32)
    residual = source + attn_total
    normed_two_f, unit_two, inverse_two = norm_parts(residual, gain_two)
    normed_two = normed_two_f.astype(low)
    flat_two = normed_two.reshape(2 * deep, model_width)
    logits = dot(flat_two, router_rows, ((1,), (1,)))
    slot_of_seq = jnp.argmax(
        permutation[None, :] == jnp.arange(sequences, dtype=jnp.int32)[:, None], axis=1
    ).astype(jnp.int32)
    own_slots = lax.dynamic_slice_in_dim(slot_of_seq, first_own, 2)
    own_named = jnp.concatenate(
        [
            lax.dynamic_slice_in_dim(named_all, own_slots[k] * rows + group * deep, deep, axis=1)
            for k in range(2)
        ],
        axis=1,
    ).T.astype(jnp.float32)
    gates = jax.nn.softmax(jnp.where(own_named > 0.5, logits, NEG_FILL), axis=-1)
    lanes = 128
    gate_rows = jnp.pad(gates, ((0, 0), (0, lanes - expert_count))).reshape(2, deep, lanes)
    all_rows, all_grad, all_gates, both_matrix, down_matrix = gather_with_casts(
        (normed_two, own_cot, gate_rows), (gate_weight, up_weight, down_weight), line, 3
    )
    tokens = sequences * rows
    moe_total, row_sums, gated, grad_pre = experts_to_rows(
        all_rows, all_grad, all_gates, both_matrix, down_matrix, local_experts, line, 4
    )
    grad_normed_two, gate_total = row_sums[..., :model_width], row_sums[..., model_width:]
    flat_rows = all_rows.reshape(tokens, model_width)
    flat_grad = all_grad.reshape(tokens, model_width)
    own_out = (residual + moe_total).astype(low)
    gate_total = gate_total.reshape(2 * deep, lanes)[:, :expert_count]
    grad_logits = (
        gates * (gate_total - jnp.sum(gates * gate_total, axis=-1, keepdims=True))
    ).astype(low)
    grad_normed_two = grad_normed_two + dot(grad_logits, router_rows).reshape(2, deep, model_width)
    router_part = dot(grad_logits, flat_two, ((0,), (0,)))
    second_part = jnp.sum(grad_normed_two * unit_two, axis=(0, 1))
    grad_state = own_cot.astype(jnp.float32) + norm_back(
        grad_normed_two, gain_two, unit_two, inverse_two
    )
    all_state, output, gate_grad, up_grad, down_grad = gather_and_spread(
        grad_state.astype(low),
        own_out,
        (flat_rows, flat_grad, grad_pre, gated),
        (gate_weight.shape, up_weight.shape, down_weight.shape),
        line,
        5,
    )

    all_state = all_state.reshape(4 * rows, model_width)
    proj_grad = dot(context, all_state, ((0,), (0,))).astype(low)
    grad_context = dot(all_state, head_proj, ((1,), (1,))).astype(low).reshape(4, rows, HD)
    grad_values = jnp.einsum("sqk,sqd->skd", probs, grad_context, preferred_element_type=jnp.float32)
    grad_probs = jnp.einsum("sqd,skd->sqk", grad_context, values, preferred_element_type=jnp.float32)
    grad_scores = (
        softmax_f * (grad_probs - jnp.sum(grad_probs * softmax_f, axis=-1, keepdims=True))
    ).astype(low)
    grad_queries = (
        jnp.einsum("sqk,skd->sqd", grad_scores, keys_rot, preferred_element_type=jnp.float32)
        / score_scale
    )
    grad_keys = (
        jnp.einsum("sqk,sqd->skd", grad_scores, queries, preferred_element_type=jnp.float32)
        / score_scale
    )
    grad_queries = rotate(grad_queries, cos_table, -sin_table)
    grad_keys = rotate(grad_keys, cos_table, -sin_table)
    query_gain_part = jnp.sum(grad_queries * query_unit, axis=(0, 1))
    key_gain_part = jnp.sum(grad_keys * key_unit, axis=(0, 1))
    grad_projected = jnp.concatenate(
        [
            norm_back(grad_queries, gain_query, query_unit, query_inverse).astype(low),
            norm_back(grad_keys, gain_key, key_unit, key_inverse).astype(low),
            grad_values.astype(low),
        ],
        axis=-1,
    ).reshape(4 * rows, 3 * HD)
    head_grad = dot(normed_one, grad_projected, ((0,), (0,))).astype(low)
    one_part = dot(grad_projected, head_weight, ((1,), (1,))).astype(low)
    grad_normed_one, cuts, proj_cuts = reduce_with_weights(
        one_part.reshape(4, rows, model_width), head_grad, proj_grad, line, 6
    )

    _, unit_one, inverse_one = norm_parts(source, gain_one)
    first_part = jnp.sum(grad_normed_one * unit_one, axis=(0, 1))
    own_grad = (grad_state + norm_back(grad_normed_one, gain_one, unit_one, inverse_one)).astype(low)

    def by_share(values):
        return jnp.pad(values.reshape(groups, share), ((0, 0), (0, width - share))).reshape(1, -1)

    small_grads = jnp.concatenate(
        [
            first_part[None],
            second_part[None],
            by_share(query_gain_part),
            by_share(key_gain_part),
            jnp.zeros((4, model_width), jnp.float32),
            router_part,
        ],
        axis=0,
    )
    input_grad, small_total = finish_rows(own_grad, small_grads, line, 7)
    owned = cuts.reshape(line, -1, 3, HD).transpose(2, 1, 0, 3).reshape(3, -1, line * HD)
    owned = owned.astype(jnp.float32)
    return (
        output,
        input_grad,
        owned[0],
        owned[1],
        owned[2],
        proj_cuts.reshape(line * HD, -1).astype(jnp.float32),
        small_total[0],
        small_total[1],
        small_total[2, :share],
        small_total[3, :share],
        small_total[8:].T,
        gate_grad,
        up_grad,
        down_grad,
    )


def on_device_paired(
    inputs,
    cotangent,
    lengths,
    permutation,
    routes,
    query_weight,
    key_weight,
    value_weight,
    proj_weight,
    first_gain,
    second_gain,
    query_gain,
    key_gain,
    router_weight,
    gate_weight,
    up_weight,
    down_weight,
):
    model_width = inputs.shape[2]
    local_heads = query_weight.shape[1] // HD
    expert_count = router_weight.shape[1]
    groups_count = lax.axis_size("expert")
    local_experts = gate_weight.shape[0]
    slot_index = lax.axis_index("expert")
    seq_ids = jnp.arange(permutation.shape[0], dtype=jnp.int32)
    my_sequence = jnp.sum(jnp.where(seq_ids == slot_index, permutation, 0))
    my_length = jnp.sum(jnp.where(seq_ids == my_sequence, lengths, 0))
    slot_of_seq = jnp.sum(
        jnp.where(permutation[None, :] == seq_ids[:, None], seq_ids[None, :], 0), axis=1
    )
    dealt_in, dealt_grad = (
        lax.all_to_all(inputs[permutation], "expert", split_axis=0, concat_axis=1, tiled=True),
        lax.all_to_all(cotangent[permutation], "expert", split_axis=0, concat_axis=1, tiled=True),
    )
    token_rows = dealt_in.shape[1]
    capacity = token_rows * TOPK * 33 // (32 * expert_count)
    block_rows = min(512, token_rows)
    score_scale = math.sqrt(HD)
    gathered = (
        lax.all_gather(query_weight.astype(jnp.bfloat16), "expert", axis=0, tiled=True),
        lax.all_gather(key_weight.astype(jnp.bfloat16), "expert", axis=0, tiled=True),
        lax.all_gather(value_weight.astype(jnp.bfloat16), "expert", axis=0, tiled=True),
        lax.all_gather(proj_weight.astype(jnp.bfloat16), "expert", axis=1, tiled=True),
        lax.all_gather(first_gain.astype(jnp.bfloat16), "expert", axis=0, tiled=True),
        lax.all_gather(second_gain.astype(jnp.bfloat16), "expert", axis=0, tiled=True),
        lax.all_gather(query_gain.astype(jnp.bfloat16), "expert", axis=0, tiled=True),
        lax.all_gather(key_gain.astype(jnp.bfloat16), "expert", axis=0, tiled=True),
        lax.all_gather(router_weight.astype(jnp.bfloat16), "expert", axis=0, tiled=True),
    )
    query_matrix = gathered[0]
    key_matrix = gathered[1]
    value_matrix = gathered[2]
    proj_matrix = gathered[3]
    gain_one = gathered[4].astype(jnp.float32)
    gain_two = gathered[5].astype(jnp.float32)
    gain_query = gathered[6].astype(jnp.float32)
    gain_key = gathered[7].astype(jnp.float32)
    router_matrix = gathered[8]
    gate_matrix = gate_weight.astype(jnp.bfloat16)
    up_matrix = up_weight.astype(jnp.bfloat16)
    down_matrix = down_weight.astype(jnp.bfloat16)
    source = dealt_in.reshape(token_rows, model_width).astype(jnp.float32)
    normed_one_f, unit_one, inverse_one = norm_parts(source, gain_one)
    normed_one = normed_one_f.astype(jnp.bfloat16)
    queries_raw = jnp.dot(normed_one, query_matrix, preferred_element_type=jnp.float32).reshape(
        token_rows, local_heads, HD
    )
    keys_raw = jnp.dot(normed_one, key_matrix, preferred_element_type=jnp.float32).reshape(
        token_rows, local_heads, HD
    )
    values = (
        jnp.dot(normed_one, value_matrix, preferred_element_type=jnp.float32)
        .astype(jnp.bfloat16)
        .reshape(token_rows, local_heads, HD)
    )
    cos_table, sin_table = rope_tables(token_rows, HD)
    query_normed, query_unit, query_inverse = norm_parts(queries_raw, gain_query)
    key_normed, key_unit, key_inverse = norm_parts(keys_raw, gain_key)
    queries = rotate(query_normed, cos_table, sin_table).astype(jnp.bfloat16)
    keys_rot = rotate(key_normed, cos_table, sin_table).astype(jnp.bfloat16)
    usable = jnp.arange(token_rows) < my_length

    def block_scores():
        scores = (
            jnp.einsum("qhd,khd->hqk", queries, keys_rot, preferred_element_type=jnp.float32)
            / score_scale
        )
        return (queries, jnp.where(usable[None, None, :], scores, NEG_FILL))

    query_block, scores = block_scores()
    maximum = jnp.max(scores, axis=-1, keepdims=True)
    exponent = jnp.exp(scores - maximum)
    row_total = jnp.sum(exponent, axis=-1, keepdims=True)
    softmax_rows = (exponent / row_total).astype(jnp.bfloat16)
    context_blocks = jnp.einsum(
        "hqk,khd->qhd", softmax_rows, values, preferred_element_type=jnp.float32
    ).astype(jnp.bfloat16)
    lse_blocks = [maximum + jnp.log(row_total)]
    context = context_blocks.reshape(token_rows, local_heads * HD)
    attn_part = jnp.dot(context, proj_matrix, preferred_element_type=jnp.float32)
    attn_total = lax.psum(attn_part, "tensor")
    residual = source + attn_total
    normed_two_f, unit_two, inverse_two = norm_parts(residual, gain_two)
    normed_two = normed_two_f.astype(jnp.bfloat16)
    logits = jnp.dot(normed_two, router_matrix, preferred_element_type=jnp.float32)
    choose = (
        routes[:, :, None] == jnp.arange(expert_count, dtype=jnp.int32)[None, None, :]
    ).astype(jnp.float32)
    chosen = jnp.sum(choose * logits[:, None, :], axis=-1)
    gate_probs = jax.nn.softmax(chosen, axis=-1)
    flat_routes = routes.reshape(-1)
    route_hits = (
        flat_routes[:, None] == jnp.arange(expert_count, dtype=jnp.int32)[None, :]
    ).astype(jnp.int32)
    rank_ids = jnp.sum(jnp.cumsum(route_hits, axis=0) * route_hits, axis=1) - 1
    slot_ids = flat_routes * capacity + rank_ids
    pair_tokens = jnp.arange(flat_routes.shape[0], dtype=jnp.int32) // TOPK
    send_rows = (
        jnp.zeros((expert_count * capacity, model_width), jnp.bfloat16)
        .at[slot_ids]
        .set(normed_two[pair_tokens])
    )
    send_rows = send_rows.reshape(groups_count, local_experts, capacity, model_width)
    received = lax.all_to_all(send_rows, "expert", split_axis=0, concat_axis=0, tiled=True)
    gate_pre = jnp.einsum(
        "secd,edf->secf", received, gate_matrix, preferred_element_type=jnp.float32
    )
    up_pre = jnp.einsum("secd,edf->secf", received, up_matrix, preferred_element_type=jnp.float32)
    hidden = (jax.nn.silu(gate_pre) * up_pre).astype(jnp.bfloat16)
    result = jnp.einsum(
        "secf,efd->secd", hidden, down_matrix, preferred_element_type=jnp.float32
    ).astype(jnp.bfloat16)
    returned = lax.all_to_all(result, "expert", split_axis=0, concat_axis=0, tiled=True)
    picked = returned.reshape(expert_count * capacity, model_width)[slot_ids].reshape(
        token_rows, TOPK, model_width
    )
    combined = jnp.sum(gate_probs[:, :, None] * picked.astype(jnp.float32), axis=1)
    moe_total = lax.psum(combined.astype(jnp.bfloat16), "tensor").astype(jnp.float32)
    output = (residual + moe_total).astype(jnp.bfloat16)
    grad_out = dealt_grad.reshape(token_rows, model_width).astype(jnp.float32)
    gate_grad_part = jnp.sum(grad_out[:, None, :] * picked.astype(jnp.float32), axis=-1)
    routed_grad = (
        (gate_probs[:, :, None] * grad_out[:, None, :])
        .astype(jnp.bfloat16)
        .reshape(token_rows * TOPK, model_width)
    )
    grad_send = (
        jnp.zeros((expert_count * capacity, model_width), jnp.bfloat16)
        .at[slot_ids]
        .set(routed_grad)
    )
    grad_send = grad_send.reshape(groups_count, local_experts, capacity, model_width)
    grad_rows, rows_in = (
        lax.all_to_all(grad_send, "expert", split_axis=0, concat_axis=0, tiled=True),
        lax.all_to_all(send_rows, "expert", split_axis=0, concat_axis=0, tiled=True),
    )
    gate_pre = jnp.einsum(
        "secd,edf->secf", rows_in, gate_matrix, preferred_element_type=jnp.float32
    )
    up_pre = jnp.einsum("secd,edf->secf", rows_in, up_matrix, preferred_element_type=jnp.float32)
    grad_hidden = jnp.einsum(
        "secd,efd->secf", grad_rows, down_matrix, preferred_element_type=jnp.float32
    )
    sigmoid_gate = jax.nn.sigmoid(gate_pre)
    silu_gate = gate_pre * sigmoid_gate
    grad_gate_pre = (
        grad_hidden * up_pre * sigmoid_gate * (1.0 + gate_pre * (1.0 - sigmoid_gate))
    ).astype(jnp.bfloat16)
    grad_up_pre = (grad_hidden * silu_gate).astype(jnp.bfloat16)
    hidden = (silu_gate * up_pre).astype(jnp.bfloat16)
    rows_grad = (
        jnp.einsum("secf,edf->secd", grad_gate_pre, gate_matrix, preferred_element_type=jnp.float32)
        + jnp.einsum("secf,edf->secd", grad_up_pre, up_matrix, preferred_element_type=jnp.float32)
    ).astype(jnp.bfloat16)
    down_grad = jnp.einsum("secf,secd->efd", hidden, grad_rows, preferred_element_type=jnp.float32)
    gate_grad = jnp.einsum(
        "secd,secf->edf", rows_in, grad_gate_pre, preferred_element_type=jnp.float32
    )
    up_grad = jnp.einsum("secd,secf->edf", rows_in, grad_up_pre, preferred_element_type=jnp.float32)
    returned_grad = lax.all_to_all(rows_grad, "expert", split_axis=0, concat_axis=0, tiled=True)
    returned_pairs = returned_grad.reshape(expert_count * capacity, model_width)[slot_ids].reshape(
        token_rows, TOPK, model_width
    )
    normed_two_part = jnp.sum(returned_pairs.astype(jnp.float32), axis=1)
    grad_normed_two, gate_grad_total = lax.psum((normed_two_part, gate_grad_part), "tensor")
    grad_chosen = gate_probs * (
        gate_grad_total - jnp.sum(gate_probs * gate_grad_total, axis=-1, keepdims=True)
    )
    grad_logits = jnp.sum(choose * grad_chosen[:, :, None], axis=1).astype(jnp.bfloat16)
    grad_normed_two = grad_normed_two + jnp.dot(
        grad_logits, router_matrix.T, preferred_element_type=jnp.float32
    )
    router_grad = jnp.dot(normed_two.T, grad_logits, preferred_element_type=jnp.float32)
    second_gain_grad = jnp.sum(grad_normed_two * unit_two, axis=0)
    grad_state = grad_out + norm_back(grad_normed_two, gain_two, unit_two, inverse_two)
    grad_context_in = grad_state.astype(jnp.bfloat16)
    proj_grad = jnp.dot(context.T, grad_context_in, preferred_element_type=jnp.float32)
    grad_context = (
        jnp.dot(grad_context_in, proj_matrix.T, preferred_element_type=jnp.float32)
        .astype(jnp.bfloat16)
        .reshape(token_rows, local_heads, HD)
    )
    grad_values = jnp.zeros((token_rows, local_heads, HD), jnp.float32)
    grad_keys_rot = jnp.zeros((token_rows, local_heads, HD), jnp.float32)
    grad_query_blocks = []
    for number, start_row in enumerate(range(0, token_rows, block_rows)):
        query_block, scores = block_scores()
        softmax_f = jnp.exp(scores - lse_blocks[number])
        grad_values = jnp.einsum(
            "hqk,qhd->khd",
            softmax_f.astype(jnp.bfloat16),
            grad_context,
            preferred_element_type=jnp.float32,
        )
        grad_probs = jnp.einsum(
            "qhd,khd->hqk", grad_context, values, preferred_element_type=jnp.float32
        )
        grad_scores = (
            softmax_f * (grad_probs - jnp.sum(grad_probs * softmax_f, axis=-1, keepdims=True))
        ).astype(jnp.bfloat16)
        grad_query_blocks.append(
            jnp.einsum("hqk,khd->qhd", grad_scores, keys_rot, preferred_element_type=jnp.float32)
            / score_scale
        )
        grad_keys_rot = (
            jnp.einsum("hqk,qhd->khd", grad_scores, query_block, preferred_element_type=jnp.float32)
            / score_scale
        )
    grad_queries_n = rotate(grad_query_blocks[0], cos_table, -sin_table)
    grad_keys_n = rotate(grad_keys_rot, cos_table, -sin_table)
    query_gain_part = jnp.sum(grad_queries_n * query_unit, axis=(0, 1))
    key_gain_part = jnp.sum(grad_keys_n * key_unit, axis=(0, 1))
    grad_queries_raw = (
        norm_back(grad_queries_n, gain_query, query_unit, query_inverse)
        .astype(jnp.bfloat16)
        .reshape(token_rows, local_heads * HD)
    )
    grad_keys_raw = (
        norm_back(grad_keys_n, gain_key, key_unit, key_inverse)
        .astype(jnp.bfloat16)
        .reshape(token_rows, local_heads * HD)
    )
    grad_values_low = grad_values.astype(jnp.bfloat16).reshape(token_rows, local_heads * HD)
    query_grad = jnp.dot(normed_one.T, grad_queries_raw, preferred_element_type=jnp.float32)
    key_grad = jnp.dot(normed_one.T, grad_keys_raw, preferred_element_type=jnp.float32)
    value_grad = jnp.dot(normed_one.T, grad_values_low, preferred_element_type=jnp.float32)
    normed_one_part = jnp.dot(grad_queries_raw, query_matrix.T, preferred_element_type=jnp.float32)
    normed_one_part = normed_one_part + jnp.dot(
        grad_keys_raw, key_matrix.T, preferred_element_type=jnp.float32
    )
    normed_one_part = normed_one_part + jnp.dot(
        grad_values_low, value_matrix.T, preferred_element_type=jnp.float32
    )
    grad_normed_one, query_gain_total, key_gain_total = (
        lax.psum(normed_one_part.astype(jnp.bfloat16), "tensor").astype(jnp.float32),
        lax.psum(query_gain_part.astype(jnp.bfloat16), "tensor").astype(jnp.float32),
        lax.psum(key_gain_part.astype(jnp.bfloat16), "tensor").astype(jnp.float32),
    )
    first_gain_grad = jnp.sum(grad_normed_one * unit_one, axis=0)
    input_grad = (grad_state + norm_back(grad_normed_one, gain_one, unit_one, inverse_one)).astype(
        jnp.bfloat16
    )
    shards = (
        lax.psum_scatter(
            query_grad.astype(jnp.bfloat16), "expert", scatter_dimension=0, tiled=True
        ).astype(jnp.float32),
        lax.psum_scatter(
            key_grad.astype(jnp.bfloat16), "expert", scatter_dimension=0, tiled=True
        ).astype(jnp.float32),
        lax.psum_scatter(
            value_grad.astype(jnp.bfloat16), "expert", scatter_dimension=0, tiled=True
        ).astype(jnp.float32),
        lax.psum_scatter(
            proj_grad.astype(jnp.bfloat16), "expert", scatter_dimension=1, tiled=True
        ).astype(jnp.float32),
        lax.psum_scatter(
            first_gain_grad.astype(jnp.bfloat16), "expert", scatter_dimension=0, tiled=True
        ).astype(jnp.float32),
        lax.psum_scatter(
            second_gain_grad.astype(jnp.bfloat16), "expert", scatter_dimension=0, tiled=True
        ).astype(jnp.float32),
        lax.psum_scatter(
            query_gain_total.astype(jnp.bfloat16), "expert", scatter_dimension=0, tiled=True
        ).astype(jnp.float32),
        lax.psum_scatter(
            key_gain_total.astype(jnp.bfloat16), "expert", scatter_dimension=0, tiled=True
        ).astype(jnp.float32),
        lax.psum_scatter(
            router_grad.astype(jnp.bfloat16), "expert", scatter_dimension=0, tiled=True
        ).astype(jnp.float32),
    )
    back_out, back_grad = (
        lax.all_to_all(
            output.reshape(1, token_rows, model_width),
            "expert",
            split_axis=1,
            concat_axis=0,
            tiled=True,
        ),
        lax.all_to_all(
            input_grad.reshape(1, token_rows, model_width),
            "expert",
            split_axis=1,
            concat_axis=0,
            tiled=True,
        ),
    )
    ordered_out = back_out[slot_of_seq]
    ordered_grad = back_grad[slot_of_seq]
    return (
        ordered_out,
        ordered_grad,
        shards[0],
        shards[1],
        shards[2],
        shards[3],
        shards[4],
        shards[5],
        shards[6],
        shards[7],
        shards[8],
        gate_grad,
        up_grad,
        down_grad,
    )


def solution(mesh):
    in_specs = (
        P(None, "expert", None),
        P(None, "expert", None),
        P(),
        P(),
        P("expert", None),
        P("expert", "tensor"),
        P("expert", "tensor"),
        P("expert", "tensor"),
        P("tensor", "expert"),
        P("expert"),
        P("expert"),
        P("expert"),
        P("expert"),
        P("expert", None),
        P("expert", None, "tensor"),
        P("expert", None, "tensor"),
        P("expert", "tensor", None),
    )
    out_specs = (
        P(None, "expert", None),
        P(None, "expert", None),
        P("expert", "tensor"),
        P("expert", "tensor"),
        P("expert", "tensor"),
        P("tensor", "expert"),
        P("expert"),
        P("expert"),
        P("expert"),
        P("expert"),
        P("expert", None),
        P("expert", None, "tensor"),
        P("expert", None, "tensor"),
        P("expert", "tensor", None),
    )
    chips = mesh.shape["expert"] * mesh.shape["tensor"] // 2

    def whole(*arrays):
        heads, sequences = arrays[5].shape[1] // HD, arrays[0].shape[0]
        fits = heads == chips and sequences == 8 and mesh.shape["tensor"] == 4
        return jax.shard_map(
            on_device if fits else on_device_paired,
            mesh=mesh,
            in_specs=in_specs,
            out_specs=out_specs,
            check_vma=False,
        )(*arrays)

    return whole
```
